32 devices in a mesh: rep: 4 (over y, core), fsdp: 8 (over z, x).
Axes of the slice: x: 2, y: 2, z: 4, core: 2. Of those that a mesh axis runs over, the one named last changes fastest.
Arguments:
- token_ids: int32 [32, 128], P(('rep', 'fsdp')), may hold values from 0 to 30527
- lengths: int32 [32], P(('rep', 'fsdp')), may hold values from 1 to 128, 2048 in all
- slot_order: int32 [32], replicated, may hold values from 0 to 31, each once
- pair_labels: int32 [32], replicated, may hold values from 0 to 31, as said below
- embedding: float32 [30528, 768], P('fsdp'), may hold values from -0.21875 to 0.21875
- attend_weight: float32 [768, 2304], P('fsdp'), may hold values from -0.21875 to 0.21875
- attention_output_matrix: float32 [768, 768], P('fsdp'), may hold values from -1.25 to 1.25
- gate_up: float32 [768, 6144], P('fsdp'), may hold values from -0.21875 to 0.21875
- contract_kernel: float32 [3072, 768], P('fsdp'), may hold values from -0.109375 to 0.109375
- norm_params: float32 [6, 768], P(None, 'fsdp'), may hold values from -0.3 to 1.4, as said below
- embedding_first: float32 [30528, 768], P('fsdp'), may hold values from -2.3841858e-06 to 2.3841858e-06
- embedding_second: float32 [30528, 768], P('fsdp'), may hold values from 1.0135626e-14 to 4.0542504e-14
- attend_first: float32 [768, 2304], P('fsdp'), may hold values from -2.3841858e-06 to 2.3841858e-06
- attend_second: float32 [768, 2304], P('fsdp'), may hold values from 1.0135626e-14 to 4.0542504e-14
- output_first: float32 [768, 768], P('fsdp'), may hold values from -2.3841858e-06 to 2.3841858e-06
- output_second: float32 [768, 768], P('fsdp'), may hold values from 1.0135626e-14 to 4.0542504e-14
- gate_up_first: float32 [768, 6144], P('fsdp'), may hold values from -2.3841858e-06 to 2.3841858e-06
- gate_up_second: float32 [768, 6144], P('fsdp'), may hold values from 1.0135626e-14 to 4.0542504e-14
- down_first: float32 [3072, 768], P('fsdp'), may hold values from -2.3841858e-06 to 2.3841858e-06
- down_second: float32 [3072, 768], P('fsdp'), may hold values from 1.0135626e-14 to 4.0542504e-14
- norm_first: float32 [6, 768], P(None, 'fsdp'), may hold values from -2.670288e-05 to 2.670288e-05
- norm_second: float32 [6, 768], P(None, 'fsdp'), may hold values from 1.0135626e-12 to 4.0542504e-12
Outputs:
- loss_value: float32 [], replicated
- grad_norm: float32 [], replicated
- embedding_next: float32 [30528, 768], P('fsdp')
- embedding_first_next: float32 [30528, 768], P('fsdp')
- embedding_second_next: float32 [30528, 768], P('fsdp')
- attend_next: float32 [768, 2304], P('fsdp')
- attend_first_next: float32 [768, 2304], P('fsdp')
- attend_second_next: float32 [768, 2304], P('fsdp')
- output_next: float32 [768, 768], P('fsdp')
- output_first_next: float32 [768, 768], P('fsdp')
- output_second_next: float32 [768, 768], P('fsdp')
- gate_up_next: float32 [768, 6144], P('fsdp')
- gate_up_first_next: float32 [768, 6144], P('fsdp')
- gate_up_second_next: float32 [768, 6144], P('fsdp')
- down_next: float32 [3072, 768], P('fsdp')
- down_first_next: float32 [3072, 768], P('fsdp')
- down_second_next: float32 [3072, 768], P('fsdp')
- norm_next: float32 [6, 768], P(None, 'fsdp')
- norm_first_next: float32 [6, 768], P(None, 'fsdp')
- norm_second_next: float32 [6, 768], P(None, 'fsdp')
The draws below stay inside these ranges and needn't reach their ends.
Inputs may be any that keep to these rules, and one draw needn't show every extreme that they name: pair_labels[pair_labels[i]] = i and pair_labels[i] != i: the 32 sequences form disjoint pairs. Slot s holds the sequence whose index in the given order is slot_order[s]; each index once. `lengths`: the longest sequence has exactly 128 tokens. `norm_params`: rows 0, 2 and 4 are gains, rows 1, 3 and 5 the matching shifts.
All inputs are finite; a program needn't handle non-finite values. No bound on the sum of `lengths` on one device may be relied on, other than what follows from the above.
Results may differ from the reference program's by a relative error of at most 0.011.
The reference program's roundings to bfloat16 on the way count: a program that leaves them out, or rounds other values in their place, can miss the bound.
Values may be sent and summed in bfloat16 or wider, within the bound.
A program may use at most 152 MiB of HBM per device.

```python
import math
import jax
import jax.numpy as jnp
import numpy as np
from jax import lax

D = 768
H = 12
HD = 64
FF = 3072
V = 30528
LMAX = 128
STEP = 4
SEQS = 32
PARAMS = 32887296


def draw_pair_labels(key, part):
    order = jax.random.permutation(jax.random.fold_in(key, 21), SEQS).astype(jnp.int32)
    partner = order.reshape(SEQS // 2, 2)[:, ::-1].reshape(SEQS)
    return jnp.zeros((SEQS,), jnp.int32).at[order].set(partner)


def draw_norm_params(key, part):
    gain_key = jax.random.fold_in(key, 31)
    shift_key = jax.random.fold_in(key, 32)
    gain_rows = jax.random.uniform(gain_key, (3, D), jnp.float32, 0.7, 1.3)
    shift_rows = jnp.clip(0.06 * jax.random.normal(shift_key, (3, D), jnp.float32), -0.3, 0.3)
    return jnp.stack([gain_rows[0], shift_rows[0], gain_rows[1], shift_rows[1], gain_rows[2], shift_rows[2]])


def with_ends(array, stream_key, least, largest):
    shape = array.shape
    place = [jax.random.randint(jax.random.fold_in(stream_key, axis), (), 0, shape[axis]) for axis in range(len(shape))]
    array = array.at[tuple(place)].set(least)
    longest = shape.index(max(shape))
    place[longest] = (place[longest] + 1) % shape[longest]
    return array.at[tuple(place)].set(largest)


def shard_levels(key, dims, split, smallest, top_value):
    level, own = 1.0, jax.random.fold_in(key, 6)
    for axis_at, shards_of in split:
        steps = jnp.exp(jax.random.uniform(jax.random.fold_in(own, axis_at), (shards_of,), jnp.float32, smallest / len(split), top_value / len(split)))
        level = level * jnp.repeat(steps, dims[axis_at] // shards_of).reshape([-1 if axis == axis_at else 1 for axis in range(len(dims))])
    return level


def rank_bounds(number_of, slope):
    loads = [(1 << 20) // math.isqrt(grade ** slope) + 1 for grade in range(1, number_of + 1)]
    scale = 1 + sum(loads) // (1 << 30)
    return np.cumsum(np.array([max(1, weight // scale) for weight in loads]))


def ranked_ids(own_key, shape, count, lean):
    grid = rank_bounds(count, lean)
    lot = jax.random.randint(jax.random.fold_in(own_key, 1), shape, 0, int(grid[count - 1]))
    rank = jnp.searchsorted(jnp.asarray(grid, jnp.int32), lot, side="right")
    return jax.random.permutation(jax.random.fold_in(own_key, 2), count)[rank].astype(jnp.int32)


def profile(count, total, most, skew):
    portions = [(1 << 20) // math.isqrt(standing ** skew) + 1 for standing in range(2, count + 1)]
    surplus, holding = total - most - (count - 1), [1] * (count - 1)
    while surplus > 0:
        free = [i for i in range(count - 1) if holding[i] < most]
        pool, left = sum([portions[i] for i in free]), surplus
        for i in free:
            addition = min(most - holding[i], max(1, left * portions[i] // pool), surplus)
            holding[i] = holding[i] + addition
            surplus = surplus - addition
    return np.array([most] + holding)


def ragged_sizes(stream_key, count, total, bound, skew):
    if count == 2:
        one = jax.random.randint(stream_key, (), max(1, total - bound), min(bound, total - 1) + 1)
        return jnp.stack([one, total - one])
    sizes = jnp.asarray(profile(count, total, bound, skew), jnp.int32)
    twos = (count - 1) // 2
    donor, sink = sizes[1:1 + 2 * twos:2], sizes[2:2 + 2 * twos:2]
    slack = jnp.minimum(donor - 1, bound - sink)
    moved = jax.random.randint(jax.random.fold_in(stream_key, 1), (twos,), 0, 1 << 20) % (slack + 1)
    sizes = sizes.at[1:1 + 2 * twos:2].set(donor - moved).at[2:2 + 2 * twos:2].set(sink + moved)
    return sizes[jax.random.permutation(jax.random.fold_in(stream_key, 2), count)]


def noise(own_key, extent, scale, most, shards=(), kind=jnp.bfloat16):
    loudness = shard_levels(own_key, extent, shards, -0.22, 0.18) if shards else 1.0
    entries = jax.random.normal(own_key, extent, jnp.float32) * scale * loudness
    return jnp.minimum(jnp.maximum(entries, -most), most).astype(kind)


def setup_inputs(seed: int = 0) -> dict:
    key_list = jax.random.split(jax.random.key(seed), 23)
    token_ids = with_ends(ranked_ids(key_list[0], (SEQS, LMAX), V, 2), jax.random.fold_in(key_list[0], 3), 0, V - 1).astype(jnp.int32)
    lengths = ragged_sizes(key_list[1], SEQS, SEQS * LMAX // 2, LMAX, 2).astype(jnp.int32)
    slot_order = jax.random.permutation(key_list[2], SEQS).astype(jnp.int32)
    pair_labels = draw_pair_labels(jax.random.fold_in(key_list[22], 71), 0)
    embedding = noise(key_list[4], (V, D), D ** -0.5, 0.21875, ((0, 8),), jnp.float32)
    attend_weight = noise(key_list[5], (D, 3 * D), D ** -0.5, 0.21875, ((0, 8),), jnp.float32)
    attention_output_matrix = noise(key_list[6], (D, D), (max(4 * D // LMAX, 1)) ** -0.5, 1.25, ((0, 8),), jnp.float32)
    gate_up = noise(key_list[7], (D, 2 * FF), D ** -0.5, 0.21875, ((0, 8),), jnp.float32)
    contract_kernel = noise(key_list[8], (FF, D), FF ** -0.5, 0.109375, ((0, 8),), jnp.float32)
    norm_params = draw_norm_params(jax.random.fold_in(key_list[22], 71), 0)
    embedding_first = noise(key_list[10], (V, D), (0.001 / PARAMS ** 0.5), 2.384185791015625e-06, ((0, 8),), jnp.float32)
    embedding_second = jnp.clip(jnp.exp(math.log(4.054250357199245e-14) - 1.3862944 * jax.random.uniform(key_list[11], (V, D), jnp.float32) ** shard_levels(key_list[11], (V, D), ((0, 8),), -0.2, 0.2)), 1.0135625892998112e-14, 4.054250357199245e-14)
    attend_first = noise(key_list[12], (D, 3 * D), (0.001 / PARAMS ** 0.5), 2.384185791015625e-06, ((0, 8),), jnp.float32)
    attend_second = jnp.clip(jnp.exp(math.log(4.054250357199245e-14) - 1.3862944 * jax.random.uniform(key_list[13], (D, 3 * D), jnp.float32) ** shard_levels(key_list[13], (D, 3 * D), ((0, 8),), -0.2, 0.2)), 1.0135625892998112e-14, 4.054250357199245e-14)
    output_first = noise(key_list[14], (D, D), (0.001 / PARAMS ** 0.5), 2.384185791015625e-06, ((0, 8),), jnp.float32)
    output_second = jnp.clip(jnp.exp(math.log(4.054250357199245e-14) - 1.3862944 * jax.random.uniform(key_list[15], (D, D), jnp.float32) ** shard_levels(key_list[15], (D, D), ((0, 8),), -0.2, 0.2)), 1.0135625892998112e-14, 4.054250357199245e-14)
    gate_up_first = noise(key_list[16], (D, 2 * FF), (0.001 / PARAMS ** 0.5), 2.384185791015625e-06, ((0, 8),), jnp.float32)
    gate_up_second = jnp.clip(jnp.exp(math.log(4.054250357199245e-14) - 1.3862944 * jax.random.uniform(key_list[17], (D, 2 * FF), jnp.float32) ** shard_levels(key_list[17], (D, 2 * FF), ((0, 8),), -0.2, 0.2)), 1.0135625892998112e-14, 4.054250357199245e-14)
    down_first = noise(key_list[18], (FF, D), (0.001 / PARAMS ** 0.5), 2.384185791015625e-06, ((0, 8),), jnp.float32)
    down_second = jnp.clip(jnp.exp(math.log(4.054250357199245e-14) - 1.3862944 * jax.random.uniform(key_list[19], (FF, D), jnp.float32) ** shard_levels(key_list[19], (FF, D), ((0, 8),), -0.2, 0.2)), 1.0135625892998112e-14, 4.054250357199245e-14)
    norm_first = noise(key_list[20], (6, D), (0.01 / PARAMS ** 0.5), 2.6702880859375e-05, ((1, 8),), jnp.float32)
    norm_second = jnp.clip(jnp.exp(math.log(4.0542504249618805e-12) - 1.3862944 * jax.random.uniform(key_list[21], (6, D), jnp.float32) ** shard_levels(key_list[21], (6, D), ((1, 8),), -0.2, 0.2)), 1.0135626062404701e-12, 4.0542504249618805e-12)
    return dict(token_ids=token_ids, lengths=lengths, slot_order=slot_order, pair_labels=pair_labels, embedding=embedding, attend_weight=attend_weight, attention_output_matrix=attention_output_matrix, gate_up=gate_up, contract_kernel=contract_kernel, norm_params=norm_params, embedding_first=embedding_first, embedding_second=embedding_second, attend_first=attend_first, attend_second=attend_second, output_first=output_first, output_second=output_second, gate_up_first=gate_up_first, gate_up_second=gate_up_second, down_first=down_first, down_second=down_second, norm_first=norm_first, norm_second=norm_second)


exact_arithmetic_mode = lax.Precision.HIGHEST
logit_divisor = 0.05
clip_level = 0.001
learn_rate = 0.02
norm_rate = 0.3
weight_decay = 0.01
beta_first = 0.5
beta_second = 0.75
adam_floor = 1e-08

@jax.custom_vjp
def low(v):
    return lax.optimization_barrier(v.astype(jnp.bfloat16)).astype(jnp.float32)

@jax.custom_vjp
def low_back(v):
    return v

def low_keep(v):
    return (low(v), None)

def low_pass(kept, grad):
    return (grad,)

def back_keep(v):
    return (v, None)

def back_low(kept, grad):
    return (low(grad),)
low.defvjp(low_keep, low_pass)
low_back.defvjp(back_keep, back_low)

def layer_norm(values, gain, shift):
    centred = values - lax.optimization_barrier(jnp.mean(values, axis=-1, keepdims=True))
    inverse = lax.rsqrt(lax.optimization_barrier(jnp.mean(centred * centred, axis=-1, keepdims=True)) + 1e-06)
    return centred * inverse * gain + shift

def rotary(seq_len, head_size):
    position = jnp.arange(seq_len).astype(jnp.float32)
    frequency = 1000.0 ** (-2.0 * jnp.arange(head_size // 2).astype(jnp.float32) / head_size)
    angles = position[:, None] * frequency[None, :]
    return (jnp.cos(angles)[:, None, :], jnp.sin(angles)[:, None, :])

def rotate(values, cosine_table, sine_table):
    middle = values.shape[-1] // 2
    lower_half, upper_half = (values[..., :middle], values[..., middle:])
    return jnp.concatenate([lower_half * cosine_table - upper_half * sine_table, upper_half * cosine_table + lower_half * sine_table], axis=-1)

def contrast(pooled, pair_labels):
    amount = pooled.shape[0]
    main_trace_entries = jnp.arange(amount)[:, None] == jnp.arange(amount)[None, :]
    summed = 0.0
    for feature_column in (pooled.shape[1] // 12, pooled.shape[1] // 3, pooled.shape[1]):
        portion = pooled[:, :feature_column]
        unit_length_embeddings = portion * lax.rsqrt(lax.optimization_barrier(jnp.sum(portion * portion, axis=1, keepdims=True)) + 1e-06)
        cosine_logit_table = jnp.dot(unit_length_embeddings, unit_length_embeddings.T, precision=exact_arithmetic_mode) / logit_divisor
        cosine_logit_table = jnp.where(main_trace_entries, -1000000000.0, cosine_logit_table)
        row_max = lax.optimization_barrier(jnp.max(cosine_logit_table, axis=1, keepdims=True))
        log_total = row_max[:, 0] + jnp.log(lax.optimization_barrier(jnp.sum(jnp.exp(cosine_logit_table - row_max), axis=1)))
        target = jnp.take_along_axis(cosine_logit_table, pair_labels[:, None], axis=1)[:, 0]
        summed = summed + jnp.mean(log_total - target)
    return summed / 3.0

def encode(weights, token_list, length):
    table, w_attend, w_output, w_gateup, w_down, gain_rows = weights
    seq_len = token_list.shape[0]
    block_size = min(512, seq_len)
    positions = jnp.arange(seq_len)
    key_mask = positions < length
    present = key_mask.astype(jnp.float32)
    embedded = jnp.take(table, token_list, axis=0)
    normed_zero = layer_norm(embedded, gain_rows[0], gain_rows[1])
    projected = low_back(jnp.dot(low(normed_zero), w_attend, precision=exact_arithmetic_mode))
    query = projected[:, :D].reshape(seq_len, H, HD)
    keys = projected[:, D:2 * D].reshape(seq_len, H, HD)
    received_entries = projected[:, 2 * D:].reshape(seq_len, H, HD)
    cosine_table, sine_table = rotary(seq_len, HD)
    query_low = low(rotate(query, cosine_table, sine_table))
    keys_low = low(rotate(keys, cosine_table, sine_table))
    values_low = low(received_entries)
    scaling = HD ** (-0.5)

    def one_block(offset):
        portion = lax.dynamic_slice_in_dim(query_low, offset, block_size, 0)
        scores = low_back(jnp.einsum('qhd,khd->hqk', portion, keys_low, precision=exact_arithmetic_mode) * scaling)
        scores = jnp.where(key_mask, scores, -1000000000.0)
        chances = jax.nn.softmax(scores, axis=-1)
        return jnp.einsum('hqk,khd->qhd', low(chances), values_low, precision=exact_arithmetic_mode)
    offsets = (jnp.arange(seq_len // block_size) * block_size).astype(jnp.int32)
    attended = lax.map(jax.checkpoint(one_block), offsets).reshape(seq_len, D)
    attended = low(low_back(attended))
    branch = low_back(jnp.dot(attended, w_output, precision=exact_arithmetic_mode))
    normed_one = layer_norm(normed_zero + branch, gain_rows[2], gain_rows[3])
    gate_all = low_back(jnp.dot(low(normed_one), w_gateup, precision=exact_arithmetic_mode))
    mixed = low(jax.nn.silu(gate_all[:, :FF]) * gate_all[:, FF:])
    feed = low_back(jnp.dot(mixed, w_down, precision=exact_arithmetic_mode))
    normed_two = layer_norm(normed_one + feed, gain_rows[4], gain_rows[5])
    return lax.optimization_barrier(jnp.sum(normed_two * present[:, None], axis=0)) / length.astype(jnp.float32)

def adamw_step(weight, grad, first, second, rate):
    first_new = beta_first * first + (1.0 - beta_first) * grad
    second_new = beta_second * second + (1.0 - beta_second) * grad * grad
    first_fix = 1.0 - beta_first ** STEP
    second_fix = 1.0 - beta_second ** STEP
    update = first_new / first_fix / (jnp.sqrt(second_new / second_fix) + adam_floor)
    return (weight - rate * (update + weight_decay * weight), first_new, second_new)

def reference(token_ids, lengths, slot_order, pair_labels, embedding, attend_weight, attention_output_matrix, gate_up, contract_kernel, norm_params, embedding_first, embedding_second, attend_first, attend_second, output_first, output_second, gate_up_first, gate_up_second, down_first, down_second, norm_first, norm_second):
    masters = (embedding, attend_weight, attention_output_matrix, gate_up, contract_kernel, norm_params)

    def forward(*params):
        weights = tuple((low(item) for item in params))

        def one_sequence(items):
            return encode(weights, items[0], items[1])
        slots = lax.map(jax.checkpoint(one_sequence), (token_ids, lengths))
        given = jnp.zeros_like(slots).at[slot_order].set(slots)
        return contrast(given, pair_labels)
    loss_value, pullback = jax.vjp(forward, *masters)
    grads = pullback(jnp.ones_like(loss_value))
    squares = jnp.sum(grads[0] * grads[0])
    for item in grads[1:]:
        squares = squares + jnp.sum(item * item)
    grad_norm = jnp.sqrt(squares)
    factor = jnp.minimum(1.0, clip_level / (grad_norm + 1e-06))
    emb_next = adamw_step(embedding, grads[0] * factor, embedding_first, embedding_second, learn_rate)
    att_next = adamw_step(attend_weight, grads[1] * factor, attend_first, attend_second, learn_rate)
    out_next = adamw_step(attention_output_matrix, grads[2] * factor, output_first, output_second, learn_rate)
    gate_next = adamw_step(gate_up, grads[3] * factor, gate_up_first, gate_up_second, learn_rate)
    down_next = adamw_step(contract_kernel, grads[4] * factor, down_first, down_second, learn_rate)
    norm_next = adamw_step(norm_params, grads[5] * factor, norm_first, norm_second, norm_rate)
    return (loss_value, grad_norm, emb_next[0], emb_next[1], emb_next[2], att_next[0], att_next[1], att_next[2], out_next[0], out_next[1], out_next[2], gate_next[0], gate_next[1], gate_next[2], down_next[0], down_next[1], down_next[2], norm_next[0], norm_next[1], norm_next[2])
```

```python
import functools

import jax
import jax.numpy as jnp
from jax import lax
from jax.experimental import pallas as pl
from jax.experimental.pallas import tpu as pltpu
from jax.sharding import PartitionSpec as P

H = 12
HD = 64
STEP = 4
TP = 4
MESH = pl.DeviceIdType.MESH
BF = jnp.bfloat16
F32 = jnp.float32

logit_divisor = 0.05
clip_level = 0.001
learn_rate = 0.02
norm_rate = 0.3
weight_decay = 0.01
beta_first = 0.5
beta_second = 0.75
adam_floor = 1e-08


def dot(a, b):
    return lax.dot_general(a, b, (((1,), (0,)), ((), ())), preferred_element_type=F32)


def dot_nt(a, b):
    return lax.dot_general(a, b, (((1,), (1,)), ((), ())), preferred_element_type=F32)


def dot_tn(a, b):
    return lax.dot_general(a, b, (((0,), (0,)), ((), ())), preferred_element_type=F32)


def layer_norm(values, gain, shift):
    centred = values - jnp.mean(values, axis=-1, keepdims=True)
    inverse = lax.rsqrt(jnp.mean(centred * centred, axis=-1, keepdims=True) + 1e-06)
    normed = centred * inverse
    return normed * gain + shift, normed, inverse


def norm_back(upstream, normed, inverse, gain):
    scaled = upstream * gain
    inner = (
        scaled
        - jnp.mean(scaled, axis=-1, keepdims=True)
        - normed * jnp.mean(scaled * normed, axis=-1, keepdims=True)
    )
    return (
        inner * inverse,
        jnp.sum(upstream * normed, axis=0, keepdims=True),
        jnp.sum(upstream, axis=0, keepdims=True),
    )


def step_kernel(sizes, *refs):
    NR, NF, S, D, rows = sizes
    NX, NZ, NG = 2, NF // 2, NR // TP
    N, nr = NR * NF, D // NF
    HI = lax.Precision.HIGHEST
    (
        ids_in, idcol_in, gn_in, table_in, pieces_in, cos_in, sin_in, present_in, keymask_in,
        share_in, pairs_in,
        ids_out, fin_out, ng_out, stats_out, ge_out,
        pool, W7, GW, EX, GNB, sids, H0B, QKV, ATT, PS, H1, MIX, DF, DG, DQB, DB,
        INV, YS, YR, PB, PROW, PM, XR, ZS, ZR, CRA, YRA, NGS, NGR, NGZ, SQ, SQS, FG, TABLE,
        ssem, rsem, lsem,
    ) = refs
    r = lax.axis_index("rep")
    f = lax.axis_index("fsdp")
    d = r * NF + f
    z, x = lax.div(f, NX), lax.rem(f, NX)
    g, t = lax.div(r, TP), lax.rem(r, TP)
    y, c = lax.div(t, 2), lax.rem(t, 2)
    ty = (1 - y) * 2 + c
    tc = y * 2 + 1 - c
    tyc = (1 - y) * 2 + 1 - c
    dev_x = (r, z * NX + 1 - x)
    dev_y = (g * TP + ty, f)
    dev_c = (g * TP + tc, f)

    GATE, UP, PT, PT2 = 0, 4 * S, 8 * S, 12 * S
    CR, CR2 = 16 * S, 18 * S
    H0F, H1F, HAT, DS2, DS1, DQ = 20 * S, 21 * S, 22 * S, 25 * S, 26 * S, 27 * S

    def blk(offset, index=0):
        return pl.ds(pl.multiple_of(offset + index * S, 128), S)

    sem_at = {}
    for name, many in (
        ("ids", 1), ("gn", 1), ("ex", NZ), ("ez", NZ), ("wu", 4 * NZ), ("wd", 4 * NZ), ("wx", 4 * NZ),
        ("ay", NF), ("ac", 2 * NF), ("h1", 3), ("fc", 2), ("fy", 1), ("pool", 1), ("df", 3),
        ("bc", 2), ("by", 1), ("gx", 4 * NZ), ("gz", 4 * NZ), ("qc", 2), ("qy", 1), ("nc", 1), ("ny", 1),
        ("nx", 1), ("nz", NZ), ("ng", NG), ("fin", 3), ("gg", NG), ("sq", 1), ("eu", 2 * NZ), ("ed", 2 * NZ),
        ("gex", NZ), ("gey", NZ), ("gez", 2 * NZ), ("e1", 1), ("e3", 4), ("eg", NG),
    ):
        sem_at[name] = (sum(n for _, n in sem_at.values()), many)
    later = []

    def copy(name, index, src, dst, dev, landing=None):
        base = sem_at[name][0]
        return pltpu.make_async_remote_copy(
            src_ref=src, dst_ref=dst, send_sem=ssem.at[base + index],
            recv_sem=rsem.at[base + (index if landing is None else landing)],
            device_id=dev, device_id_type=MESH,
        )

    def send(name, index, src, dst, dev, only=None, landing=None):
        def start():
            copy(name, index, src, dst, dev, landing).start()

        def finish():
            copy(name, index, src, dst, dev, landing).wait_send()

        if only is None:
            start()
            later.append(finish)
        else:
            pl.when(only)(start)
            later.append(lambda: pl.when(only)(finish))

    def arrive(name, index, dst, only=None):
        def wait():
            sem = rsem.at[sem_at[name][0] + index]
            pltpu.make_async_copy(dst, dst, sem).wait()

        if only is None:
            wait()
        else:
            pl.when(only)(wait)

    def spread(name, src, dst):
        base = sem_at[name][0]

        def one(k, carry):
            to = lax.rem(d + k, N)
            pltpu.make_async_remote_copy(
                src_ref=src, dst_ref=dst.at[d], send_sem=ssem.at[base], recv_sem=rsem.at[base],
                device_id=(lax.div(to, NF), lax.rem(to, NF)), device_id_type=MESH,
            ).start()
            return carry

        lax.fori_loop(1, N, one, 0)
        rest = dst.at[pl.ds(0, N - 1)]
        later.append(lambda: pltpu.make_async_copy(rest, rest, ssem.at[base]).wait())

    def gather_all(name, dst):
        rest = dst.at[pl.ds(0, N - 1)]
        pltpu.make_async_copy(rest, rest, rsem.at[sem_at[name][0]]).wait()

    def keep(only, ref, at, value):
        @pl.when(only)
        def _():
            ref[at] = value

    def load(src, dst, sem):
        done = pltpu.make_async_copy(src, dst, lsem.at[sem])
        done.start()
        return done

    table = TABLE if rows % 8 else pool.at[pl.ds(0, rows)]
    got_table = load(table_in, table, 0)
    slots = [t, 4, 5, 6]

    def wrow(index):
        return pl.ds(pl.multiple_of(index * nr, 16), nr)

    got_piece = [load(pieces_in.at[t, m], W7.at[slots[m], wrow(f)], 1 + m) for m in range(4)]
    got_ids = load(ids_in, ids_out.at[d], 5)
    got_gn = load(gn_in, GNB.at[f], 6)
    barrier = pltpu.get_barrier_semaphore()

    def greet(k, carry):
        to = lax.rem(d + k, N)
        pl.semaphore_signal(
            barrier, inc=1, device_id=(lax.div(to, NF), lax.rem(to, NF)), device_id_type=MESH
        )
        return carry

    lax.fori_loop(1, N, greet, 0)
    got_ids.wait()
    got_gn.wait()
    for item in got_piece:
        item.wait()
    pl.semaphore_wait(barrier, N - 1)

    spread("ids", ids_out.at[d], ids_out)
    base = sem_at["gn"][0]

    def gn_one(k, carry):
        pltpu.make_async_remote_copy(
            src_ref=GNB.at[f], dst_ref=GNB.at[f], send_sem=ssem.at[base], recv_sem=rsem.at[base],
            device_id=(r, lax.rem(f + k, NF)), device_id_type=MESH,
        ).start()
        return carry

    lax.fori_loop(1, NF, gn_one, 0)
    gn_rest = GNB.at[pl.ds(0, NF - 1)]
    later.append(lambda: pltpu.make_async_copy(gn_rest, gn_rest, ssem.at[base]).wait())

    def piece(m, origin_z, origin_x):
        return W7.at[slots[m], wrow(origin_z * NX + origin_x)]

    def up_to(m, origin, only):
        send("wu", m * NZ + origin, piece(m, origin, x), piece(m, origin, x), (r, f + NX), only)

    def down_to(m, origin, only):
        send("wd", m * NZ + origin, piece(m, origin, x), piece(m, origin, x), (r, f - NX), only)

    def across(m, origin, only=None):
        send("wx", m * NZ + origin, piece(m, origin, x), piece(m, origin, x), dev_x, only)

    def own_pieces(m):
        up_to(m, z, z + 1 < NZ)
        down_to(m, z, z >= 1)
        across(m, z)

    def relay(m):
        for k in range(1, NZ):
            low, high = z - k, z + k
            below, above = jnp.maximum(low, 0), jnp.minimum(high, NZ - 1)
            arrive("wu", m * NZ + below, piece(m, below, x), low >= 0)
            up_to(m, below, (low >= 0) & (z + 1 < NZ))
            across(m, below, low >= 0)
            arrive("wd", m * NZ + above, piece(m, above, x), high < NZ)
            down_to(m, above, (high < NZ) & (z >= 1))
            across(m, above, high < NZ)

    own_pieces(0)
    own_pieces(1)

    gather_all("ids", ids_out)
    got_sids = load(ids_out.at[pl.ds(pl.multiple_of(r * NF, NF), NF)], sids, 5)
    got_sids.wait()
    got_table.wait()
    start_row = f * rows
    EXS, EXO, EXR, EZR = (EX.at[i] for i in range(4))

    def rows_of(other, store):
        stage = pool.at[pl.ds(0 if rows % 8 else rows, S)]

        def block(i, carry):
            owner = i * NX + other

            def token(j, inner):
                wanted = sids[owner, 0, j] - start_row
                inside = (wanted >= 0) & (wanted < rows)
                row = table[pl.ds(jnp.clip(wanted, 0, rows - 1), 1), :]
                stage[pl.ds(j, 1), :] = jnp.where(inside, row, 0.0)
                return inner

            lax.fori_loop(0, S, token, 0, unroll=8)
            store(i, stage[...].astype(BF))
            return carry

        lax.fori_loop(0, NZ, block, 0)

    def store_other(i, value):
        EXS[i] = value

    def store_own(i, value):
        EXO[i] = value

    rows_of(1 - x, store_other)
    for i in range(NZ):
        send("ex", i, EXS.at[i], EXR.at[i], dev_x)
    rows_of(x, store_own)
    relay(0)
    own_pieces(2)
    for i in range(NZ):
        arrive("ex", i, EXR.at[i])
        total = EXO[i] + EXR[i]
        EXO[i] = total
        keep(z == i, EZR, i, total)
        send("ez", i, EXO.at[i], EZR.at[z], (r, i * NX + x), z != i, z)

    for i in range(NZ):
        arrive("wx", i, piece(0, i, 1 - x))
    for i in range(NF):
        here = W7.at[t, wrow(i)]
        send("ay", i, here, here, dev_y)
        send("ac", i, here, here, dev_c)
    relay(1)
    own_pieces(3)
    for i in range(NF):
        there = W7.at[ty, wrow(i)]
        arrive("ay", i, there)
        send("ac", NF + i, there, there, dev_c)

    arrive("gn", 0, gn_rest)
    tiles = jnp.concatenate([GNB[i] for i in range(NF)], axis=1).astype(BF)
    at_row = lax.broadcasted_iota(jnp.int32, (NF * 128, D), 0)
    at_col = lax.broadcasted_iota(jnp.int32, (NF * 128, D), 1)
    lane = lax.bitwise_and(at_row, 127)
    pick = (lane < nr) & (lax.shift_right_logical(at_row, 7) * nr + lane == at_col)
    gains = dot(tiles, jnp.where(pick, 1.0, 0.0).astype(BF))
    gain = [gains[i : i + 1] for i in range(6)]

    for i in range(NZ):
        pl.when(z != i)(functools.partial(arrive, "ez", i, EZR.at[i]))
    embedded = EZR[0].astype(F32)
    for i in range(1, NZ):
        embedded = embedded + EZR[i].astype(F32)
    normed, hat, inverse = layer_norm(embedded, gain[0], gain[1])
    pool[blk(H0F), :] = normed
    pool[blk(HAT, 0), :] = hat
    INV[0] = inverse
    H0B[...] = normed.astype(BF)
    relay(2)

    for i in range(NF):
        arrive("ac", i, W7.at[tc, wrow(i)])
    for i in range(NF):
        arrive("ac", NF + i, W7.at[tyc, wrow(i)])
    tables = [jnp.concatenate([ref[...]] * (D // 128), axis=1) for ref in (cos_in, sin_in)]
    in_half = lax.bitwise_and(lax.broadcasted_iota(jnp.int32, (S, D), 1), HD - 1) < HD // 2

    def turn(values, sign):
        partner = jnp.where(
            in_half, pltpu.roll(values, D - HD // 2, 1), pltpu.roll(values, HD // 2, 1)
        )
        signed = jnp.where(in_half, -sign, sign) * tables[1]
        return values * tables[0] + partner * signed

    for j in range(3):
        projected = dot(H0B[...], W7[j])
        QKV[j] = (turn(projected, 1.0) if j < 2 else projected).astype(BF)
    allowed = keymask_in[...][0:1, :] > 0.0
    scaling = HD ** (-0.5)
    first_half = lax.broadcasted_iota(jnp.int32, (S, 128), 1) < HD

    def half(values, which):
        keep = first_half if which == 0 else jnp.logical_not(first_half)
        return jnp.where(keep, values, jnp.zeros_like(values))

    def attend(p, carry):
        lanes = pl.ds(pl.multiple_of(p * 128, 128), 128)
        query, keys, values = QKV[0, :, lanes], QKV[1, :, lanes], QKV[2, :, lanes]
        result = jnp.zeros((S, 128), F32)
        for which in range(2):
            scores = dot_nt(query, half(keys, which)) * scaling
            scores = jnp.where(allowed, scores, -1000000000.0)
            raised = jnp.exp(scores - jnp.max(scores, axis=-1, keepdims=True))
            chances = raised / jnp.sum(raised, axis=-1, keepdims=True)
            PS[2 * p + which] = chances
            result = result + dot(chances.astype(BF), half(values, which))
        ATT[:, lanes] = result.astype(BF)
        return carry

    lax.fori_loop(0, D // 128, attend, 0)
    branch = dot(ATT[...], W7[3])
    normed, hat, inverse = layer_norm(pool[blk(H0F), :] + branch, gain[2], gain[3])
    pool[blk(H1F), :] = normed
    pool[blk(HAT, 1), :] = hat
    INV[1] = inverse
    H1[t] = normed.astype(BF)

    def share(name, buffer):
        send(name, 0, buffer.at[t], buffer.at[t], dev_y)
        send(name, 1, buffer.at[t], buffer.at[t], dev_c)
        arrive(name, 0, buffer.at[ty])
        send(name, 2, buffer.at[ty], buffer.at[ty], dev_c)
        arrive(name, 1, buffer.at[tc])
        arrive(name, 2, buffer.at[tyc])

    def reduce(names, offset, landing, which):
        for i in range(2):
            send(names[0], i, pool.at[blk(offset, i * 2 + 1 - c)], pool.at[blk(landing, i)], dev_c)
        for i in range(2):
            arrive(names[0], i, pool.at[blk(landing, i)])
        away = pool[blk(offset, (1 - y) * 2 + c), :] + pool[blk(landing, 1 - y), :]
        YS[which] = away.astype(BF)
        send(names[1], 0, YS.at[which], YR.at[which], dev_y)
        mine = pool[blk(offset, t), :] + pool[blk(landing, y), :]
        arrive(names[1], 0, YR.at[which])
        return mine + YR[which].astype(F32)

    share("h1", H1)
    relay(3)
    for m in range(1, 4):
        for i in range(NZ):
            arrive("wx", m * NZ + i, piece(m, i, 1 - x))

    def forward(b, carry):
        gate, up = dot(H1[b], W7[4]), dot(H1[b], W7[5])
        pool[blk(GATE, b), :] = gate
        pool[blk(UP, b), :] = up
        mixed = (gate / (1.0 + jnp.exp(-gate)) * up).astype(BF)
        MIX[b] = mixed
        pool[blk(PT, b), :] = dot(mixed, W7[6])
        return carry

    lax.fori_loop(0, TP, forward, 0)
    feed = reduce(("fc", "fy"), PT, CR, 0)
    normed, hat, inverse = layer_norm(pool[blk(H1F), :] + feed, gain[4], gain[5])
    pool[blk(HAT, 2), :] = hat
    INV[2] = inverse
    PROW[0] = jnp.sum(normed * present_in[...][:, 0:1], axis=0, keepdims=True) / share_in[...][0:1, 0:1]

    spread("pool", PROW.at[0], PB)
    PB[d] = PROW[0]
    gather_all("pool", PB)
    for i in range(N):
        PM[pl.ds(i, 1), :] = PB[i]
    pooled = PM[...]
    wide = lax.broadcasted_iota(jnp.int32, (N, D), 1)
    row_at = lax.broadcasted_iota(jnp.int32, (N, N), 0)
    col_at = lax.broadcasted_iota(jnp.int32, (N, N), 1)
    paired = pairs_in[...]
    loss_value = jnp.zeros((1, 1), F32)
    d_pooled = jnp.zeros((N, D), F32)
    for width in (D // 12, D // 3, D):
        portion = jnp.where(wide < width, pooled, 0.0)
        inverse = lax.rsqrt(jnp.sum(portion * portion, axis=1, keepdims=True) + 1e-06)
        unit = portion * inverse
        similar = lax.dot_general(
            unit, unit, (((1,), (1,)), ((), ())), precision=HI, preferred_element_type=F32
        ) / logit_divisor
        similar = jnp.where(row_at == col_at, -1000000000.0, similar)
        row_max = jnp.max(similar, axis=1, keepdims=True)
        raised = jnp.exp(similar - row_max)
        total = jnp.sum(raised, axis=1, keepdims=True)
        target = jnp.sum(jnp.where(paired > 0.0, similar, 0.0), axis=1, keepdims=True)
        term = row_max + jnp.log(total) - target
        loss_value = loss_value + jnp.sum(term, axis=0, keepdims=True) / N
        col_max = jnp.max(similar, axis=0, keepdims=True)
        raised_t = jnp.exp(similar - col_max)
        turned = raised_t / jnp.sum(raised_t, axis=0, keepdims=True)
        d_similar = (raised / total + turned - 2.0 * paired) / (3.0 * N) / logit_divisor
        d_unit = lax.dot_general(
            d_similar, unit, (((1,), (0,)), ((), ())), precision=HI, preferred_element_type=F32
        )
        inner = jnp.sum(d_unit * unit, axis=1, keepdims=True)
        d_pooled = d_pooled + inverse * (d_unit - unit * inner)
    loss_value = loss_value / 3.0
    own_row = lax.broadcasted_iota(jnp.int32, (N, D), 0) == d
    d_mine = jnp.sum(jnp.where(own_row, d_pooled, 0.0), axis=0, keepdims=True)

    d_two = d_mine * present_in[...][:, 0:1] / share_in[...][0:1, 0:1]
    d_sum, d_gain_two, d_shift_two = norm_back(d_two, pool[blk(HAT, 2), :], INV[2], gain[4])
    pool[blk(DS2), :] = d_sum
    DF[t] = d_sum.astype(BF)
    share("df", DF)

    def back(b, carry):
        d_mixed = dot_nt(DF[b], W7[6])
        gate, up = pool[blk(GATE, b), :], pool[blk(UP, b), :]
        logistic = 1.0 / (1.0 + jnp.exp(-gate))
        d_gate = (d_mixed * up * (logistic * (1.0 + gate * (1.0 - logistic)))).astype(BF)
        d_up = (d_mixed * (gate * logistic)).astype(BF)
        DG[0, b] = d_gate
        DG[1, b] = d_up
        pool[blk(PT2, b), :] = dot_nt(d_gate, W7[4]) + dot_nt(d_up, W7[5])
        return carry

    TILE = 256

    def product(left, right, m):
        def tile(i, carry):
            at = pl.ds(pl.multiple_of(i * TILE, TILE), TILE)
            GW[m, at, :] = dot_tn(left(at), right()).astype(BF)
            return carry

        lax.fori_loop(0, D // TILE, tile, 0)

    def part(m, i, other):
        return GW.at[slots[m], wrow(i * NX + other)]

    def give(m):
        for i in range(NZ):
            send("gx", m * NZ + i, part(m, i, 1 - x), XR.at[m, i], dev_x)

    def pass_on(m):
        for i in range(NZ):
            arrive("gx", m * NZ + i, XR.at[m, i])
            total = (part(m, i, x)[...].astype(F32) + XR[m, i].astype(F32)).astype(BF)
            ZS[m, i] = total
            keep(z == i, ZR, (m, i), total)
            send("gz", m * NZ + i, ZS.at[m, i], ZR.at[m, z], (r, i * NX + x), z != i, m * NZ + z)

    def product_rows(buffer):
        return lambda at: buffer[:, :, at].reshape(TP * S, TILE)

    product(product_rows(MIX), lambda: DF[...].reshape(TP * S, D), 6)
    give(3)
    lax.fori_loop(0, TP, back, 0)
    for i in range(2):
        send("bc", i, pool.at[blk(PT2, i * 2 + 1 - c)], pool.at[blk(CR2, i)], dev_c)
    product(product_rows(H1), lambda: DG[0].reshape(TP * S, D), 4)
    give(1)
    for i in range(2):
        arrive("bc", i, pool.at[blk(CR2, i)])
    away = pool[blk(PT2, (1 - y) * 2 + c), :] + pool[blk(CR2, 1 - y), :]
    YS[1] = away.astype(BF)
    send("by", 0, YS.at[1], YR.at[1], dev_y)
    product(product_rows(H1), lambda: DG[1].reshape(TP * S, D), 5)
    give(2)
    pass_on(3)
    mine = pool[blk(PT2, t), :] + pool[blk(CR2, y), :]
    arrive("by", 0, YR.at[1])
    d_one = pool[blk(DS2), :] + (mine + YR[1].astype(F32))

    d_sum, d_gain_one, d_shift_one = norm_back(d_one, pool[blk(HAT, 1), :], INV[1], gain[2])
    pool[blk(DS1), :] = d_sum
    DB[0] = d_sum.astype(BF)
    product(lambda at: ATT[:, at], lambda: DB[0], 3)
    DB[1] = dot_nt(DB[0], W7[3]).astype(BF)
    pass_on(1)

    def attend_back(p, carry):
        lanes = pl.ds(pl.multiple_of(p * 128, 128), 128)
        query, keys, values = QKV[0, :, lanes], QKV[1, :, lanes], QKV[2, :, lanes]
        grad = DB[1, :, lanes]
        d_query = jnp.zeros((S, 128), F32)
        d_keys = jnp.zeros((S, 128), F32)
        d_values = jnp.zeros((S, 128), F32)
        for which in range(2):
            chances = PS[2 * p + which]
            d_values = d_values + dot_tn(chances.astype(BF), half(grad, which))
            d_chances = dot_nt(grad, half(values, which))
            inner = jnp.sum(chances * d_chances, axis=-1, keepdims=True)
            d_scores = (chances * (d_chances - inner)).astype(BF)
            d_query = d_query + dot(d_scores, half(keys, which)) * scaling
            d_keys = d_keys + dot_tn(d_scores, half(query, which)) * scaling
        pool[blk(DQ, 0), lanes] = d_query
        pool[blk(DQ, 1), lanes] = d_keys
        DQB[2, :, lanes] = d_values.astype(BF)
        return carry

    lax.fori_loop(0, D // 128, attend_back, 0)
    for j in range(2):
        DQB[j] = turn(pool[blk(DQ, j), :], -1.0).astype(BF)

    def attend_weights(j, carry):
        def tile(i, inner):
            at = pl.ds(pl.multiple_of(i * TILE, TILE), TILE)
            GW[j, at, :] = dot_tn(H0B[:, at], DQB[j]).astype(BF)
            return inner

        return lax.fori_loop(0, D // TILE, tile, carry)

    lax.fori_loop(0, 3, attend_weights, 0)
    for i in range(2):
        send("qc", i, GW.at[i * 2 + 1 - c], CRA.at[i], dev_c)
    d_zero = pool[blk(DS1), :]
    for j in range(3):
        d_zero = d_zero + dot_nt(DQB[j], W7[j])
    d_embedded, d_gain_zero, d_shift_zero = norm_back(d_zero, pool[blk(HAT, 0), :], INV[0], gain[0])
    DB[2] = d_embedded.astype(BF)

    got_own = load(DB.at[2], ge_out.at[d], 0)
    cols = [pl.ds(0, D // 2), pl.ds(D // 2, D // 2)]

    def ge(order, origin):
        return ge_out.at[r * NF + origin * NX + x, :, cols[order]]

    def ge_up(order, origin, src, only):
        send("eu", order * NZ + origin, src, ge(order, origin), (r, f + NX), only)

    def ge_down(order, origin, src, only):
        send("ed", order * NZ + origin, src, ge(order, origin), (r, f - NX), only)

    for order in range(2):
        ge_up(order, z, DB.at[2, :, cols[order]], z + 1 < NZ)
        ge_down(order, z, DB.at[2, :, cols[order]], z >= 1)

    NGS[0] = jnp.concatenate(
        [d_gain_zero, d_shift_zero, d_gain_one, d_shift_one, d_gain_two, d_shift_two,
         jnp.zeros((2, D), F32)], axis=0)
    stages = (("nc", dev_c), ("ny", dev_y), ("nx", dev_x))
    for i, (name, dev) in enumerate(stages):
        send(name, 0, NGS.at[i], NGR.at[i], dev)
        arrive(name, 0, NGR.at[i])
        NGS[i + 1] = NGS[i] + NGR[i]
    for i in range(NZ):
        send("nz", i, NGS.at[3], NGZ.at[z], (r, i * NX + x), z != i, z)
        keep(z == i, NGZ, i, NGS[3])

    pass_on(2)
    for i in range(2):
        arrive("qc", i, CRA.at[i])

    def add_mats(target, other):
        def tile(i, carry):
            at = pl.ds(pl.multiple_of(i * TILE, TILE), TILE)
            GW[target, at, :] = (GW[target, at, :].astype(F32) + other[at, :].astype(F32)).astype(BF)
            return carry

        lax.fori_loop(0, D // TILE, tile, 0)

    add_mats(ty, CRA.at[1 - y])
    send("qy", 0, GW.at[ty], YRA, dev_y)
    add_mats(t, CRA.at[y])
    got_own.wait()

    for k in range(1, NZ):
        low, high = z - k, z + k
        below, above = jnp.maximum(low, 0), jnp.minimum(high, NZ - 1)
        for order in range(2):
            arrive("eu", order * NZ + below, ge(order, below), low >= 0)
            ge_up(order, below, ge(order, below), (low >= 0) & (z + 1 < NZ))
            arrive("ed", order * NZ + above, ge(order, above), high < NZ)
            ge_down(order, above, ge(order, above), (high < NZ) & (z >= 1))

    def line(rep, which_x, order, i):
        return ge_out.at[rep * NF + i * NX + which_x, :, cols[order]]

    def all_of(rep, order):
        return ge_out.at[pl.ds(pl.multiple_of(rep * NF, NF), NF), :, cols[order]]

    ry, rc, ryc = g * TP + ty, g * TP + tc, g * TP + tyc
    for i in range(NZ):
        copy_at = line(r, x, 0, i)
        send("gex", i, copy_at, copy_at, dev_x)
    for i in range(NZ):
        copy_at = line(r, x, 1, i)
        send("gey", i, copy_at, copy_at, dev_y)

    arrive("qy", 0, YRA)
    add_mats(t, YRA)
    give(0)

    for i in range(NZ):
        arrive("gex", i, line(r, 1 - x, 0, i))
    send("e1", 0, all_of(r, 0), all_of(r, 0), dev_y)
    send("e3", 0, all_of(r, 0), all_of(r, 0), dev_c)
    for i in range(NZ):
        arrive("gey", i, line(ry, x, 1, i))
    for i in range(NZ):
        for which, rep in enumerate((r, ry)):
            copy_at = line(rep, x, 1, i)
            send("gez", which * NZ + i, copy_at, copy_at, dev_x)
    pass_on(0)

    for i in range(NZ):
        pl.when(z != i)(functools.partial(arrive, "nz", i, NGZ.at[i]))
    total_norms = NGZ[0]
    for i in range(1, NZ):
        total_norms = total_norms + NGZ[i]

    for m in (3, 1, 2, 0):
        for i in range(NZ):
            pl.when(z != i)(functools.partial(arrive, "gz", m * NZ + i, ZR.at[m, i]))
        total = ZR[m, 0].astype(F32)
        for i in range(1, NZ):
            total = total + ZR[m, i].astype(F32)
        fin_out[t, pl.ds(m * nr, nr), :] = total.astype(BF)

    if NG > 1:
        FG[g] = fin_out[t]
        for k in range(1, NG):
            other = lax.rem(g + k, NG)
            send("gg", k, FG.at[g], FG.at[g], (other * TP + t, f), None, g)
        for k in range(1, NG):
            other = lax.rem(g + k, NG)
            arrive("gg", other, FG.at[other])
        total = FG[0].astype(F32)
        for k in range(1, NG):
            total = total + FG[k].astype(F32)
        fin_out[t] = total.astype(BF)
    own = fin_out[t].astype(F32)
    squares = jnp.where(g == 0, jnp.sum(own * own), 0.0)
    share("fin", fin_out)

    arrive("e1", 0, all_of(ry, 0))
    send("e3", 1, all_of(ry, 0), all_of(ry, 0), dev_c)
    for i in range(NZ):
        for which, rep in enumerate((r, ry)):
            arrive("gez", which * NZ + i, line(rep, 1 - x, 1, i))
    send("e3", 2, all_of(r, 1), all_of(r, 1), dev_c)
    send("e3", 3, all_of(ry, 1), all_of(ry, 1), dev_c)
    for which, (rep, order) in enumerate(((rc, 0), (ryc, 0), (rc, 1), (ryc, 1))):
        arrive("e3", which, all_of(rep, order))
    if NG > 1:

        def group(which):
            return ge_out.at[pl.ds(pl.multiple_of(which * TP * NF, TP * NF), TP * NF)]

        for k in range(1, NG):
            other = lax.rem(g + k, NG)
            send("eg", k, group(g), group(g), (other * TP + t, f), None, g)
        for k in range(1, NG):
            other = lax.rem(g + k, NG)
            arrive("eg", other, group(other))

    def fetch(b):
        return pltpu.make_async_copy(
            ge_out.at[pl.ds(b * NZ, NZ)], EX.at[2 + lax.rem(b, 2)], lsem.at[1 + lax.rem(b, 2)]
        )

    fetch(0).start()

    def pairs_of(b, carry):
        pl.when(b + 1 < N // NZ)(lambda: fetch(b + 1).start())
        fetch(b).wait()
        for i in range(NZ):
            both = dot_nt(DB[2], EX[2 + lax.rem(b, 2), i])
            carry = carry + jnp.where(idcol_in[...] == ids_out[b * NZ + i], both, 0.0)
        return carry

    both = lax.fori_loop(0, N // NZ, pairs_of, jnp.zeros((S, S), F32))
    squares = squares + jnp.sum(both)
    squares = squares + jnp.where(d == 0, jnp.sum(total_norms * total_norms), 0.0)
    SQ[0] = jnp.zeros((1, 128), F32) + squares
    spread("sq", SQ.at[0], SQS)
    SQS[d] = SQ[0]
    ng_out[...] = total_norms
    gather_all("sq", SQS)
    all_squares = SQS[0]
    for i in range(1, N):
        all_squares = all_squares + SQS[i]
    stats_out[...] = jnp.concatenate(
        [jnp.zeros((1, 128), F32) + loss_value, jnp.sqrt(all_squares), jnp.zeros((6, 128), F32)], axis=0
    )
    arrive_last = later
    for finish in arrive_last:
        finish()


def run_step(sizes, *args):
    NR, NF, S, D, rows = sizes
    NZ, NG = NF // 2, NR // TP
    N, nr = NR * NF, D // NF
    vmem = pl.BlockSpec(memory_space=pltpu.VMEM)
    hbm = pl.BlockSpec(memory_space=pl.ANY)
    sems = 13 + 23 * NZ + 3 * NF + 3 * NG + 27 + 8 * NZ
    shapes = [
        ((30 * S if rows % 8 else max(rows + S, 30 * S), D), F32),
        ((7, D, D), BF), ((7, D, D), BF), ((4, NZ, S, D), BF), ((NF, 8, 128), F32), None,
        ((S, D), BF), ((3, S, D), BF), ((S, D), BF), ((D // HD, S, S), F32), ((TP, S, D), BF),
        ((TP, S, D), BF), ((TP, S, D), BF), ((2, TP, S, D), BF), ((3, S, D), BF), ((3, S, D), BF),
        ((3, S, 1), F32), ((2, S, D), BF), ((2, S, D), BF), ((N, 1, D), F32), ((1, 1, D), F32), ((N, D), F32),
        ((4, NZ, nr, D), BF), ((4, NZ, nr, D), BF), ((4, NZ, nr, D), BF), ((2, D, D), BF), ((D, D), BF),
        ((4, 8, D), F32), ((3, 8, D), F32), ((NZ, 8, D), F32), ((1, 1, 128), F32), ((N, 1, 128), F32),
        ((NG, 4 * nr, D) if NG > 1 else (1, 16, 128), BF), ((rows, D) if rows % 8 else (8, 128), F32),
    ]
    scratch = [pltpu.VMEM(*item) if item else pltpu.SMEM((NF, 1, S), jnp.int32) for item in shapes]
    return pl.pallas_call(
        functools.partial(step_kernel, sizes),
        name="step",
        out_shape=(
            jax.ShapeDtypeStruct((N, 1, S), jnp.int32),
            jax.ShapeDtypeStruct((TP, 4 * nr, D), BF),
            jax.ShapeDtypeStruct((8, D), F32),
            jax.ShapeDtypeStruct((8, 128), F32),
            jax.ShapeDtypeStruct((N, S, D), BF),
        ),
        in_specs=[vmem, vmem, vmem, hbm, hbm] + [vmem] * 6,
        out_specs=(vmem, vmem, vmem, vmem, hbm),
        scratch_shapes=scratch
        + [pltpu.SemaphoreType.DMA((sems,)), pltpu.SemaphoreType.DMA((sems,)), pltpu.SemaphoreType.DMA((8,))],
        compiler_params=pltpu.CompilerParams(
            collective_id=0, has_side_effects=True, vmem_limit_bytes=67_000_000
        ),
    )(*args)


def adamw(weight, grad, first, second, rate):
    first_new = beta_first * first + (1.0 - beta_first) * grad
    second_new = beta_second * second + (1.0 - beta_second) * grad * grad
    first_fix = 1.0 - beta_first**STEP
    second_fix = 1.0 - beta_second**STEP
    update = first_new / first_fix / (jnp.sqrt(second_new / second_fix) + adam_floor)
    return (weight - rate * (update + weight_decay * weight), first_new, second_new)


def table_kernel(sizes, ids, ge, factor, w, m, v, w_out, m_out, v_out, grads, landing, stage, sems):
    NR, NF, S, D, rows = sizes
    N = NR * NF
    step = pl.program_id(0)
    block = w.shape[0]

    @pl.when(step == 0)
    def _():
        start_row = lax.axis_index("fsdp") * rows

        def fetch(s):
            return pltpu.make_async_copy(ge.at[s], landing.at[lax.rem(s, 4)], sems.at[lax.rem(s, 4)])

        for s in range(3):
            fetch(s).start()

        def clear(i, carry):
            grads[pl.ds(pl.multiple_of(i * block, 8), block), :] = jnp.zeros((block, D), F32)
            return carry

        lax.fori_loop(0, grads.shape[0] // block, clear, 0)

        def sequence(s, carry):
            pl.when(s + 3 < N)(lambda: fetch(s + 3).start())
            fetch(s).wait()
            stage[...] = landing[lax.rem(s, 4)].astype(F32)

            def token(j, inner):
                wanted = ids[s, 0, j] - start_row

                @pl.when((wanted >= 0) & (wanted < rows))
                def _():
                    at = pl.ds(wanted, 1)
                    grads[at, :] = grads[at, :] + stage[pl.ds(j, 1), :]

                return inner

            return lax.fori_loop(0, S, token, carry)

        lax.fori_loop(0, N, sequence, 0)

    grad = grads[pl.ds(pl.multiple_of(step * block, 8), block), :] * factor[0:1, 0:1]
    w_out[...], m_out[...], v_out[...] = adamw(w[...], grad, m[...], v[...], learn_rate)


def update_table(sizes, ids, ge, factor, w, m, v):
    NR, NF, S, D, rows = sizes
    block = 424
    steps = pl.cdiv(rows, block)
    part = pl.BlockSpec((block, D), lambda i: (i, 0))
    return pl.pallas_call(
        functools.partial(table_kernel, sizes),
        name="table",
        grid=(steps,),
        out_shape=(jax.ShapeDtypeStruct((rows, D), F32),) * 3,
        in_specs=[
            pl.BlockSpec(memory_space=pltpu.SMEM), pl.BlockSpec(memory_space=pl.ANY),
            pl.BlockSpec((8, 128), lambda i: (0, 0)), part, part, part,
        ],
        out_specs=(part, part, part),
        scratch_shapes=[
            pltpu.VMEM((steps * block, D), F32), pltpu.VMEM((4, S, D), BF), pltpu.VMEM((S, D), F32),
            pltpu.SemaphoreType.DMA((4,)),
        ],
        compiler_params=pltpu.CompilerParams(vmem_limit_bytes=60_000_000),
    )(ids, ge, factor, w, m, v)


def local(
    sizes,
    token_ids,
    lengths,
    slot_order,
    pair_labels,
    embedding,
    attend_weight,
    attention_output_matrix,
    gate_up,
    contract_kernel,
    norm_params,
    embedding_first,
    embedding_second,
    attend_first,
    attend_second,
    output_first,
    output_second,
    gate_up_first,
    gate_up_second,
    down_first,
    down_second,
    norm_first,
    norm_second,
):
    NR, NF, S, D, rows = sizes
    nr = D // NF
    f = lax.axis_index("fsdp")
    length = lengths[0]
    positions = jnp.arange(S)
    present = (positions < length).astype(F32)
    angles = (
        positions.astype(F32)[:, None]
        * (1000.0 ** (-2.0 * jnp.arange(HD // 2).astype(F32) / HD))[None, :]
    )
    cosine, sine = jnp.tile(jnp.cos(angles), (1, 128 * 2 // HD)), jnp.tile(jnp.sin(angles), (1, 128 * 2 // HD))
    partner = pair_labels[slot_order]
    paired = (partner[:, None] == slot_order[None, :]).astype(F32)
    gains = jnp.zeros((8, 128), F32).at[:6, :nr].set(norm_params.astype(BF).astype(F32))
    attention = jnp.concatenate(
        [attend_weight.reshape(nr, 3, D).transpose(1, 0, 2), attention_output_matrix[None]], axis=0
    ).astype(BF)
    hidden = gate_up.astype(BF).reshape(nr, 2, NF, TP, nr).transpose(3, 1, 0, 2, 4).reshape(TP, 2, nr, D)
    down = contract_kernel.astype(BF).reshape(TP, 1, nr, D)
    pieces = jnp.concatenate([attention[:, None], hidden, down], axis=1)
    ids, fin, norms, stats, ge = run_step(
        sizes,
        token_ids.reshape(1, S),
        jnp.broadcast_to(token_ids.reshape(S, 1), (S, 128)),
        gains,
        embedding,
        pieces,
        cosine,
        sine,
        jnp.broadcast_to(present[:, None], (S, 128)),
        jnp.broadcast_to(present[None, :], (8, S)),
        jnp.broadcast_to(length.astype(F32), (8, 128)),
        paired,
    )
    loss_value, grad_norm = stats[0, 0], stats[1, 0]
    factor = jnp.minimum(1.0, clip_level / (grad_norm + 1e-06))
    emb_next = update_table(
        sizes, ids, ge, jnp.broadcast_to(factor, (8, 128)), embedding, embedding_first, embedding_second
    )
    fin = fin.reshape(TP, 4, nr, D)
    grad_attend = fin[:3, 0].transpose(1, 0, 2).reshape(nr, 3 * D).astype(F32)
    grad_output = fin[3, 0].astype(F32)
    grad_hidden = (
        fin[:, 1:3].reshape(TP, 2, nr, NF, nr).transpose(2, 1, 3, 0, 4).reshape(nr, 8 * D).astype(F32)
    )
    grad_down = fin[:, 3].reshape(TP * nr, D).astype(F32)
    grad_norms = lax.dynamic_slice(norms, (0, f * nr), (6, nr))
    att_next = adamw(attend_weight, grad_attend * factor, attend_first, attend_second, learn_rate)
    out_next = adamw(
        attention_output_matrix, grad_output * factor, output_first, output_second, learn_rate
    )
    gate_next = adamw(gate_up, grad_hidden * factor, gate_up_first, gate_up_second, learn_rate)
    down_next = adamw(contract_kernel, grad_down * factor, down_first, down_second, learn_rate)
    norm_next = adamw(norm_params, grad_norms * factor, norm_first, norm_second, norm_rate)
    return (
        loss_value, grad_norm, *emb_next, *att_next, *out_next, *gate_next, *down_next, *norm_next
    )


def solution(mesh):
    NR, NF = mesh.shape["rep"], mesh.shape["fsdp"]
    rows_spec, cols_spec = P("fsdp", None), P(None, "fsdp")

    def step(*args):
        S, D, rows = args[0].shape[1], args[4].shape[1], args[4].shape[0] // NF
        run = jax.shard_map(
            functools.partial(local, (NR, NF, S, D, rows)),
            mesh=mesh,
            in_specs=(P(("rep", "fsdp"), None), P(("rep", "fsdp")), P(), P())
            + (rows_spec,) * 5 + (cols_spec,) + (rows_spec,) * 10 + (cols_spec,) * 2,
            out_specs=(P(), P()) + (rows_spec,) * 15 + (cols_spec,) * 3,
            check_vma=False,
        )
        return run(*args)

    return step
```

```python
import functools
import types

import jax
import jax.numpy as jnp
from jax import lax
from jax.experimental import pallas as pl
from jax.experimental.pallas import tpu as pltpu
from jax.sharding import PartitionSpec as P

H = 12
HD = 64
STEP = 4
TP = 4
MESH = pl.DeviceIdType.MESH
BF = jnp.bfloat16
F32 = jnp.float32

logit_divisor = 0.05
clip_level = 0.001
learn_rate = 0.02
norm_rate = 0.3
weight_decay = 0.01
beta_first = 0.5
beta_second = 0.75
adam_floor = 1e-08


def dot(a, b):
    return lax.dot_general(a, b, (((1,), (0,)), ((), ())), preferred_element_type=F32)


def dot_nt(a, b):
    return lax.dot_general(a, b, (((1,), (1,)), ((), ())), preferred_element_type=F32)


def dot_tn(a, b):
    return lax.dot_general(a, b, (((0,), (0,)), ((), ())), preferred_element_type=F32)


def layer_norm(values, gain, shift):
    centred = values - jnp.mean(values, axis=-1, keepdims=True)
    inverse = lax.rsqrt(jnp.mean(centred * centred, axis=-1, keepdims=True) + 1e-06)
    normed = centred * inverse
    return normed * gain + shift, normed, inverse


def norm_back(upstream, normed, inverse, gain):
    scaled = upstream * gain
    inner = (
        scaled
        - jnp.mean(scaled, axis=-1, keepdims=True)
        - normed * jnp.mean(scaled * normed, axis=-1, keepdims=True)
    )
    return (
        inner * inverse,
        jnp.sum(upstream * normed, axis=0, keepdims=True),
        jnp.sum(upstream, axis=0, keepdims=True),
    )


def step_layout(sizes):
    NR, NF, S, D, rows = sizes
    NZ, NG = NF // 2, NR // TP
    N, nr = NR * NF, D // NF
    block = (S, D)
    buffers = dict(
        pool=((max(0 if rows % 8 else rows, 30 * S), D), F32),
        table=((rows, D) if rows % 8 else (8, 128), F32),
        stage=(block, F32),
        W7=((7, D, D), BF),
        GW=((4, D, D), BF),
        EX=((4, NZ, S, D), BF),
        GNB=((NF, 8, 128), F32),
        H0B=(block, BF), QKV=((3, S, D), BF), ATT=(block, BF), PS=((D // HD, S, S), F32),
        H1=((TP, S, D), BF), MIX=((TP, S, D), BF), DF=((TP, S, D), BF), DG=((2, TP, S, D), BF),
        LX=((TP, S, D), BF), RX=((TP, S, D), BF), DQB=((3, S, D), BF), DB=((3, S, D), BF),
        INV=((3, S, 1), F32), YS=((2, S, D), BF), YR=((2, S, D), BF),
        PB=((N, 1, D), F32), PROW=((1, 1, D), F32), PM=((N, D), F32),
        XR=((4, NZ, nr, D), BF), ZS=((4, NZ, nr, D), BF), ZR=((4, NZ, nr, D), BF),
        NGS=((4, 8, D), F32), NGR=((3, 8, D), F32), NGZ=((NZ, 8, D), F32),
        SQ=((1, 1, 128), F32), SQS=((N, 1, 128), F32),
        FG=((NG, 4 * nr, D) if NG > 1 else (1, 16, 128), BF),
    )
    copies = dict(
        ids=1, gn=1, ex=NZ, ez=NZ, wu=3 * NZ, wd=3 * NZ, wx0=NZ, wx1=NZ, wx2=NZ, wx3=NZ, vu=2 * NZ, vd=2 * NZ, ay=NF, ac=2 * NF,
        h1=3, fc=2, fy=1, pool=1, df=3, bc=2, by=1, lx=TP, rx=TP, gx=4 * NZ, gz=4 * NZ, nc=1, ny=1, nx=1,
        nz=NZ, ff=3, fa=3, gg=2 * NG, sq=1, eu=2 * NZ, ed=2 * NZ, gex=NZ, gey=NZ, gez=2 * NZ, e1=1, e3=4, eg=NG,
    )
    return buffers, copies


def step_kernel(sizes, *refs):
    NR, NF, S, D, rows = sizes
    NX, NZ, NG = 2, NF // 2, NR // TP
    N, nr = NR * NF, D // NF
    HI = lax.Precision.HIGHEST
    buffers, copies = step_layout(sizes)
    given = (
        "length_in", "ids_in", "gn_in", "order_in", "labels_in", "cos_in", "sin_in", "pieces_in", "w_in",
        "ids_out", "ff_out", "fa_out", "ng_out", "stats_out", "ge_out",
    )
    v = types.SimpleNamespace(**dict(zip((*given, *buffers, "sids", "ssem", "rsem", "lsem"), refs, strict=True)))
    pool, W7, GW, DB, DQB, QKV = v.pool, v.W7, v.GW, v.DB, v.DQB, v.QKV
    ssem, rsem, lsem, ids_out, ge_out = v.ssem, v.rsem, v.lsem, v.ids_out, v.ge_out
    r = lax.axis_index("rep")
    f = lax.axis_index("fsdp")
    d = r * NF + f
    z, x = lax.div(f, NX), lax.rem(f, NX)
    g, t = lax.div(r, TP), lax.rem(r, TP)
    y, c = lax.div(t, 2), lax.rem(t, 2)
    ty = (1 - y) * 2 + c
    tc = y * 2 + 1 - c
    tyc = (1 - y) * 2 + 1 - c
    dev_x = (r, z * NX + 1 - x)
    dev_y = (g * TP + ty, f)
    dev_c = (g * TP + tc, f)

    GATE, UP, PT, PT2 = 0, 4 * S, 8 * S, 12 * S
    CR, CR2 = 16 * S, 18 * S
    H0F, H1F, HAT, DS2, DS1, DQ = 20 * S, 21 * S, 22 * S, 25 * S, 26 * S, 27 * S

    def blk(offset, index=0):
        return pl.ds(pl.multiple_of(offset + index * S, 128), S)

    sem_at, used = {}, 0
    for name, many in copies.items():
        sem_at[name] = used
        used += many
    later = []

    def copy(name, index, src, dst, dev, landing=None):
        base = sem_at[name]
        return pltpu.make_async_remote_copy(
            src_ref=src, dst_ref=dst, send_sem=ssem.at[base + index],
            recv_sem=rsem.at[base + (index if landing is None else landing)],
            device_id=dev, device_id_type=MESH,
        )

    def send(name, index, src, dst, dev, only=None, landing=None):
        def start():
            copy(name, index, src, dst, dev, landing).start()

        def finish():
            copy(name, index, src, dst, dev, landing).wait_send()

        if only is None:
            start()
            later.append(finish)
        else:
            pl.when(only)(start)
            later.append(lambda: pl.when(only)(finish))

    def arrive(name, index, dst, only=None):
        def wait():
            pltpu.make_async_copy(dst, dst, rsem.at[sem_at[name] + index]).wait()

        if only is None:
            wait()
        else:
            pl.when(only)(wait)

    def spread(name, src, dst):
        base = sem_at[name]

        def one(k, carry):
            to = lax.rem(d + k, N)
            pltpu.make_async_remote_copy(
                src_ref=src, dst_ref=dst.at[d], send_sem=ssem.at[base], recv_sem=rsem.at[base],
                device_id=(lax.div(to, NF), lax.rem(to, NF)), device_id_type=MESH,
            ).start()
            return carry

        lax.fori_loop(1, N, one, 0)
        rest = dst.at[pl.ds(0, N - 1)]
        later.append(lambda: pltpu.make_async_copy(rest, rest, ssem.at[base]).wait())

    def gather_all(name, dst):
        rest = dst.at[pl.ds(0, N - 1)]
        pltpu.make_async_copy(rest, rest, rsem.at[sem_at[name]]).wait()

    def keep(only, ref, at, value):
        @pl.when(only)
        def _():
            ref[at] = value

    def load(src, dst, sem):
        done = pltpu.make_async_copy(src, dst, lsem.at[sem])
        done.start()
        return done

    table = v.table if rows % 8 else pool.at[pl.ds(0, rows)]
    got_table = load(v.w_in, table, 0)
    slots = [t, 4, 5, 6]

    def wrow(index):
        return pl.ds(pl.multiple_of(index * nr, 16), nr)

    got_piece = [load(v.pieces_in.at[t, m], W7.at[slots[m], wrow(f)], 1 + m) for m in range(4)]
    got_ids = load(v.ids_in, ids_out.at[d], 5)
    v.GNB[f] = jnp.zeros((8, 128), F32)
    v.GNB[f, 0:6, 0:nr] = v.gn_in[...].astype(BF).astype(F32)
    barrier = pltpu.get_barrier_semaphore()

    def greet(k, carry):
        to = lax.rem(d + k, N)
        pl.semaphore_signal(
            barrier, inc=1, device_id=(lax.div(to, NF), lax.rem(to, NF)), device_id_type=MESH
        )
        return carry

    lax.fori_loop(1, N, greet, 0)
    got_ids.wait()
    for item in got_piece:
        item.wait()
    pl.semaphore_wait(barrier, N - 1)

    spread("ids", ids_out.at[d], ids_out)

    def piece(m, origin_z, origin_x):
        return W7.at[slots[m], wrow(origin_z * NX + origin_x)]

    def up_to(m, origin, only, which):
        here = piece(m, origin, which)
        if m < 3:
            send("wu", m * NZ + origin, here, here, (r, f + NX), only)
        else:
            send("vu", which * NZ + origin, here, here, (r, f + NX), only)

    def down_to(m, origin, only, which):
        here = piece(m, origin, which)
        if m < 3:
            send("wd", m * NZ + origin, here, here, (r, f - NX), only)
        else:
            send("vd", which * NZ + origin, here, here, (r, f - NX), only)

    def across(m, origin, only=None):
        here = piece(m, origin, x)
        send(f"wx{m}", origin, here, here, dev_x, only)

    def publish(index, only=None):
        here = W7.at[t, wrow(index)]
        send("ay", index, here, here, dev_y, only)
        send("ac", index, here, here, dev_c, only)

    def own_pieces(m):
        up_to(m, z, z + 1 < NZ, x)
        down_to(m, z, z >= 1, x)
        across(m, z)

    def relay(m, k):
        low, high = z - k, z + k
        below, above = jnp.maximum(low, 0), jnp.minimum(high, NZ - 1)
        for which in (x,) if m < 3 else (x, 1 - x):
            first = m * NZ if m < 3 else which * NZ
            arrive("wu" if m < 3 else "vu", first + below, piece(m, below, which), low >= 0)
            up_to(m, below, (low >= 0) & (z + 1 < NZ), which)
            if m < 3:
                across(m, below, low >= 0)
            if m == 0:
                publish(below * NX + x, low >= 0)
            arrive("wd" if m < 3 else "vd", first + above, piece(m, above, which), high < NZ)
            down_to(m, above, (high < NZ) & (z >= 1), which)
            if m < 3:
                across(m, above, high < NZ)
            if m == 0:
                publish(above * NX + x, high < NZ)

    own_pieces(0)
    publish(f)
    base_gn = sem_at["gn"]

    def gn_one(k, carry):
        pltpu.make_async_remote_copy(
            src_ref=v.GNB.at[f], dst_ref=v.GNB.at[f], send_sem=ssem.at[base_gn], recv_sem=rsem.at[base_gn],
            device_id=(r, lax.rem(f + k, NF)), device_id_type=MESH,
        ).start()
        return carry

    lax.fori_loop(1, NF, gn_one, 0)
    gn_rest = v.GNB.at[pl.ds(0, NF - 1)]
    later.append(lambda: pltpu.make_async_copy(gn_rest, gn_rest, ssem.at[base_gn]).wait())
    for m in (1, 2, 3):
        own_pieces(m)

    gather_all("ids", ids_out)
    got_sids = load(ids_out.at[pl.ds(pl.multiple_of(r * NF, NF), NF)], v.sids, 5)
    got_sids.wait()
    got_table.wait()
    start_row = f * rows
    EXS, EXO, EXR, EZR = (v.EX.at[i] for i in range(4))

    def rows_of(i, other):
        owner = i * NX + other

        def token(j, inner):
            wanted = v.sids[owner, 0, j] - start_row
            inside = (wanted >= 0) & (wanted < rows)
            row = table[pl.ds(jnp.clip(wanted, 0, rows - 1), 1), :]
            v.stage[pl.ds(j, 1), :] = jnp.where(inside, row, 0.0)
            return inner

        lax.fori_loop(0, S, token, 0, unroll=8)
        return v.stage[...].astype(BF)

    steps = [(m, k) for k in range(1, NZ) for m in (0, 1, 2, 3)]
    jobs = [(i, True) for i in range(NZ)] + [(i, False) for i in range(NZ)]
    at_step = 0
    for number, (i, away) in enumerate(jobs):
        if away:
            EXS[i] = rows_of(i, 1 - x)
            send("ex", i, EXS.at[i], EXR.at[i], dev_x)
        else:
            EXO[i] = rows_of(i, x)
        if number == 1:
            arrive("wx3", z, piece(3, z, 1 - x))
            up_to(3, z, z + 1 < NZ, 1 - x)
            down_to(3, z, z >= 1, 1 - x)
        while at_step < len(steps) * (number + 1) // (len(jobs) + 2) - 1:
            relay(*steps[at_step])
            at_step += 1

    for i in range(NZ):
        arrive("ex", i, EXR.at[i])
        total = EXO[i] + EXR[i]
        EXO[i] = total
        keep(z == i, EZR, i, total)
        send("ez", i, EXO.at[i], EZR.at[z], (r, i * NX + x), z != i, z)
    while at_step < len(steps):
        relay(*steps[at_step])
        at_step += 1

    for i in range(NZ):
        arrive("wx0", i, piece(0, i, 1 - x))
        publish(i * NX + 1 - x)
    for i in range(NF):
        there = W7.at[ty, wrow(i)]
        arrive("ay", i, there)
        send("ac", NF + i, there, there, dev_c)

    arrive("gn", 0, gn_rest)
    tiles = jnp.concatenate([v.GNB[i] for i in range(NF)], axis=1).astype(BF)
    at_row = lax.broadcasted_iota(jnp.int32, (NF * 128, D), 0)
    at_col = lax.broadcasted_iota(jnp.int32, (NF * 128, D), 1)
    lane = lax.bitwise_and(at_row, 127)
    pick = (lane < nr) & (lax.shift_right_logical(at_row, 7) * nr + lane == at_col)
    gains = dot(tiles, jnp.where(pick, 1.0, 0.0).astype(BF))
    gain = [gains[i : i + 1] for i in range(6)]

    for i in range(NZ):
        pl.when(z != i)(functools.partial(arrive, "ez", i, EZR.at[i]))
    embedded = EZR[0].astype(F32)
    for i in range(1, NZ):
        embedded = embedded + EZR[i].astype(F32)
    normed, hat, inverse = layer_norm(embedded, gain[0], gain[1])
    pool[blk(H0F), :] = normed
    pool[blk(HAT, 0), :] = hat
    v.INV[0] = inverse
    v.H0B[...] = normed.astype(BF)

    def to_rank(name, which, src, buffer):
        send(name, which, src, buffer.at[t], (g * TP + which, f), t != which, t)
        keep(t == which, buffer, which, src[...])

    for which in range(3):
        to_rank("lx", which, v.H0B, v.LX)

    for i in range(NF):
        arrive("ac", i, W7.at[tc, wrow(i)])
    for i in range(NF):
        arrive("ac", NF + i, W7.at[tyc, wrow(i)])
    tables = [jnp.concatenate([ref[...]] * (D // 128), axis=1) for ref in (v.cos_in, v.sin_in)]
    in_half = lax.bitwise_and(lax.broadcasted_iota(jnp.int32, (S, D), 1), HD - 1) < HD // 2

    def turn(values, sign):
        partner = jnp.where(
            in_half, pltpu.roll(values, D - HD // 2, 1), pltpu.roll(values, HD // 2, 1)
        )
        signed = jnp.where(in_half, -sign, sign) * tables[1]
        return values * tables[0] + partner * signed

    for j in range(3):
        projected = dot(v.H0B[...], W7[j])
        QKV[j] = (turn(projected, 1.0) if j < 2 else projected).astype(BF)
    length = v.length_in[0]
    allowed = lax.broadcasted_iota(jnp.int32, (1, S), 1) < length
    scaling = HD ** (-0.5)
    first_half = lax.broadcasted_iota(jnp.int32, (S, 128), 1) < HD

    def half(values, which):
        keep = first_half if which == 0 else jnp.logical_not(first_half)
        return jnp.where(keep, values, jnp.zeros_like(values))

    def attend(p, carry):
        lanes = pl.ds(pl.multiple_of(p * 128, 128), 128)
        query, keys, values = QKV[0, :, lanes], QKV[1, :, lanes], QKV[2, :, lanes]
        result = jnp.zeros((S, 128), F32)
        for which in range(2):
            scores = dot_nt(query, half(keys, which)) * scaling
            scores = jnp.where(allowed, scores, -1000000000.0)
            raised = jnp.exp(scores - jnp.max(scores, axis=-1, keepdims=True))
            chances = raised / jnp.sum(raised, axis=-1, keepdims=True)
            v.PS[2 * p + which] = chances
            result = result + dot(chances.astype(BF), half(values, which))
        v.ATT[:, lanes] = result.astype(BF)
        return carry

    lax.fori_loop(0, D // 128, attend, 0)
    branch = dot(v.ATT[...], W7[3])
    normed, hat, inverse = layer_norm(pool[blk(H0F), :] + branch, gain[2], gain[3])
    pool[blk(H1F), :] = normed
    pool[blk(HAT, 1), :] = hat
    v.INV[1] = inverse
    v.H1[t] = normed.astype(BF)

    def share(name, buffer):
        send(name, 0, buffer.at[t], buffer.at[t], dev_y)
        send(name, 1, buffer.at[t], buffer.at[t], dev_c)
        arrive(name, 0, buffer.at[ty])
        send(name, 2, buffer.at[ty], buffer.at[ty], dev_c)
        arrive(name, 1, buffer.at[tc])
        arrive(name, 2, buffer.at[tyc])

    def reduce(names, offset, landing, which):
        for i in range(2):
            send(names[0], i, pool.at[blk(offset, i * 2 + 1 - c)], pool.at[blk(landing, i)], dev_c)
        for i in range(2):
            arrive(names[0], i, pool.at[blk(landing, i)])
        away = pool[blk(offset, (1 - y) * 2 + c), :] + pool[blk(landing, 1 - y), :]
        v.YS[which] = away.astype(BF)
        send(names[1], 0, v.YS.at[which], v.YR.at[which], dev_y)
        mine = pool[blk(offset, t), :] + pool[blk(landing, y), :]
        arrive(names[1], 0, v.YR.at[which])
        return mine + v.YR[which].astype(F32)

    share("h1", v.H1)
    to_rank("lx", 3, v.ATT, v.LX)
    for m in range(1, 3):
        for i in range(NZ):
            arrive(f"wx{m}", i, piece(m, i, 1 - x))

    def forward(b, carry):
        gate, up = dot(v.H1[b], W7[4]), dot(v.H1[b], W7[5])
        pool[blk(GATE, b), :] = gate
        pool[blk(UP, b), :] = up
        mixed = (gate / (1.0 + jnp.exp(-gate)) * up).astype(BF)
        v.MIX[b] = mixed
        pool[blk(PT, b), :] = dot(mixed, W7[6])
        return carry

    lax.fori_loop(0, TP, forward, 0)
    feed = reduce(("fc", "fy"), PT, CR, 0)
    normed, hat, inverse = layer_norm(pool[blk(H1F), :] + feed, gain[4], gain[5])
    pool[blk(HAT, 2), :] = hat
    v.INV[2] = inverse
    present = jnp.where(lax.broadcasted_iota(jnp.int32, (S, 1), 0) < length, 1.0, 0.0)
    share_of = length.astype(F32)
    v.PROW[0] = jnp.sum(normed * present, axis=0, keepdims=True) / share_of

    spread("pool", v.PROW.at[0], v.PB)
    v.PB[d] = v.PROW[0]
    gather_all("pool", v.PB)
    for i in range(N):
        v.PM[pl.ds(i, 1), :] = v.PB[i]
    pooled = v.PM[...]
    wide = lax.broadcasted_iota(jnp.int32, (N, D), 1)
    row_at = lax.broadcasted_iota(jnp.int32, (N, N), 0)
    col_at = lax.broadcasted_iota(jnp.int32, (N, N), 1)
    order, labels = v.order_in[...].astype(F32), v.labels_in[...].astype(F32)

    def column(row):
        return jnp.sum(jnp.where(row_at == col_at, row, 0.0), axis=1, keepdims=True)

    slot_has = jnp.where(column(order) == col_at.astype(F32), 1.0, 0.0).astype(BF)
    label_is = jnp.where(column(labels) == order, 1.0, 0.0).astype(BF)
    paired = dot(slot_has, label_is)
    loss_value = jnp.zeros((1, 1), F32)
    d_pooled = jnp.zeros((N, D), F32)
    for width in (D // 12, D // 3, D):
        portion = jnp.where(wide < width, pooled, 0.0)
        inverse = lax.rsqrt(jnp.sum(portion * portion, axis=1, keepdims=True) + 1e-06)
        unit = portion * inverse
        similar = lax.dot_general(
            unit, unit, (((1,), (1,)), ((), ())), precision=HI, preferred_element_type=F32
        ) / logit_divisor
        similar = jnp.where(row_at == col_at, -1000000000.0, similar)
        row_max = jnp.max(similar, axis=1, keepdims=True)
        raised = jnp.exp(similar - row_max)
        total = jnp.sum(raised, axis=1, keepdims=True)
        target = jnp.sum(jnp.where(paired > 0.0, similar, 0.0), axis=1, keepdims=True)
        term = row_max + jnp.log(total) - target
        loss_value = loss_value + jnp.sum(term, axis=0, keepdims=True) / N
        col_max = jnp.max(similar, axis=0, keepdims=True)
        raised_t = jnp.exp(similar - col_max)
        turned = raised_t / jnp.sum(raised_t, axis=0, keepdims=True)
        d_similar = (raised / total + turned - 2.0 * paired) / (3.0 * N) / logit_divisor
        d_unit = lax.dot_general(
            d_similar, unit, (((1,), (0,)), ((), ())), precision=HI, preferred_element_type=F32
        )
        inner = jnp.sum(d_unit * unit, axis=1, keepdims=True)
        d_pooled = d_pooled + inverse * (d_unit - unit * inner)
    loss_value = loss_value / 3.0
    own_row = lax.broadcasted_iota(jnp.int32, (N, D), 0) == d
    d_mine = jnp.sum(jnp.where(own_row, d_pooled, 0.0), axis=0, keepdims=True)

    d_two = d_mine * present / share_of
    d_sum, d_gain_two, d_shift_two = norm_back(d_two, pool[blk(HAT, 2), :], v.INV[2], gain[4])
    pool[blk(DS2), :] = d_sum
    v.DF[t] = d_sum.astype(BF)
    share("df", v.DF)

    def back(b, carry):
        d_mixed = dot_nt(v.DF[b], W7[6])
        gate, up = pool[blk(GATE, b), :], pool[blk(UP, b), :]
        logistic = 1.0 / (1.0 + jnp.exp(-gate))
        d_gate = (d_mixed * up * (logistic * (1.0 + gate * (1.0 - logistic)))).astype(BF)
        d_up = (d_mixed * (gate * logistic)).astype(BF)
        v.DG[0, b] = d_gate
        v.DG[1, b] = d_up
        pool[blk(PT2, b), :] = dot_nt(d_gate, W7[4]) + dot_nt(d_up, W7[5])
        return carry

    TILE = 256

    def product(left, right, m):
        def tile(i, carry):
            at = pl.ds(pl.multiple_of(i * TILE, TILE), TILE)
            GW[m, at, :] = dot_tn(left(at), right()).astype(BF)
            return carry

        lax.fori_loop(0, D // TILE, tile, 0)

    def part(m, i, other):
        return GW.at[m, wrow(i * NX + other)]

    def give(m):
        for i in range(NZ):
            send("gx", m * NZ + i, part(m, i, 1 - x), v.XR.at[m, i], dev_x)

    def pass_on(m):
        for i in range(NZ):
            arrive("gx", m * NZ + i, v.XR.at[m, i])
            total = (part(m, i, x)[...].astype(F32) + v.XR[m, i].astype(F32)).astype(BF)
            v.ZS[m, i] = total
            keep(z == i, v.ZR, (m, i), total)
            send("gz", m * NZ + i, v.ZS.at[m, i], v.ZR.at[m, z], (r, i * NX + x), z != i, m * NZ + z)

    def product_rows(buffer):
        return lambda at: buffer[:, :, at].reshape(TP * S, TILE)

    product(product_rows(v.MIX), lambda: v.DF[...].reshape(TP * S, D), 3)
    give(3)
    lax.fori_loop(0, TP, back, 0)
    for i in range(2):
        send("bc", i, pool.at[blk(PT2, i * 2 + 1 - c)], pool.at[blk(CR2, i)], dev_c)
    product(product_rows(v.H1), lambda: v.DG[0].reshape(TP * S, D), 1)
    give(1)
    for i in range(2):
        arrive("bc", i, pool.at[blk(CR2, i)])
    away = pool[blk(PT2, (1 - y) * 2 + c), :] + pool[blk(CR2, 1 - y), :]
    v.YS[1] = away.astype(BF)
    send("by", 0, v.YS.at[1], v.YR.at[1], dev_y)
    product(product_rows(v.H1), lambda: v.DG[1].reshape(TP * S, D), 2)
    give(2)
    pass_on(3)
    mine = pool[blk(PT2, t), :] + pool[blk(CR2, y), :]
    arrive("by", 0, v.YR.at[1])
    d_one = pool[blk(DS2), :] + (mine + v.YR[1].astype(F32))

    d_sum, d_gain_one, d_shift_one = norm_back(d_one, pool[blk(HAT, 1), :], v.INV[1], gain[2])
    pool[blk(DS1), :] = d_sum
    DB[0] = d_sum.astype(BF)
    to_rank("rx", 3, DB.at[0], v.RX)
    DB[1] = dot_nt(DB[0], W7[3]).astype(BF)
    pass_on(1)

    def attend_back(p, carry):
        lanes = pl.ds(pl.multiple_of(p * 128, 128), 128)
        query, keys, values = QKV[0, :, lanes], QKV[1, :, lanes], QKV[2, :, lanes]
        grad = DB[1, :, lanes]
        d_query = jnp.zeros((S, 128), F32)
        d_keys = jnp.zeros((S, 128), F32)
        d_values = jnp.zeros((S, 128), F32)
        for which in range(2):
            chances = v.PS[2 * p + which]
            d_values = d_values + dot_tn(chances.astype(BF), half(grad, which))
            d_chances = dot_nt(grad, half(values, which))
            inner = jnp.sum(chances * d_chances, axis=-1, keepdims=True)
            d_scores = (chances * (d_chances - inner)).astype(BF)
            d_query = d_query + dot(d_scores, half(keys, which)) * scaling
            d_keys = d_keys + dot_tn(d_scores, half(query, which)) * scaling
        pool[blk(DQ, 0), lanes] = d_query
        pool[blk(DQ, 1), lanes] = d_keys
        DQB[2, :, lanes] = d_values.astype(BF)
        return carry

    lax.fori_loop(0, D // 128, attend_back, 0)
    for j in range(2):
        DQB[j] = turn(pool[blk(DQ, j), :], -1.0).astype(BF)

    for which in range(3):
        to_rank("rx", which, DQB.at[which], v.RX)
    d_zero = pool[blk(DS1), :]
    for j in range(3):
        d_zero = d_zero + dot_nt(DQB[j], W7[j])
    d_embedded, d_gain_zero, d_shift_zero = norm_back(d_zero, pool[blk(HAT, 0), :], v.INV[0], gain[0])
    DB[2] = d_embedded.astype(BF)

    got_own = load(DB.at[2], ge_out.at[d], 0)
    cut = D * 2 // 3
    cols = [pl.ds(0, cut), pl.ds(cut, D - cut)]

    def line(rep, which_x, order, i):
        return ge_out.at[rep * NF + i * NX + which_x, :, cols[order]]

    def all_of(rep, order):
        return ge_out.at[pl.ds(pl.multiple_of(rep * NF, NF), NF), :, cols[order]]

    def ge_up(order, origin, src, only):
        send("eu", order * NZ + origin, src, line(r, x, order, origin), (r, f + NX), only)

    def ge_down(order, origin, src, only):
        send("ed", order * NZ + origin, src, line(r, x, order, origin), (r, f - NX), only)

    for order in range(2):
        ge_up(order, z, DB.at[2, :, cols[order]], z + 1 < NZ)
        ge_down(order, z, DB.at[2, :, cols[order]], z >= 1)

    def ge_relay(k):
        low, high = z - k, z + k
        below, above = jnp.maximum(low, 0), jnp.minimum(high, NZ - 1)
        for order in range(2):
            arrive("eu", order * NZ + below, line(r, x, order, below), low >= 0)
            ge_up(order, below, line(r, x, order, below), (low >= 0) & (z + 1 < NZ))
            arrive("ed", order * NZ + above, line(r, x, order, above), high < NZ)
            ge_down(order, above, line(r, x, order, above), (high < NZ) & (z >= 1))

    v.NGS[0] = jnp.concatenate(
        [d_gain_zero, d_shift_zero, d_gain_one, d_shift_one, d_gain_two, d_shift_two,
         jnp.zeros((2, D), F32)], axis=0)
    stages = (("nc", dev_c), ("ny", dev_y), ("nx", dev_x))

    def norm_send(i):
        send(stages[i][0], 0, v.NGS.at[i], v.NGR.at[i], stages[i][1])

    def norm_add(i):
        arrive(stages[i][0], 0, v.NGR.at[i])
        v.NGS[i + 1] = v.NGS[i] + v.NGR[i]

    norm_send(0)
    pass_on(2)
    for which in range(TP):
        arrive("lx", which, v.LX.at[which], t != which)
        arrive("rx", which, v.RX.at[which], t != which)
    product(product_rows(v.LX), lambda: v.RX[...].reshape(TP * S, D), 0)
    give(0)
    norm_add(0)
    norm_send(1)
    got_own.wait()
    ge_relay(1)
    norm_add(1)
    norm_send(2)

    def settle(m, out, at):
        for i in range(NZ):
            arrive("gz", m * NZ + i, v.ZR.at[m, i], z != i)
        total = v.ZR[m, 0].astype(F32)
        for i in range(1, NZ):
            total = total + v.ZR[m, i].astype(F32)
        out[t, at, :] = total.astype(BF)

    def group_sum(out, first, size):
        own = v.FG.at[g, pl.ds(first, size)]
        own[...] = out[t]
        for k in range(1, NG):
            other = lax.rem(g + k, NG)
            index = (0 if first else NG) + k
            send("gg", index, own, own, (other * TP + t, f), None, (0 if first else NG) + g)
        for k in range(1, NG):
            other = lax.rem(g + k, NG)
            arrive("gg", (0 if first else NG) + other, v.FG.at[other, pl.ds(first, size)])
        total = v.FG[0, pl.ds(first, size)].astype(F32)
        for k in range(1, NG):
            total = total + v.FG[k, pl.ds(first, size)].astype(F32)
        out[t] = total.astype(BF)

    settle(3, v.ff_out, pl.ds(2 * nr, nr))
    settle(1, v.ff_out, pl.ds(0, nr))
    for k in range(2, NZ):
        ge_relay(k)
    norm_add(2)
    for i in range(NZ):
        send("nz", i, v.NGS.at[3], v.NGZ.at[z], (r, i * NX + x), z != i, z)
        keep(z == i, v.NGZ, i, v.NGS[3])
    for i in range(NZ):
        here = line(r, x, 0, i)
        send("gex", i, here, here, dev_x)
    for i in range(NZ):
        here = line(r, x, 1, i)
        send("gey", i, here, here, dev_y)
    pass_on(0)
    settle(2, v.ff_out, pl.ds(nr, nr))
    if NG > 1:
        group_sum(v.ff_out, nr, 3 * nr)
    own = v.ff_out[t].astype(F32)
    squares = jnp.sum(own * own)
    ry, rc, ryc = g * TP + ty, g * TP + tc, g * TP + tyc
    for i in range(NZ):
        arrive("gex", i, line(r, 1 - x, 0, i))
    send("e1", 0, all_of(r, 0), all_of(r, 0), dev_y)
    send("e3", 0, all_of(r, 0), all_of(r, 0), dev_c)
    for i in range(NZ):
        arrive("gey", i, line(ry, x, 1, i))
    for i in range(NZ):
        for which, rep in enumerate((r, ry)):
            here = line(rep, x, 1, i)
            send("gez", which * NZ + i, here, here, dev_x)
    share("ff", v.ff_out)
    settle(0, v.fa_out, pl.ds(0, nr))
    if NG > 1:
        group_sum(v.fa_out, 0, nr)
    own = v.fa_out[t].astype(F32)
    squares = squares + jnp.sum(own * own)
    squares = jnp.where(g == 0, squares, 0.0)
    share("fa", v.fa_out)

    for i in range(NZ):
        arrive("nz", i, v.NGZ.at[i], z != i)
    total_norms = v.NGZ[0]
    for i in range(1, NZ):
        total_norms = total_norms + v.NGZ[i]
    arrive("e1", 0, all_of(ry, 0))
    send("e3", 1, all_of(ry, 0), all_of(ry, 0), dev_c)
    for i in range(NZ):
        for which, rep in enumerate((r, ry)):
            arrive("gez", which * NZ + i, line(rep, 1 - x, 1, i))
    send("e3", 2, all_of(r, 1), all_of(r, 1), dev_c)
    send("e3", 3, all_of(ry, 1), all_of(ry, 1), dev_c)
    for which, (rep, order) in enumerate(((rc, 0), (ryc, 0), (rc, 1), (ryc, 1))):
        arrive("e3", which, all_of(rep, order))
    if NG > 1:

        def group(which):
            return ge_out.at[pl.ds(pl.multiple_of(which * TP * NF, TP * NF), TP * NF)]

        for k in range(1, NG):
            other = lax.rem(g + k, NG)
            send("eg", k, group(g), group(g), (other * TP + t, f), None, g)
        for k in range(1, NG):
            other = lax.rem(g + k, NG)
            arrive("eg", other, group(other))

    def fetch(b):
        return pltpu.make_async_copy(
            ge_out.at[pl.ds(b * NZ, NZ)], v.EX.at[2 + lax.rem(b, 2)], lsem.at[1 + lax.rem(b, 2)]
        )

    fetch(0).start()
    same = lax.broadcasted_iota(jnp.int32, (S, S), 0) == lax.broadcasted_iota(jnp.int32, (S, S), 1)
    own_ids = jnp.sum(
        jnp.where(same, ids_out[d, :, pl.ds(0, S)].astype(F32), 0.0), axis=1, keepdims=True
    )

    def pairs_of(b, carry):
        pl.when(b + 1 < N // NZ)(lambda: fetch(b + 1).start())
        fetch(b).wait()
        for i in range(NZ):
            both = dot_nt(DB[2], v.EX[2 + lax.rem(b, 2), i])
            theirs = ids_out[b * NZ + i, :, pl.ds(0, S)].astype(F32)
            carry = carry + jnp.where(own_ids == theirs, both, 0.0)
        return carry

    both = lax.fori_loop(0, N // NZ, pairs_of, jnp.zeros((S, S), F32))
    squares = squares + jnp.sum(both)
    squares = squares + jnp.where(d == 0, jnp.sum(total_norms * total_norms), 0.0)
    v.SQ[0] = jnp.zeros((1, 128), F32) + squares
    spread("sq", v.SQ.at[0], v.SQS)
    v.SQS[d] = v.SQ[0]
    v.ng_out[...] = total_norms
    gather_all("sq", v.SQS)
    all_squares = v.SQS[0]
    for i in range(1, N):
        all_squares = all_squares + v.SQS[i]
    v.stats_out[...] = jnp.concatenate(
        [jnp.zeros((1, 128), F32) + loss_value, jnp.sqrt(all_squares), jnp.zeros((6, 128), F32)], axis=0
    )
    for finish in later:
        finish()


def run_step(sizes, *args):
    NR, NF, S, D, rows = sizes
    N, nr = NR * NF, D // NF
    vmem = pl.BlockSpec(memory_space=pltpu.VMEM)
    smem = pl.BlockSpec(memory_space=pltpu.SMEM)
    hbm = pl.BlockSpec(memory_space=pl.ANY)
    buffers, copies = step_layout(sizes)
    many = sum(copies.values())
    return pl.pallas_call(
        functools.partial(step_kernel, sizes),
        name="step",
        out_shape=(
            jax.ShapeDtypeStruct((N, 1, 2 * S), jnp.int32),
            jax.ShapeDtypeStruct((TP, 3 * nr, D), BF),
            jax.ShapeDtypeStruct((TP, nr, D), BF),
            jax.ShapeDtypeStruct((8, D), F32),
            jax.ShapeDtypeStruct((8, 128), F32),
            jax.ShapeDtypeStruct((N, S, D), BF),
        ),
        in_specs=[smem] + [vmem] * 6 + [hbm] * 2,
        out_specs=(vmem,) * 5 + (hbm,),
        scratch_shapes=[pltpu.VMEM(*item) for item in buffers.values()]
        + [
            pltpu.SMEM((NF, 1, 2 * S), jnp.int32), pltpu.SemaphoreType.DMA((many,)),
            pltpu.SemaphoreType.DMA((many,)), pltpu.SemaphoreType.DMA((8,)),
        ],
        compiler_params=pltpu.CompilerParams(
            collective_id=0, has_side_effects=True, vmem_limit_bytes=67_000_000
        ),
    )(*args)


def adamw(weight, grad, first, second, rate):
    first_new = beta_first * first + (1.0 - beta_first) * grad
    second_new = beta_second * second + (1.0 - beta_second) * grad * grad
    first_fix = 1.0 - beta_first**STEP
    second_fix = 1.0 - beta_second**STEP
    update = first_new / first_fix / (jnp.sqrt(second_new / second_fix) + adam_floor)
    return (weight - rate * (update + weight_decay * weight), first_new, second_new)


CHUNK, SLOTS = 424, 6


def finish_kernel(sizes, *refs):
    NR, NF, S, D, rows = sizes
    N, nr = NR * NF, D // NF
    names = ("ids", "ge", "ff", "fa", "norms", "stats", "pw", "pm", "pv") + tuple(
        f"{kind}{which}" for kind in "eaogd" for which in range(3)
    )
    results = ("qw", "qm", "qv") + tuple(f"{kind}{which}_new" for kind in "eaogd" for which in range(3))
    scratch = (
        "grads", "landing", "stage", "TB", "LA", "LO", "LG", "LD", "row_of", "token_of", "first_of", "sems",
        "ins", "outs", "tin", "tout",
    )
    v = types.SimpleNamespace(**dict(zip((*names, *results, *scratch), refs, strict=True)))
    start_row = lax.axis_index("fsdp") * rows
    n_chunks = rows // CHUNK

    def fetch(s):
        return pltpu.make_async_copy(v.ge.at[s], v.landing.at[lax.rem(s, 4)], v.sems.at[lax.rem(s, 4)])

    for s in range(3):
        fetch(s).start()
    layers = (("a", v.LA), ("o", v.LO), ("d", v.LD), ("g", v.LG))

    def layer(index, inward):
        kind, buffer = layers[index]
        for which in range(3):
            if inward:
                yield pltpu.make_async_copy(
                    getattr(v, f"{kind}{which}"), buffer.at[which], v.ins.at[index * 3 + which]
                )
            else:
                yield pltpu.make_async_copy(
                    buffer.at[which], getattr(v, f"{kind}{which}_new"), v.outs.at[index * 3 + which]
                )

    def chunk(k, inward):
        at, slot = pl.ds(k * CHUNK, CHUNK), k % SLOTS
        for which in range(3):
            old, new = getattr(v, f"e{which}"), getattr(v, f"e{which}_new")
            if inward:
                yield pltpu.make_async_copy(old.at[at], v.TB.at[slot, which], v.tin.at[slot, which])
            else:
                yield pltpu.make_async_copy(v.TB.at[slot, which], new.at[at], v.tout.at[slot, which])

    for index in range(4):
        for item in layer(index, True):
            item.start()
    for k in range(min(SLOTS, n_chunks)):
        for item in chunk(k, True):
            item.start()

    factor = jnp.minimum(1.0, clip_level / (v.stats[1:2, 0:1] + 1e-06))

    def apply(buffer, at, grad):
        index = tuple(at)
        new = adamw(
            buffer[(0, *index)], grad * factor, buffer[(1, *index)], buffer[(2, *index)], learn_rate
        )
        for which in range(3):
            buffer[(which, *index)] = new[which]

    def finish_layer(index):
        for item in layer(index, False):
            item.start()

    whole = pl.ds(0, nr)
    for item in layer(0, True):
        item.wait()
    for q in range(3):
        apply(v.LA, (whole, pl.ds(q * D, D)), v.fa[q].astype(F32))
    finish_layer(0)
    for item in layer(1, True):
        item.wait()
    apply(v.LO, (whole, pl.ds(0, D)), v.fa[3].astype(F32))
    finish_layer(1)
    for item in layer(2, True):
        item.wait()

    def down(q, carry):
        at = pl.ds(pl.multiple_of(q * nr, 16), nr)
        apply(v.LD, (at, pl.ds(0, D)), v.ff[q, pl.ds(2 * nr, nr), :].astype(F32))
        return carry

    lax.fori_loop(0, TP, down, 0)
    finish_layer(2)
    for item in layer(3, True):
        item.wait()
    quarter, span = D // TP, 2 * D // 6
    at_row = lax.broadcasted_iota(jnp.int32, (span, D), 0)
    at_col = lax.broadcasted_iota(jnp.int32, (span, D), 1)
    group = lax.div(at_col, nr)
    unit = lax.div(group, TP) * nr + (at_col - group * nr)
    holder = lax.rem(group, TP)
    for b in range(TP):
        first = quarter * b // 128 * 128
        total = jnp.zeros((2 * nr, D), F32)
        for q in range(TP):
            pick = (at_row + (first - quarter * b) == unit) & (holder == q)
            total = total + dot(
                v.ff[q, pl.ds(0, 2 * nr), pl.ds(first, span)], jnp.where(pick, 1.0, 0.0).astype(BF)
            )
        apply(v.LG, (whole, pl.ds(b * D, D)), total[:nr])
        apply(v.LG, (whole, pl.ds((TP + b) * D, D)), total[nr:])
    finish_layer(3)
    at_row = lax.broadcasted_iota(jnp.int32, (D, 128), 0)
    at_col = lax.broadcasted_iota(jnp.int32, (D, 128), 1)
    pick = (at_row - lax.axis_index("fsdp") * nr == at_col) & (at_col < nr)
    mine = lax.dot_general(
        v.norms[...], jnp.where(pick, 1.0, 0.0), (((1,), (0,)), ((), ())),
        precision=lax.Precision.HIGHEST, preferred_element_type=F32,
    )
    v.qw[...], v.qm[...], v.qv[...] = adamw(
        v.pw[...], mine[:6, :nr] * factor, v.pm[...], v.pv[...], norm_rate
    )

    def clear(i, carry):
        v.grads[pl.ds(pl.multiple_of(i * CHUNK, 8), CHUNK), :] = jnp.zeros((CHUNK, D), F32)
        return carry

    lax.fori_loop(0, n_chunks, clear, 0)

    def scan(s, count):
        v.first_of[s] = count

        def eight(b, inner):
            for i in range(8):
                j = b * 8 + i
                row = v.ids[s, 0, j] - start_row
                inside = (row >= 0) & (row < rows)
                v.row_of[inner] = row
                v.token_of[inner] = j
                inner = inner + inside.astype(jnp.int32)
            return inner

        return lax.fori_loop(0, lax.shift_right_logical(v.ids[s, 0, S] + 7, 3), eight, count)

    v.first_of[N] = lax.fori_loop(0, N, scan, 0)

    def sequence(s, carry):
        pl.when(s + 3 < N)(lambda: fetch(s + 3).start())
        fetch(s).wait()
        v.stage[...] = v.landing[lax.rem(s, 4)].astype(F32)

        def token(k, inner):
            at = pl.ds(v.row_of[k], 1)
            v.grads[at, :] = v.grads[at, :] + v.stage[pl.ds(v.token_of[k], 1), :]
            return inner

        return lax.fori_loop(v.first_of[s], v.first_of[s + 1], token, carry)

    lax.fori_loop(0, N, sequence, 0)

    for k in range(n_chunks):
        for item in chunk(k, True):
            item.wait()
        slot = k % SLOTS

        def part(first, size, k=k, slot=slot):
            at = pl.ds(pl.multiple_of(k * CHUNK + first, 8), size)
            grad = v.grads[at, :]
            apply(v.TB.at[slot], (pl.ds(pl.multiple_of(first, 8), size), pl.ds(0, D)), grad)

        def tile(i, carry, part=part):
            part(i * 32, 32)
            return carry

        lax.fori_loop(0, CHUNK // 32, tile, 0)
        if CHUNK % 32:
            part(CHUNK // 32 * 32, CHUNK % 32)
        for item in chunk(k, False):
            item.start()
        if k >= 1 and k - 1 + SLOTS < n_chunks:
            for item in chunk(k - 1, False):
                item.wait()
            for item in chunk(k - 1 + SLOTS, True):
                item.start()
    for k in range(n_chunks):
        if k + SLOTS >= n_chunks or k == n_chunks - 1:
            for item in chunk(k, False):
                item.wait()
    for index in range(4):
        for item in layer(index, False):
            item.wait()


def finish(sizes, ids, ge, ff, fa, norms, stats, norm_state, states):
    NR, NF, S, D, rows = sizes
    N, nr = NR * NF, D // NF
    hbm = pl.BlockSpec(memory_space=pl.ANY)
    vmem = pl.BlockSpec(memory_space=pltpu.VMEM)
    smem = pl.BlockSpec(memory_space=pltpu.SMEM)
    flat = [item for state in states for item in state]
    shapes = [jax.ShapeDtypeStruct(item.shape, F32) for item in (*norm_state, *flat)]
    return pl.pallas_call(
        functools.partial(finish_kernel, sizes),
        name="finish",
        out_shape=tuple(shapes),
        in_specs=[smem, hbm] + [vmem] * 7 + [hbm] * 15,
        out_specs=(vmem,) * 3 + (hbm,) * 15,
        scratch_shapes=[
            pltpu.VMEM((rows, D), F32), pltpu.VMEM((4, S, D), BF), pltpu.VMEM((S, D), F32),
            pltpu.VMEM((SLOTS, 3, CHUNK, D), F32),
            pltpu.VMEM((3, nr, 3 * D), F32), pltpu.VMEM((3, nr, D), F32), pltpu.VMEM((3, nr, 8 * D), F32),
            pltpu.VMEM((3, 4 * nr, D), F32),
            pltpu.SMEM((N * S + 8,), jnp.int32), pltpu.SMEM((N * S + 8,), jnp.int32),
            pltpu.SMEM((N + 1,), jnp.int32), pltpu.SemaphoreType.DMA((4,)), pltpu.SemaphoreType.DMA((12,)),
            pltpu.SemaphoreType.DMA((12,)), pltpu.SemaphoreType.DMA((SLOTS, 3)),
            pltpu.SemaphoreType.DMA((SLOTS, 3)),
        ],
        compiler_params=pltpu.CompilerParams(vmem_limit_bytes=62_000_000),
    )(ids, ge, ff, fa, norms, stats, *norm_state, *flat)


def table_kernel(sizes, ids, ge, factor, w, m, v, w_out, m_out, v_out, grads, landing, stage, sems):
    NR, NF, S, D, rows = sizes
    N = NR * NF
    step = pl.program_id(0)
    block = w.shape[0]

    @pl.when(step == 0)
    def _():
        start_row = lax.axis_index("fsdp") * rows

        def fetch(s):
            return pltpu.make_async_copy(ge.at[s], landing.at[lax.rem(s, 4)], sems.at[lax.rem(s, 4)])

        for s in range(3):
            fetch(s).start()

        def clear(i, carry):
            grads[pl.ds(pl.multiple_of(i * block, 8), block), :] = jnp.zeros((block, D), F32)
            return carry

        lax.fori_loop(0, grads.shape[0] // block, clear, 0)

        def sequence(s, carry):
            pl.when(s + 3 < N)(lambda: fetch(s + 3).start())
            fetch(s).wait()
            stage[...] = landing[lax.rem(s, 4)].astype(F32)

            def token(j, inner):
                wanted = ids[s, 0, j] - start_row

                @pl.when((wanted >= 0) & (wanted < rows))
                def _():
                    at = pl.ds(wanted, 1)
                    grads[at, :] = grads[at, :] + stage[pl.ds(j, 1), :]

                return inner

            return lax.fori_loop(0, S, token, carry)

        lax.fori_loop(0, N, sequence, 0)

    grad = grads[pl.ds(pl.multiple_of(step * block, 8), block), :] * factor[0:1, 0:1]
    w_out[...], m_out[...], v_out[...] = adamw(w[...], grad, m[...], v[...], learn_rate)


def update_table(sizes, ids, ge, factor, w, m, v):
    NR, NF, S, D, rows = sizes
    block = 424
    steps = pl.cdiv(rows, block)
    part = pl.BlockSpec((block, D), lambda i: (i, 0))
    return pl.pallas_call(
        functools.partial(table_kernel, sizes),
        name="table",
        grid=(steps,),
        out_shape=(jax.ShapeDtypeStruct((rows, D), F32),) * 3,
        in_specs=[
            pl.BlockSpec(memory_space=pltpu.SMEM), pl.BlockSpec(memory_space=pl.ANY),
            pl.BlockSpec((8, 128), lambda i: (0, 0)), part, part, part,
        ],
        out_specs=(part, part, part),
        scratch_shapes=[
            pltpu.VMEM((steps * block, D), F32), pltpu.VMEM((4, S, D), BF), pltpu.VMEM((S, D), F32),
            pltpu.SemaphoreType.DMA((4,)),
        ],
        compiler_params=pltpu.CompilerParams(vmem_limit_bytes=60_000_000),
    )(ids, ge, factor, w, m, v)


def local(
    sizes,
    token_ids,
    lengths,
    slot_order,
    pair_labels,
    embedding,
    attend_weight,
    attention_output_matrix,
    gate_up,
    contract_kernel,
    norm_params,
    embedding_first,
    embedding_second,
    attend_first,
    attend_second,
    output_first,
    output_second,
    gate_up_first,
    gate_up_second,
    down_first,
    down_second,
    norm_first,
    norm_second,
):
    NR, NF, S, D, rows = sizes
    nr = D // NF
    f = lax.axis_index("fsdp")
    N = NR * NF
    positions = jnp.arange(S)
    angles = (
        positions.astype(F32)[:, None]
        * (1000.0 ** (-2.0 * jnp.arange(HD // 2).astype(F32) / HD))[None, :]
    )
    cosine, sine = jnp.tile(jnp.cos(angles), (1, 128 * 2 // HD)), jnp.tile(jnp.sin(angles), (1, 128 * 2 // HD))
    attention = jnp.concatenate(
        [attend_weight.reshape(nr, 3, D).transpose(1, 0, 2), attention_output_matrix[None]], axis=0
    ).astype(BF)
    hidden = gate_up.astype(BF).reshape(nr, 2, NF, TP, nr).transpose(3, 1, 0, 2, 4).reshape(TP, 2, nr, D)
    down = contract_kernel.astype(BF).reshape(TP, 1, nr, D)
    pieces = jnp.concatenate([attention[:, None], hidden, down], axis=1)
    ids, ffn, att, norms, stats, ge = run_step(
        sizes,
        lengths,
        jnp.concatenate([token_ids, jnp.broadcast_to(lengths[:, None], (1, S))], axis=1),
        norm_params,
        slot_order.reshape(1, N),
        pair_labels.reshape(1, N),
        cosine,
        sine,
        pieces,
        embedding,
    )
    loss_value, grad_norm = stats[0, 0], stats[1, 0]
    if rows % CHUNK == 0:
        norm_next, *rest = split_three(
            finish(
                sizes, ids, ge, ffn, att, norms, stats, (norm_params, norm_first, norm_second),
                (
                    (embedding, embedding_first, embedding_second),
                    (attend_weight, attend_first, attend_second),
                    (attention_output_matrix, output_first, output_second),
                    (gate_up, gate_up_first, gate_up_second),
                    (contract_kernel, down_first, down_second),
                ),
            )
        )
        return (loss_value, grad_norm, *(item for state in rest for item in state), *norm_next)
    factor = jnp.minimum(1.0, clip_level / (grad_norm + 1e-06))
    factor_tile = jnp.broadcast_to(factor, (8, 128))
    emb_next = update_table(sizes, ids, ge, factor_tile, embedding, embedding_first, embedding_second)
    fin = ffn.reshape(TP, 3, nr, D)
    grad_attend = att[:3].transpose(1, 0, 2).reshape(nr, 3 * D).astype(F32)
    grad_output = att[3].astype(F32)
    grad_hidden = (
        fin[:, :2].reshape(TP, 2, nr, NF, nr).transpose(2, 1, 3, 0, 4).reshape(nr, 8 * D).astype(F32)
    )
    grad_down = fin[:, 2].reshape(TP * nr, D).astype(F32)
    grad_norms = lax.dynamic_slice(norms, (0, f * nr), (6, nr))
    att_next = adamw(attend_weight, grad_attend * factor, attend_first, attend_second, learn_rate)
    out_next = adamw(
        attention_output_matrix, grad_output * factor, output_first, output_second, learn_rate
    )
    gate_next = adamw(gate_up, grad_hidden * factor, gate_up_first, gate_up_second, learn_rate)
    down_next = adamw(contract_kernel, grad_down * factor, down_first, down_second, learn_rate)
    norm_next = adamw(norm_params, grad_norms * factor, norm_first, norm_second, norm_rate)
    return (
        loss_value, grad_norm, *emb_next, *att_next, *out_next, *gate_next, *down_next, *norm_next
    )


def split_three(flat):
    return [flat[i : i + 3] for i in range(0, len(flat), 3)]


def solution(mesh):
    NR, NF = mesh.shape["rep"], mesh.shape["fsdp"]
    rows_spec, cols_spec = P("fsdp", None), P(None, "fsdp")

    def step(*args):
        S, D, rows = args[0].shape[1], args[4].shape[1], args[4].shape[0] // NF
        run = jax.shard_map(
            functools.partial(local, (NR, NF, S, D, rows)),
            mesh=mesh,
            in_specs=(P(("rep", "fsdp"), None), P(("rep", "fsdp")), P(), P())
            + (rows_spec,) * 5 + (cols_spec,) + (rows_spec,) * 10 + (cols_spec,) * 2,
            out_specs=(P(), P()) + (rows_spec,) * 15 + (cols_spec,) * 3,
            check_vma=False,
        )
        return run(*args)

    return step
```

```python
import functools
import types

import jax
import jax.numpy as jnp
from jax import lax
from jax.experimental import pallas as pl
from jax.experimental.pallas import tpu as pltpu
from jax.sharding import PartitionSpec as P

H = 12
HD = 64
STEP = 4
TP = 4
MESH = pl.DeviceIdType.MESH
BF = jnp.bfloat16
F32 = jnp.float32

logit_divisor = 0.05
clip_level = 0.001
learn_rate = 0.02
norm_rate = 0.3
weight_decay = 0.01
beta_first = 0.5
beta_second = 0.75
adam_floor = 1e-08


def dot(a, b):
    return lax.dot_general(a, b, (((1,), (0,)), ((), ())), preferred_element_type=F32)


def dot_nt(a, b):
    return lax.dot_general(a, b, (((1,), (1,)), ((), ())), preferred_element_type=F32)


def dot_tn(a, b):
    return lax.dot_general(a, b, (((0,), (0,)), ((), ())), preferred_element_type=F32)


def layer_norm(values, gain, shift):
    centred = values - jnp.mean(values, axis=-1, keepdims=True)
    inverse = lax.rsqrt(jnp.mean(centred * centred, axis=-1, keepdims=True) + 1e-06)
    normed = centred * inverse
    return normed * gain + shift, normed, inverse


def norm_back(upstream, normed, inverse, gain):
    scaled = upstream * gain
    inner = (
        scaled
        - jnp.mean(scaled, axis=-1, keepdims=True)
        - normed * jnp.mean(scaled * normed, axis=-1, keepdims=True)
    )
    return (
        inner * inverse,
        jnp.sum(upstream * normed, axis=0, keepdims=True),
        jnp.sum(upstream, axis=0, keepdims=True),
    )


def step_layout(sizes):
    NR, NF, S, D, rows = sizes
    NZ, NG = NF // 2, NR // TP
    N, nr = NR * NF, D // NF
    block = (S, D)
    buffers = dict(
        pool=((max(0 if rows % 8 else rows, 30 * S), D), F32),
        table=((rows, D) if rows % 8 else (8, 128), F32),
        stage=(block, F32),
        W7=((7, D, D), BF),
        GW=((4, D, D), BF),
        EX=((4, NZ, S, D), BF),
        GNB=((NF, 8, 128), F32),
        H0B=(block, BF), QKV=((3, S, D), BF), ATT=(block, BF), PS=((D // HD, S, S), F32),
        H1=((TP, S, D), BF), MIX=((TP, S, D), BF), DF=((TP, S, D), BF), DG=((2, TP, S, D), BF),
        LX=((TP, S, D), BF), RX=((TP, S, D), BF), DQB=((3, S, D), BF), DB=((3, S, D), BF),
        INV=((3, S, 1), F32), YS=((2, S, D), BF), YR=((2, S, D), BF),
        PB=((N, 1, D), F32), PROW=((1, 1, D), F32), PM=((N, D), F32),
        XR=((4, NZ, nr, D), BF), ZS=((4, NZ, nr, D), BF), ZR=((4, NZ, nr, D), BF),
        NGS=((4, 8, D), F32), NGR=((3, 8, D), F32), NGZ=((NZ, 8, D), F32),
        SQ=((1, 1, 128), F32), SQS=((N, 1, 128), F32),
        PA=((nr, D), F32), PD=((nr, D), F32), PG=((nr, 8 * D), F32), IDF=((N, S), F32), RANK=((2, N, S), F32),
        FG=((NG, 4 * nr, D) if NG > 1 else (1, 16, 128), BF),
    )
    copies = dict(
        ids=1, gn=1, ex=NZ, ez=NZ, wu=3 * NZ, wd=3 * NZ, wx0=NZ, wx1=NZ, wx2=NZ, wx3=NZ, vu=2 * NZ, vd=2 * NZ, ay=NF, ac=2 * NF,
        h1=3, fc=2, fy=1, pool=1, df=3, bc=2, by=1, lx=TP, rx=TP, gx=4 * NZ, gz=4 * NZ, nc=1, ny=1, nx=1,
        nz=NZ, ff=3, fa=3, gg=2 * NG, sq=1, eu=2 * NZ, ed=2 * NZ, e0x=NZ, e0y=NF, e0c=2 * NF, e1x=2 * NZ, e1y=NZ,
        e1c=2 * NF, eg=NG,
    )
    return buffers, copies


def step_kernel(sizes, *refs):
    NR, NF, S, D, rows = sizes
    NX, NZ, NG = 2, NF // 2, NR // TP
    N, nr = NR * NF, D // NF
    HI = lax.Precision.HIGHEST
    buffers, copies = step_layout(sizes)
    given = (
        "length_in", "ids_in", "gn_in", "order_in", "labels_in", "cos_in", "sin_in", "qkv_in", "o_in", "gu_in", "down_in",
        "w_in", "ids_out", "ff_out", "fa_out", "ng_out", "stats_out", "list_out", "ge_out",
    )
    v = types.SimpleNamespace(**dict(zip((*given, *buffers, "sids", "ssem", "rsem", "lsem"), refs, strict=True)))
    pool, W7, GW, DB, DQB, QKV = v.pool, v.W7, v.GW, v.DB, v.DQB, v.QKV
    ssem, rsem, lsem, ids_out, ge_out = v.ssem, v.rsem, v.lsem, v.ids_out, v.ge_out
    r = lax.axis_index("rep")
    f = lax.axis_index("fsdp")
    d = r * NF + f
    z, x = lax.div(f, NX), lax.rem(f, NX)
    g, t = lax.div(r, TP), lax.rem(r, TP)
    y, c = lax.div(t, 2), lax.rem(t, 2)
    ty = (1 - y) * 2 + c
    tc = y * 2 + 1 - c
    tyc = (1 - y) * 2 + 1 - c
    dev_x = (r, z * NX + 1 - x)
    dev_y = (g * TP + ty, f)
    dev_c = (g * TP + tc, f)

    GATE, UP, PT, PT2 = 0, 4 * S, 8 * S, 12 * S
    CR, CR2 = 16 * S, 18 * S
    H0F, H1F, HAT, DS2, DS1, DQ = 20 * S, 21 * S, 22 * S, 25 * S, 26 * S, 27 * S

    def blk(offset, index=0):
        return pl.ds(pl.multiple_of(offset + index * S, 128), S)

    sem_at, used = {}, 0
    for name, many in copies.items():
        sem_at[name] = used
        used += many
    later = []

    def copy(name, index, src, dst, dev, landing=None):
        base = sem_at[name]
        return pltpu.make_async_remote_copy(
            src_ref=src, dst_ref=dst, send_sem=ssem.at[base + index],
            recv_sem=rsem.at[base + (index if landing is None else landing)],
            device_id=dev, device_id_type=MESH,
        )

    def send(name, index, src, dst, dev, only=None, landing=None):
        def start():
            copy(name, index, src, dst, dev, landing).start()

        def finish():
            copy(name, index, src, dst, dev, landing).wait_send()

        if only is None:
            start()
            later.append(finish)
        else:
            pl.when(only)(start)
            later.append(lambda: pl.when(only)(finish))

    def arrive(name, index, dst, only=None):
        def wait():
            pltpu.make_async_copy(dst, dst, rsem.at[sem_at[name] + index]).wait()

        if only is None:
            wait()
        else:
            pl.when(only)(wait)

    def spread(name, src, dst):
        base = sem_at[name]

        def one(k, carry):
            to = lax.rem(d + k, N)
            pltpu.make_async_remote_copy(
                src_ref=src, dst_ref=dst.at[d], send_sem=ssem.at[base], recv_sem=rsem.at[base],
                device_id=(lax.div(to, NF), lax.rem(to, NF)), device_id_type=MESH,
            ).start()
            return carry

        lax.fori_loop(1, N, one, 0)
        rest = dst.at[pl.ds(0, N - 1)]
        later.append(lambda: pltpu.make_async_copy(rest, rest, ssem.at[base]).wait())

    def gather_all(name, dst):
        rest = dst.at[pl.ds(0, N - 1)]
        pltpu.make_async_copy(rest, rest, rsem.at[sem_at[name]]).wait()

    def keep(only, ref, at, value):
        @pl.when(only)
        def _():
            ref[at] = value

    def load(src, dst, sem):
        done = pltpu.make_async_copy(src, dst, lsem.at[sem])
        done.start()
        return done

    table = v.table if rows % 8 else pool.at[pl.ds(0, rows)]
    slots = [t, 4, 5, 6]

    def wrow(index):
        return pl.ds(pl.multiple_of(index * nr, 16), nr)

    got_gate = load(v.gu_in, v.PG, 1)
    got_down = load(v.down_in.at[wrow(t)], v.PD, 2)

    @pl.when(t < 3)
    def _():
        load(v.qkv_in.at[:, pl.ds(pl.multiple_of(jnp.minimum(t, 2) * D, 128), D)], v.PA, 3)

    @pl.when(t == 3)
    def _():
        load(v.o_in, v.PA, 3)

    length = v.length_in[0]
    ids_out[d, :, pl.ds(0, S)] = v.ids_in[...]
    ids_out[d, :, pl.ds(S, S)] = jnp.zeros((1, S), jnp.int32) + length
    v.GNB[f] = jnp.zeros((8, 128), F32)
    v.GNB[f, 0:6, 0:nr] = v.gn_in[...].astype(BF).astype(F32)
    barrier = pltpu.get_barrier_semaphore()

    def greet(k, carry):
        to = lax.rem(d + k, N)
        pl.semaphore_signal(
            barrier, inc=1, device_id=(lax.div(to, NF), lax.rem(to, NF)), device_id_type=MESH
        )
        return carry

    lax.fori_loop(1, N, greet, 0)
    pltpu.make_async_copy(v.o_in, v.PA, lsem.at[3]).wait()
    W7[t, wrow(f), :] = v.PA[...].astype(BF)
    got_down.wait()
    W7[6, wrow(f), :] = v.PD[...].astype(BF)
    got_gate.wait()
    got_table = load(v.w_in, table, 0)
    quarter, span = D // TP, D // 3
    unit_row = lax.broadcasted_iota(jnp.int32, (D, span), 0)
    unit_col = lax.broadcasted_iota(jnp.int32, (D, span), 1)
    unit_group = lax.div(unit_row, nr)
    unit_at = lax.div(unit_group, TP) * nr + (unit_row - unit_group * nr)
    unit_mine = lax.rem(unit_group, TP) == t
    tiles = [jnp.zeros((2 * nr, 128), F32) for _ in range(D // 128)]
    for b in range(TP):
        first = quarter * b // 128 * 128
        choose = unit_mine & (unit_at + (quarter * b - first) == unit_col)
        both = jnp.concatenate(
            [v.PG[:, pl.ds(b * D, D)], v.PG[:, pl.ds((TP + b) * D, D)]], axis=0
        ).astype(BF)
        found = dot(both, jnp.where(choose, 1.0, 0.0).astype(BF))
        for i in range(span // 128):
            tiles[first // 128 + i] = tiles[first // 128 + i] + found[:, i * 128 : (i + 1) * 128]
    hidden = jnp.concatenate(tiles, axis=1).astype(BF)
    W7[4, wrow(f), :] = hidden[:nr]
    W7[5, wrow(f), :] = hidden[nr:]
    pl.semaphore_wait(barrier, N - 1)

    spread("ids", ids_out.at[d], ids_out)

    def piece(m, origin_z, origin_x):
        return W7.at[slots[m], wrow(origin_z * NX + origin_x)]

    def up_to(m, origin, only, which):
        here = piece(m, origin, which)
        if m < 3:
            send("wu", m * NZ + origin, here, here, (r, f + NX), only)
        else:
            send("vu", which * NZ + origin, here, here, (r, f + NX), only)

    def down_to(m, origin, only, which):
        here = piece(m, origin, which)
        if m < 3:
            send("wd", m * NZ + origin, here, here, (r, f - NX), only)
        else:
            send("vd", which * NZ + origin, here, here, (r, f - NX), only)

    def across(m, origin, only=None):
        here = piece(m, origin, x)
        send(f"wx{m}", origin, here, here, dev_x, only)

    def publish(index, only=None):
        here = W7.at[t, wrow(index)]
        send("ay", index, here, here, dev_y, only)
        send("ac", index, here, here, dev_c, only)

    def own_pieces(m):
        up_to(m, z, z + 1 < NZ, x)
        down_to(m, z, z >= 1, x)
        across(m, z)

    def relay(m, k):
        low, high = z - k, z + k
        below, above = jnp.maximum(low, 0), jnp.minimum(high, NZ - 1)
        for which in (x,) if m < 3 else (x, 1 - x):
            first = m * NZ if m < 3 else which * NZ
            arrive("wu" if m < 3 else "vu", first + below, piece(m, below, which), low >= 0)
            up_to(m, below, (low >= 0) & (z + 1 < NZ), which)
            if m < 3:
                across(m, below, low >= 0)
            if m == 0:
                publish(below * NX + x, low >= 0)
            arrive("wd" if m < 3 else "vd", first + above, piece(m, above, which), high < NZ)
            down_to(m, above, (high < NZ) & (z >= 1), which)
            if m < 3:
                across(m, above, high < NZ)
            if m == 0:
                publish(above * NX + x, high < NZ)

    own_pieces(0)
    publish(f)
    base_gn = sem_at["gn"]

    def gn_one(k, carry):
        pltpu.make_async_remote_copy(
            src_ref=v.GNB.at[f], dst_ref=v.GNB.at[f], send_sem=ssem.at[base_gn], recv_sem=rsem.at[base_gn],
            device_id=(r, lax.rem(f + k, NF)), device_id_type=MESH,
        ).start()
        return carry

    lax.fori_loop(1, NF, gn_one, 0)
    gn_rest = v.GNB.at[pl.ds(0, NF - 1)]
    later.append(lambda: pltpu.make_async_copy(gn_rest, gn_rest, ssem.at[base_gn]).wait())
    for m in (1, 2, 3):
        own_pieces(m)

    gather_all("ids", ids_out)
    got_sids = load(ids_out.at[pl.ds(pl.multiple_of(r * NF, NF), NF)], v.sids, 5)
    got_sids.wait()
    got_table.wait()
    start_row = f * rows
    EXS, EXO, EXR, EZR = (v.EX.at[i] for i in range(4))

    def rows_of(i, other):
        owner = i * NX + other

        def token(j, inner):
            wanted = v.sids[owner, 0, j] - start_row
            inside = (wanted >= 0) & (wanted < rows)
            row = table[pl.ds(jnp.clip(wanted, 0, rows - 1), 1), :]
            v.stage[pl.ds(j, 1), :] = jnp.where(inside, row, 0.0)
            return inner

        lax.fori_loop(0, S, token, 0, unroll=8)
        return v.stage[...].astype(BF)

    steps = [(m, k) for k in range(1, NZ) for m in (0, 1, 2, 3)]
    jobs = [(i, True) for i in range(NZ)] + [(i, False) for i in range(NZ)]
    at_step = 0
    for number, (i, away) in enumerate(jobs):
        if away:
            EXS[i] = rows_of(i, 1 - x)
            send("ex", i, EXS.at[i], EXR.at[i], dev_x)
        else:
            EXO[i] = rows_of(i, x)
        if number == 1:
            arrive("wx3", z, piece(3, z, 1 - x))
            up_to(3, z, z + 1 < NZ, 1 - x)
            down_to(3, z, z >= 1, 1 - x)
        while at_step < len(steps) * (number + 1) // (len(jobs) + 2) - 1:
            relay(*steps[at_step])
            at_step += 1

    for i in range(NZ):
        arrive("ex", i, EXR.at[i])
        total = EXO[i] + EXR[i]
        EXO[i] = total
        keep(z == i, EZR, i, total)
        send("ez", i, EXO.at[i], EZR.at[z], (r, i * NX + x), z != i, z)
    while at_step < len(steps):
        relay(*steps[at_step])
        at_step += 1

    for i in range(NZ):
        arrive("wx0", i, piece(0, i, 1 - x))
        publish(i * NX + 1 - x)
    for i in range(NF):
        there = W7.at[ty, wrow(i)]
        arrive("ay", i, there)
        send("ac", NF + i, there, there, dev_c)

    arrive("gn", 0, gn_rest)
    tiles = jnp.concatenate([v.GNB[i] for i in range(NF)], axis=1).astype(BF)
    at_row = lax.broadcasted_iota(jnp.int32, (NF * 128, D), 0)
    at_col = lax.broadcasted_iota(jnp.int32, (NF * 128, D), 1)
    lane = lax.bitwise_and(at_row, 127)
    pick = (lane < nr) & (lax.shift_right_logical(at_row, 7) * nr + lane == at_col)
    gains = dot(tiles, jnp.where(pick, 1.0, 0.0).astype(BF))
    gain = [gains[i : i + 1] for i in range(6)]

    for i in range(NZ):
        pl.when(z != i)(functools.partial(arrive, "ez", i, EZR.at[i]))
    embedded = EZR[0].astype(F32)
    for i in range(1, NZ):
        embedded = embedded + EZR[i].astype(F32)
    normed, hat, inverse = layer_norm(embedded, gain[0], gain[1])
    pool[blk(H0F), :] = normed
    pool[blk(HAT, 0), :] = hat
    v.INV[0] = inverse
    v.H0B[...] = normed.astype(BF)

    def to_rank(name, which, src, buffer):
        send(name, which, src, buffer.at[t], (g * TP + which, f), t != which, t)
        keep(t == which, buffer, which, src[...])

    for which in range(3):
        to_rank("lx", which, v.H0B, v.LX)

    for i in range(NF):
        arrive("ac", i, W7.at[tc, wrow(i)])
    for i in range(NF):
        arrive("ac", NF + i, W7.at[tyc, wrow(i)])
    tables = [jnp.concatenate([ref[...]] * (D // 128), axis=1) for ref in (v.cos_in, v.sin_in)]
    in_half = lax.bitwise_and(lax.broadcasted_iota(jnp.int32, (S, D), 1), HD - 1) < HD // 2

    def turn(values, sign):
        partner = jnp.where(
            in_half, pltpu.roll(values, D - HD // 2, 1), pltpu.roll(values, HD // 2, 1)
        )
        signed = jnp.where(in_half, -sign, sign) * tables[1]
        return values * tables[0] + partner * signed

    for j in range(3):
        projected = dot(v.H0B[...], W7[j])
        QKV[j] = (turn(projected, 1.0) if j < 2 else projected).astype(BF)
    allowed = lax.broadcasted_iota(jnp.int32, (1, S), 1) < length
    scaling = HD ** (-0.5)
    first_half = lax.broadcasted_iota(jnp.int32, (S, 128), 1) < HD

    def half(values, which):
        keep = first_half if which == 0 else jnp.logical_not(first_half)
        return jnp.where(keep, values, jnp.zeros_like(values))

    def attend(p, carry):
        lanes = pl.ds(pl.multiple_of(p * 128, 128), 128)
        query, keys, values = QKV[0, :, lanes], QKV[1, :, lanes], QKV[2, :, lanes]
        result = jnp.zeros((S, 128), F32)
        for which in range(2):
            scores = dot_nt(query, half(keys, which)) * scaling
            scores = jnp.where(allowed, scores, -1000000000.0)
            raised = jnp.exp(scores - jnp.max(scores, axis=-1, keepdims=True))
            chances = raised / jnp.sum(raised, axis=-1, keepdims=True)
            v.PS[2 * p + which] = chances
            result = result + dot(chances.astype(BF), half(values, which))
        v.ATT[:, lanes] = result.astype(BF)
        return carry

    lax.fori_loop(0, D // 128, attend, 0)
    branch = dot(v.ATT[...], W7[3])
    normed, hat, inverse = layer_norm(pool[blk(H0F), :] + branch, gain[2], gain[3])
    pool[blk(H1F), :] = normed
    pool[blk(HAT, 1), :] = hat
    v.INV[1] = inverse
    v.H1[t] = normed.astype(BF)

    def share(name, buffer):
        send(name, 0, buffer.at[t], buffer.at[t], dev_y)
        send(name, 1, buffer.at[t], buffer.at[t], dev_c)
        arrive(name, 0, buffer.at[ty])
        send(name, 2, buffer.at[ty], buffer.at[ty], dev_c)
        arrive(name, 1, buffer.at[tc])
        arrive(name, 2, buffer.at[tyc])

    def reduce(names, offset, landing, which):
        for i in range(2):
            send(names[0], i, pool.at[blk(offset, i * 2 + 1 - c)], pool.at[blk(landing, i)], dev_c)
        for i in range(2):
            arrive(names[0], i, pool.at[blk(landing, i)])
        away = pool[blk(offset, (1 - y) * 2 + c), :] + pool[blk(landing, 1 - y), :]
        v.YS[which] = away.astype(BF)
        send(names[1], 0, v.YS.at[which], v.YR.at[which], dev_y)
        mine = pool[blk(offset, t), :] + pool[blk(landing, y), :]
        arrive(names[1], 0, v.YR.at[which])
        return mine + v.YR[which].astype(F32)

    share("h1", v.H1)
    to_rank("lx", 3, v.ATT, v.LX)
    for m in range(1, 3):
        for i in range(NZ):
            arrive(f"wx{m}", i, piece(m, i, 1 - x))

    def forward(b, carry):
        gate, up = dot(v.H1[b], W7[4]), dot(v.H1[b], W7[5])
        pool[blk(GATE, b), :] = gate
        pool[blk(UP, b), :] = up
        mixed = (gate / (1.0 + jnp.exp(-gate)) * up).astype(BF)
        v.MIX[b] = mixed
        pool[blk(PT, b), :] = dot(mixed, W7[6])
        return carry

    lax.fori_loop(0, TP, forward, 0)
    feed = reduce(("fc", "fy"), PT, CR, 0)
    normed, hat, inverse = layer_norm(pool[blk(H1F), :] + feed, gain[4], gain[5])
    pool[blk(HAT, 2), :] = hat
    v.INV[2] = inverse
    present = jnp.where(lax.broadcasted_iota(jnp.int32, (S, 1), 0) < length, 1.0, 0.0)
    share_of = length.astype(F32)
    v.PROW[0] = jnp.sum(normed * present, axis=0, keepdims=True) / share_of

    spread("pool", v.PROW.at[0], v.PB)
    v.PB[d] = v.PROW[0]
    gather_all("pool", v.PB)
    for i in range(N):
        v.PM[pl.ds(i, 1), :] = v.PB[i]
    pooled = v.PM[...]
    wide = lax.broadcasted_iota(jnp.int32, (N, D), 1)
    row_at = lax.broadcasted_iota(jnp.int32, (N, N), 0)
    col_at = lax.broadcasted_iota(jnp.int32, (N, N), 1)
    order, labels = v.order_in[...].astype(F32), v.labels_in[...].astype(F32)

    def column(row):
        return jnp.sum(jnp.where(row_at == col_at, row, 0.0), axis=1, keepdims=True)

    slot_has = jnp.where(column(order) == col_at.astype(F32), 1.0, 0.0).astype(BF)
    label_is = jnp.where(column(labels) == order, 1.0, 0.0).astype(BF)
    paired = dot(slot_has, label_is)
    loss_value = jnp.zeros((1, 1), F32)
    d_pooled = jnp.zeros((N, D), F32)
    for width in (D // 12, D // 3, D):
        portion = jnp.where(wide < width, pooled, 0.0)
        inverse = lax.rsqrt(jnp.sum(portion * portion, axis=1, keepdims=True) + 1e-06)
        unit = portion * inverse
        similar = lax.dot_general(
            unit, unit, (((1,), (1,)), ((), ())), precision=HI, preferred_element_type=F32
        ) / logit_divisor
        similar = jnp.where(row_at == col_at, -1000000000.0, similar)
        row_max = jnp.max(similar, axis=1, keepdims=True)
        raised = jnp.exp(similar - row_max)
        total = jnp.sum(raised, axis=1, keepdims=True)
        target = jnp.sum(jnp.where(paired > 0.0, similar, 0.0), axis=1, keepdims=True)
        term = row_max + jnp.log(total) - target
        loss_value = loss_value + jnp.sum(term, axis=0, keepdims=True) / N
        col_max = jnp.max(similar, axis=0, keepdims=True)
        raised_t = jnp.exp(similar - col_max)
        turned = raised_t / jnp.sum(raised_t, axis=0, keepdims=True)
        d_similar = (raised / total + turned - 2.0 * paired) / (3.0 * N) / logit_divisor
        d_unit = lax.dot_general(
            d_similar, unit, (((1,), (0,)), ((), ())), precision=HI, preferred_element_type=F32
        )
        inner = jnp.sum(d_unit * unit, axis=1, keepdims=True)
        d_pooled = d_pooled + inverse * (d_unit - unit * inner)
    loss_value = loss_value / 3.0
    own_row = lax.broadcasted_iota(jnp.int32, (N, D), 0) == d
    d_mine = jnp.sum(jnp.where(own_row, d_pooled, 0.0), axis=0, keepdims=True)

    d_two = d_mine * present / share_of
    d_sum, d_gain_two, d_shift_two = norm_back(d_two, pool[blk(HAT, 2), :], v.INV[2], gain[4])
    pool[blk(DS2), :] = d_sum
    v.DF[t] = d_sum.astype(BF)
    share("df", v.DF)

    def back(b, carry):
        d_mixed = dot_nt(v.DF[b], W7[6])
        gate, up = pool[blk(GATE, b), :], pool[blk(UP, b), :]
        logistic = 1.0 / (1.0 + jnp.exp(-gate))
        d_gate = (d_mixed * up * (logistic * (1.0 + gate * (1.0 - logistic)))).astype(BF)
        d_up = (d_mixed * (gate * logistic)).astype(BF)
        v.DG[0, b] = d_gate
        v.DG[1, b] = d_up
        pool[blk(PT2, b), :] = dot_nt(d_gate, W7[4]) + dot_nt(d_up, W7[5])
        return carry

    TILE = 256

    def product(left, right, m):
        def tile(i, carry):
            at = pl.ds(pl.multiple_of(i * TILE, TILE), TILE)
            GW[m, at, :] = dot_tn(left(at), right()).astype(BF)
            return carry

        lax.fori_loop(0, D // TILE, tile, 0)

    def part(m, i, other):
        return GW.at[m, wrow(i * NX + other)]

    def give(m):
        for i in range(NZ):
            send("gx", m * NZ + i, part(m, i, 1 - x), v.XR.at[m, i], dev_x)

    def pass_on(m):
        for i in range(NZ):
            arrive("gx", m * NZ + i, v.XR.at[m, i])
            total = (part(m, i, x)[...].astype(F32) + v.XR[m, i].astype(F32)).astype(BF)
            v.ZS[m, i] = total
            keep(z == i, v.ZR, (m, i), total)
            send("gz", m * NZ + i, v.ZS.at[m, i], v.ZR.at[m, z], (r, i * NX + x), z != i, m * NZ + z)

    def product_rows(buffer):
        return lambda at: buffer[:, :, at].reshape(TP * S, TILE)

    product(product_rows(v.MIX), lambda: v.DF[...].reshape(TP * S, D), 3)
    give(3)
    lax.fori_loop(0, TP, back, 0)
    for i in range(2):
        send("bc", i, pool.at[blk(PT2, i * 2 + 1 - c)], pool.at[blk(CR2, i)], dev_c)
    product(product_rows(v.H1), lambda: v.DG[0].reshape(TP * S, D), 1)
    give(1)
    for i in range(2):
        arrive("bc", i, pool.at[blk(CR2, i)])
    away = pool[blk(PT2, (1 - y) * 2 + c), :] + pool[blk(CR2, 1 - y), :]
    v.YS[1] = away.astype(BF)
    send("by", 0, v.YS.at[1], v.YR.at[1], dev_y)
    product(product_rows(v.H1), lambda: v.DG[1].reshape(TP * S, D), 2)
    give(2)
    pass_on(3)
    mine = pool[blk(PT2, t), :] + pool[blk(CR2, y), :]
    arrive("by", 0, v.YR.at[1])
    d_one = pool[blk(DS2), :] + (mine + v.YR[1].astype(F32))

    d_sum, d_gain_one, d_shift_one = norm_back(d_one, pool[blk(HAT, 1), :], v.INV[1], gain[2])
    pool[blk(DS1), :] = d_sum
    DB[0] = d_sum.astype(BF)
    to_rank("rx", 3, DB.at[0], v.RX)
    DB[1] = dot_nt(DB[0], W7[3]).astype(BF)
    pass_on(1)

    def attend_back(p, carry):
        lanes = pl.ds(pl.multiple_of(p * 128, 128), 128)
        query, keys, values = QKV[0, :, lanes], QKV[1, :, lanes], QKV[2, :, lanes]
        grad = DB[1, :, lanes]
        d_query = jnp.zeros((S, 128), F32)
        d_keys = jnp.zeros((S, 128), F32)
        d_values = jnp.zeros((S, 128), F32)
        for which in range(2):
            chances = v.PS[2 * p + which]
            d_values = d_values + dot_tn(chances.astype(BF), half(grad, which))
            d_chances = dot_nt(grad, half(values, which))
            inner = jnp.sum(chances * d_chances, axis=-1, keepdims=True)
            d_scores = (chances * (d_chances - inner)).astype(BF)
            d_query = d_query + dot(d_scores, half(keys, which)) * scaling
            d_keys = d_keys + dot_tn(d_scores, half(query, which)) * scaling
        pool[blk(DQ, 0), lanes] = d_query
        pool[blk(DQ, 1), lanes] = d_keys
        DQB[2, :, lanes] = d_values.astype(BF)
        return carry

    lax.fori_loop(0, D // 128, attend_back, 0)
    for j in range(2):
        DQB[j] = turn(pool[blk(DQ, j), :], -1.0).astype(BF)

    for which in range(3):
        to_rank("rx", which, DQB.at[which], v.RX)
    d_zero = pool[blk(DS1), :]
    for j in range(3):
        d_zero = d_zero + dot_nt(DQB[j], W7[j])
    d_embedded, d_gain_zero, d_shift_zero = norm_back(d_zero, pool[blk(HAT, 0), :], v.INV[0], gain[0])
    DB[2] = d_embedded.astype(BF)

    got_own = load(DB.at[2], ge_out.at[d], 0)
    cut = D * 2 // 3
    cols = [pl.ds(0, cut), pl.ds(cut, D - cut)]

    def line(rep, which_x, order, i):
        return ge_out.at[rep * NF + i * NX + which_x, :, cols[order]]

    def all_of(rep, order):
        return ge_out.at[pl.ds(pl.multiple_of(rep * NF, NF), NF), :, cols[order]]

    def ge_up(order, origin, src, only):
        send("eu", order * NZ + origin, src, line(r, x, order, origin), (r, f + NX), only)

    def ge_down(order, origin, src, only):
        send("ed", order * NZ + origin, src, line(r, x, order, origin), (r, f - NX), only)

    ry, rc, ryc = g * TP + ty, g * TP + tc, g * TP + tyc

    def ge_line(order, i, only=None, src=None):
        here = line(r, x, order, i)
        src = here if src is None else src
        if order == 0:
            send("e0x", i, src, here, dev_x, only)
            send("e0y", i * NX + x, src, here, dev_y, only)
            send("e0c", i * NX + x, src, here, dev_c, only)
        else:
            send("e1y", i, src, here, dev_y, only)
            send("e1x", i, src, here, dev_x, only)
            send("e1c", i * NX + x, src, here, dev_c, only)

    def ge_second(i, only):
        here = line(r, 1 - x, 0, i)
        arrive("e0x", i, here, only)
        send("e0y", i * NX + 1 - x, here, here, dev_y, only)
        send("e0c", i * NX + 1 - x, here, here, dev_c, only)
        here = line(ry, x, 1, i)
        arrive("e1y", i, here, only)
        send("e1x", NZ + i, here, here, dev_x, only)
        send("e1c", NF + i * NX + x, here, here, dev_c, only)

    def ge_third(i, only):
        for which_x in (x, 1 - x):
            here = line(ry, which_x, 0, i)
            arrive("e0y", i * NX + which_x, here, only)
            send("e0c", NF + i * NX + which_x, here, here, dev_c, only)
        for which, rep in enumerate((r, ry)):
            here = line(rep, 1 - x, 1, i)
            arrive("e1x", which * NZ + i, here, only)
            send("e1c", which * NF + i * NX + 1 - x, here, here, dev_c, only)

    def at_distance(step, k):
        low, high = z - k, z + k
        step(jnp.maximum(low, 0), low >= 0)
        if k:
            step(jnp.minimum(high, NZ - 1), high < NZ)

    for order in range(2):
        own_cols = DB.at[2, :, cols[order]]
        ge_up(order, z, own_cols, z + 1 < NZ)
        ge_down(order, z, own_cols, z >= 1)
        ge_line(order, z, None, own_cols)

    def ge_relay(k):
        low, high = z - k, z + k
        below, above = jnp.maximum(low, 0), jnp.minimum(high, NZ - 1)
        for order in range(2):
            arrive("eu", order * NZ + below, line(r, x, order, below), low >= 0)
            ge_up(order, below, line(r, x, order, below), (low >= 0) & (z + 1 < NZ))
            ge_line(order, below, low >= 0)
            arrive("ed", order * NZ + above, line(r, x, order, above), high < NZ)
            ge_down(order, above, line(r, x, order, above), (high < NZ) & (z >= 1))
            ge_line(order, above, high < NZ)

    def own_lists():
        for i in range(N):
            v.IDF[pl.ds(i, 1), :] = ids_out[i, :, pl.ds(0, S)].astype(F32)
            v.PM[pl.ds(i, 1), pl.ds(0, S)] = ids_out[i, :, pl.ds(S, S)].astype(F32)
        local_row = v.IDF[...] - (f * rows).astype(F32)
        valid = lax.broadcasted_iota(jnp.int32, (N, S), 1).astype(F32) < v.PM[:, 0:S]
        mine = valid & (local_row >= 0.0) & (local_row < 1.0 * rows)
        marks = jnp.where(mine, 1.0, 0.0).astype(BF)
        before = lax.broadcasted_iota(jnp.int32, (S, S), 0) < lax.broadcasted_iota(jnp.int32, (S, S), 1)
        prefix = dot(marks, jnp.where(before, 1.0, 0.0).astype(BF))
        counts = jnp.zeros((N, S), F32) + jnp.sum(marks.astype(F32), axis=1, keepdims=True)
        offsets = dot(jnp.where(row_at > col_at, 1.0, 0.0).astype(BF), counts.astype(BF))
        place = prefix + offsets
        high = jnp.floor(place * (1.0 / S))
        v.RANK[0] = high
        v.RANK[1] = jnp.where(mine, place - high * S, -1.0)
        v.IDF[...] = jnp.where(mine, local_row, 0.0)
        slot_at = lax.broadcasted_iota(jnp.int32, (N, S), 0).astype(F32)
        low_at = lax.broadcasted_iota(jnp.int32, (S, S), 0).astype(F32)
        token_at = lax.broadcasted_iota(jnp.int32, (1, S), 1).astype(F32)

        def one(i, carry):
            at = pl.ds(i, 1)
            row = v.IDF[at, :]
            row_high = jnp.floor(row * (1.0 / 64))
            spot = v.RANK[0, at, :] == slot_at
            left = jnp.concatenate(
                [jnp.where(spot, item, 0.0) for item in (row_high, row - row_high * 64.0, token_at)], axis=0
            ).astype(BF)
            right = jnp.where(v.RANK[1, at, :] == low_at, 1.0, 0.0).astype(BF)
            return carry + dot_nt(left, right)

        found = lax.fori_loop(0, N, one, jnp.zeros((3 * N, S), F32))
        v.list_out[0] = (found[:N] * 64.0 + found[N : 2 * N]).astype(jnp.int32)
        v.list_out[1] = found[2 * N :].astype(jnp.int32)
        v.list_out[2] = offsets.astype(jnp.int32)
        v.list_out[3] = (offsets + counts).astype(jnp.int32)

    v.NGS[0] = jnp.concatenate(
        [d_gain_zero, d_shift_zero, d_gain_one, d_shift_one, d_gain_two, d_shift_two,
         jnp.zeros((2, D), F32)], axis=0)
    stages = (("nc", dev_c), ("ny", dev_y), ("nx", dev_x))

    def norm_send(i):
        send(stages[i][0], 0, v.NGS.at[i], v.NGR.at[i], stages[i][1])

    def norm_add(i):
        arrive(stages[i][0], 0, v.NGR.at[i])
        v.NGS[i + 1] = v.NGS[i] + v.NGR[i]

    def settle(m, out, at):
        for i in range(NZ):
            arrive("gz", m * NZ + i, v.ZR.at[m, i], z != i)
        total = v.ZR[m, 0].astype(F32)
        for i in range(1, NZ):
            total = total + v.ZR[m, i].astype(F32)
        out[t, at, :] = total.astype(BF)

    def group_sum(out, first, size):
        own = v.FG.at[g, pl.ds(first, size)]
        own[...] = out[t]
        for k in range(1, NG):
            other = lax.rem(g + k, NG)
            index = (0 if first else NG) + k
            send("gg", index, own, own, (other * TP + t, f), None, (0 if first else NG) + g)
        for k in range(1, NG):
            other = lax.rem(g + k, NG)
            arrive("gg", (0 if first else NG) + other, v.FG.at[other, pl.ds(first, size)])
        total = v.FG[0, pl.ds(first, size)].astype(F32)
        for k in range(1, NG):
            total = total + v.FG[k, pl.ds(first, size)].astype(F32)
        out[t] = total.astype(BF)

    def share_start(name, buffer):
        send(name, 0, buffer.at[t], buffer.at[t], dev_y)
        send(name, 1, buffer.at[t], buffer.at[t], dev_c)

    def share_pass(name, buffer):
        arrive(name, 0, buffer.at[ty])
        send(name, 2, buffer.at[ty], buffer.at[ty], dev_c)

    def share_end(name, buffer):
        arrive(name, 1, buffer.at[tc])
        arrive(name, 2, buffer.at[tyc])

    norm_send(0)
    pass_on(2)
    for which in range(TP):
        arrive("lx", which, v.LX.at[which], t != which)
        arrive("rx", which, v.RX.at[which], t != which)
    product(product_rows(v.LX), lambda: v.RX[...].reshape(TP * S, D), 0)
    give(0)
    norm_add(0)
    norm_send(1)
    got_own.wait()
    ge_relay(1)
    at_distance(ge_second, 0)
    settle(3, v.ff_out, pl.ds(2 * nr, nr))
    settle(1, v.ff_out, pl.ds(0, nr))
    norm_add(1)
    norm_send(2)
    pass_on(0)
    for k in range(2, NZ):
        ge_relay(k)
        at_distance(ge_second, k - 1)
    settle(2, v.ff_out, pl.ds(nr, nr))
    if NG > 1:
        group_sum(v.ff_out, nr, 3 * nr)
    share_start("ff", v.ff_out)
    at_distance(ge_second, NZ - 1)
    norm_add(2)
    for i in range(NZ):
        send("nz", i, v.NGS.at[3], v.NGZ.at[z], (r, i * NX + x), z != i, z)
        keep(z == i, v.NGZ, i, v.NGS[3])
    own = v.ff_out[t].astype(F32)
    squares = jnp.sum(own * own)
    settle(0, v.fa_out, pl.ds(0, nr))
    if NG > 1:
        group_sum(v.fa_out, 0, nr)
    share_start("fa", v.fa_out)
    own = v.fa_out[t].astype(F32)
    squares = squares + jnp.sum(own * own)
    squares = jnp.where(g == 0, squares, 0.0)
    own_lists()
    for k in range(NZ):
        at_distance(ge_third, k)
    for name, buffer in (("ff", v.ff_out), ("fa", v.fa_out)):
        share_pass(name, buffer)
    for i in range(NZ):
        arrive("nz", i, v.NGZ.at[i], z != i)
    total_norms = v.NGZ[0]
    for i in range(1, NZ):
        total_norms = total_norms + v.NGZ[i]
    for name, buffer in (("ff", v.ff_out), ("fa", v.fa_out)):
        share_end(name, buffer)
    for order, name in enumerate(("e0c", "e1c")):
        for which, rep in enumerate((rc, ryc)):
            for i in range(NF):
                arrive(name, which * NF + i, ge_out.at[rep * NF + i, :, cols[order]])
    if NG > 1:

        def group(which):
            return ge_out.at[pl.ds(pl.multiple_of(which * TP * NF, TP * NF), TP * NF)]

        for k in range(1, NG):
            other = lax.rem(g + k, NG)
            send("eg", k, group(g), group(g), (other * TP + t, f), None, g)
        for k in range(1, NG):
            other = lax.rem(g + k, NG)
            arrive("eg", other, group(other))

    def fetch(b):
        return pltpu.make_async_copy(
            ge_out.at[pl.ds(b * NZ, NZ)], v.EX.at[2 + lax.rem(b, 2)], lsem.at[1 + lax.rem(b, 2)]
        )

    fetch(0).start()
    same = lax.broadcasted_iota(jnp.int32, (S, S), 0) == lax.broadcasted_iota(jnp.int32, (S, S), 1)
    own_ids = jnp.sum(
        jnp.where(same, ids_out[d, :, pl.ds(0, S)].astype(F32), 0.0), axis=1, keepdims=True
    )

    def pairs_of(b, carry):
        pl.when(b + 1 < N // NZ)(lambda: fetch(b + 1).start())
        fetch(b).wait()
        for i in range(NZ):
            both = dot_nt(DB[2], v.EX[2 + lax.rem(b, 2), i])
            theirs = ids_out[b * NZ + i, :, pl.ds(0, S)].astype(F32)
            carry = carry + jnp.where(own_ids == theirs, both, 0.0)
        return carry

    both = lax.fori_loop(0, N // NZ, pairs_of, jnp.zeros((S, S), F32))
    squares = squares + jnp.sum(both)
    squares = squares + jnp.where(d == 0, jnp.sum(total_norms * total_norms), 0.0)
    v.SQ[0] = jnp.zeros((1, 128), F32) + squares
    spread("sq", v.SQ.at[0], v.SQS)
    v.SQS[d] = v.SQ[0]
    v.ng_out[...] = total_norms
    gather_all("sq", v.SQS)
    all_squares = v.SQS[0]
    for i in range(1, N):
        all_squares = all_squares + v.SQS[i]
    v.stats_out[...] = jnp.concatenate(
        [jnp.zeros((1, 128), F32) + loss_value, jnp.sqrt(all_squares), jnp.zeros((6, 128), F32)], axis=0
    )
    for finish in later:
        finish()


def run_step(sizes, *args):
    NR, NF, S, D, rows = sizes
    N, nr = NR * NF, D // NF
    vmem = pl.BlockSpec(memory_space=pltpu.VMEM)
    smem = pl.BlockSpec(memory_space=pltpu.SMEM)
    hbm = pl.BlockSpec(memory_space=pl.ANY)
    buffers, copies = step_layout(sizes)
    many = sum(copies.values())
    return pl.pallas_call(
        functools.partial(step_kernel, sizes),
        name="step",
        out_shape=(
            jax.ShapeDtypeStruct((N, 1, 2 * S), jnp.int32),
            jax.ShapeDtypeStruct((TP, 3 * nr, D), BF),
            jax.ShapeDtypeStruct((TP, nr, D), BF),
            jax.ShapeDtypeStruct((8, D), F32),
            jax.ShapeDtypeStruct((8, 128), F32),
            jax.ShapeDtypeStruct((4, N, S), jnp.int32),
            jax.ShapeDtypeStruct((N, S, D), BF),
        ),
        in_specs=[smem] + [vmem] * 6 + [hbm] * 5,
        out_specs=(vmem,) * 6 + (hbm,),
        scratch_shapes=[pltpu.VMEM(*item) for item in buffers.values()]
        + [
            pltpu.SMEM((NF, 1, 2 * S), jnp.int32), pltpu.SemaphoreType.DMA((many,)),
            pltpu.SemaphoreType.DMA((many,)), pltpu.SemaphoreType.DMA((8,)),
        ],
        compiler_params=pltpu.CompilerParams(
            collective_id=0, has_side_effects=True, vmem_limit_bytes=67_000_000
        ),
    )(*args)


def adamw(weight, grad, first, second, rate):
    first_new = beta_first * first + (1.0 - beta_first) * grad
    second_new = beta_second * second + (1.0 - beta_second) * grad * grad
    first_fix = 1.0 - beta_first**STEP
    second_fix = 1.0 - beta_second**STEP
    update = first_new / first_fix / (jnp.sqrt(second_new / second_fix) + adam_floor)
    return (weight - rate * (update + weight_decay * weight), first_new, second_new)


CHUNK, SLOTS = 424, 6


def finish_kernel(sizes, *refs):
    NR, NF, S, D, rows = sizes
    N, nr = NR * NF, D // NF
    names = ("lists", "ge", "ff", "fa", "norms", "stats", "pw", "pm", "pv") + tuple(
        f"{kind}{which}" for kind in "eaogd" for which in range(3)
    )
    results = ("qw", "qm", "qv") + tuple(f"{kind}{which}_new" for kind in "eaogd" for which in range(3))
    scratch = (
        "grads", "landing", "stage", "TB", "LA", "LO", "LG", "LD", "sems",
        "ins", "outs", "tin", "tout",
    )
    v = types.SimpleNamespace(**dict(zip((*names, *results, *scratch), refs, strict=True)))
    n_chunks = rows // CHUNK

    def fetch(s):
        return pltpu.make_async_copy(v.ge.at[s], v.landing.at[lax.rem(s, 4)], v.sems.at[lax.rem(s, 4)])

    for s in range(3):
        fetch(s).start()
    layers = (("a", v.LA), ("o", v.LO), ("d", v.LD), ("g", v.LG))

    def layer(index, inward):
        kind, buffer = layers[index]
        for which in range(3):
            if inward:
                yield pltpu.make_async_copy(
                    getattr(v, f"{kind}{which}"), buffer.at[which], v.ins.at[index * 3 + which]
                )
            else:
                yield pltpu.make_async_copy(
                    buffer.at[which], getattr(v, f"{kind}{which}_new"), v.outs.at[index * 3 + which]
                )

    def chunk(k, inward):
        at, slot = pl.ds(k * CHUNK, CHUNK), k % SLOTS
        for which in range(3):
            old, new = getattr(v, f"e{which}"), getattr(v, f"e{which}_new")
            if inward:
                yield pltpu.make_async_copy(old.at[at], v.TB.at[slot, which], v.tin.at[slot, which])
            else:
                yield pltpu.make_async_copy(v.TB.at[slot, which], new.at[at], v.tout.at[slot, which])

    for index in range(4):
        for item in layer(index, True):
            item.start()
    for k in range(min(SLOTS, n_chunks)):
        for item in chunk(k, True):
            item.start()

    factor = jnp.minimum(1.0, clip_level / (v.stats[1:2, 0:1] + 1e-06))

    def apply(buffer, at, grad):
        index = tuple(at)
        new = adamw(
            buffer[(0, *index)], grad * factor, buffer[(1, *index)], buffer[(2, *index)], learn_rate
        )
        for which in range(3):
            buffer[(which, *index)] = new[which]

    def finish_layer(index):
        for item in layer(index, False):
            item.start()

    whole = pl.ds(0, nr)
    for item in layer(0, True):
        item.wait()
    for q in range(3):
        apply(v.LA, (whole, pl.ds(q * D, D)), v.fa[q].astype(F32))
    finish_layer(0)
    for item in layer(1, True):
        item.wait()
    apply(v.LO, (whole, pl.ds(0, D)), v.fa[3].astype(F32))
    finish_layer(1)
    for item in layer(2, True):
        item.wait()

    def down(q, carry):
        at = pl.ds(pl.multiple_of(q * nr, 16), nr)
        apply(v.LD, (at, pl.ds(0, D)), v.ff[q, pl.ds(2 * nr, nr), :].astype(F32))
        return carry

    lax.fori_loop(0, TP, down, 0)
    finish_layer(2)
    for item in layer(3, True):
        item.wait()
    quarter, span = D // TP, 2 * D // 6
    at_row = lax.broadcasted_iota(jnp.int32, (span, D), 0)
    at_col = lax.broadcasted_iota(jnp.int32, (span, D), 1)
    group = lax.div(at_col, nr)
    unit = lax.div(group, TP) * nr + (at_col - group * nr)
    holder = lax.rem(group, TP)
    for b in range(TP):
        first = quarter * b // 128 * 128
        total = jnp.zeros((2 * nr, D), F32)
        for q in range(TP):
            pick = (at_row + (first - quarter * b) == unit) & (holder == q)
            total = total + dot(
                v.ff[q, pl.ds(0, 2 * nr), pl.ds(first, span)], jnp.where(pick, 1.0, 0.0).astype(BF)
            )
        apply(v.LG, (whole, pl.ds(b * D, D)), total[:nr])
        apply(v.LG, (whole, pl.ds((TP + b) * D, D)), total[nr:])
    finish_layer(3)
    at_row = lax.broadcasted_iota(jnp.int32, (D, 128), 0)
    at_col = lax.broadcasted_iota(jnp.int32, (D, 128), 1)
    pick = (at_row - lax.axis_index("fsdp") * nr == at_col) & (at_col < nr)
    mine = lax.dot_general(
        v.norms[...], jnp.where(pick, 1.0, 0.0), (((1,), (0,)), ((), ())),
        precision=lax.Precision.HIGHEST, preferred_element_type=F32,
    )
    v.qw[...], v.qm[...], v.qv[...] = adamw(
        v.pw[...], mine[:6, :nr] * factor, v.pm[...], v.pv[...], norm_rate
    )

    def clear(i, carry):
        v.grads[pl.ds(pl.multiple_of(i * CHUNK, 8), CHUNK), :] = jnp.zeros((CHUNK, D), F32)
        return carry

    lax.fori_loop(0, n_chunks, clear, 0)

    def sequence(s, carry):
        pl.when(s + 3 < N)(lambda: fetch(s + 3).start())
        fetch(s).wait()
        v.stage[...] = v.landing[lax.rem(s, 4)].astype(F32)

        def token(k, inner):
            high, low = lax.shift_right_logical(k, shift), lax.bitwise_and(k, S - 1)
            at = pl.ds(v.lists[0, high, low], 1)
            v.grads[at, :] = v.grads[at, :] + v.stage[pl.ds(v.lists[1, high, low], 1), :]
            return inner

        return lax.fori_loop(v.lists[2, s, 0], v.lists[3, s, 0], token, carry)

    shift = S.bit_length() - 1
    lax.fori_loop(0, N, sequence, 0)

    for k in range(n_chunks):
        for item in chunk(k, True):
            item.wait()
        slot = k % SLOTS

        def part(first, size, k=k, slot=slot):
            at = pl.ds(pl.multiple_of(k * CHUNK + first, 8), size)
            grad = v.grads[at, :]
            apply(v.TB.at[slot], (pl.ds(pl.multiple_of(first, 8), size), pl.ds(0, D)), grad)

        def tile(i, carry, part=part):
            part(i * 32, 32)
            return carry

        lax.fori_loop(0, CHUNK // 32, tile, 0)
        if CHUNK % 32:
            part(CHUNK // 32 * 32, CHUNK % 32)
        for item in chunk(k, False):
            item.start()
        if k >= 1 and k - 1 + SLOTS < n_chunks:
            for item in chunk(k - 1, False):
                item.wait()
            for item in chunk(k - 1 + SLOTS, True):
                item.start()
    for k in range(n_chunks):
        if k + SLOTS >= n_chunks or k == n_chunks - 1:
            for item in chunk(k, False):
                item.wait()
    for index in range(4):
        for item in layer(index, False):
            item.wait()


def finish(sizes, lists, ge, ff, fa, norms, stats, norm_state, states):
    NR, NF, S, D, rows = sizes
    N, nr = NR * NF, D // NF
    hbm = pl.BlockSpec(memory_space=pl.ANY)
    vmem = pl.BlockSpec(memory_space=pltpu.VMEM)
    smem = pl.BlockSpec(memory_space=pltpu.SMEM)
    flat = [item for state in states for item in state]
    shapes = [jax.ShapeDtypeStruct(item.shape, F32) for item in (*norm_state, *flat)]
    return pl.pallas_call(
        functools.partial(finish_kernel, sizes),
        name="finish",
        out_shape=tuple(shapes),
        in_specs=[smem, hbm] + [vmem] * 7 + [hbm] * 15,
        out_specs=(vmem,) * 3 + (hbm,) * 15,
        scratch_shapes=[
            pltpu.VMEM((rows, D), F32), pltpu.VMEM((4, S, D), BF), pltpu.VMEM((S, D), F32),
            pltpu.VMEM((SLOTS, 3, CHUNK, D), F32),
            pltpu.VMEM((3, nr, 3 * D), F32), pltpu.VMEM((3, nr, D), F32), pltpu.VMEM((3, nr, 8 * D), F32),
            pltpu.VMEM((3, 4 * nr, D), F32),
            pltpu.SemaphoreType.DMA((4,)), pltpu.SemaphoreType.DMA((12,)),
            pltpu.SemaphoreType.DMA((12,)), pltpu.SemaphoreType.DMA((SLOTS, 3)),
            pltpu.SemaphoreType.DMA((SLOTS, 3)),
        ],
        compiler_params=pltpu.CompilerParams(vmem_limit_bytes=62_000_000),
    )(lists, ge, ff, fa, norms, stats, *norm_state, *flat)


def table_kernel(sizes, ids, ge, factor, w, m, v, w_out, m_out, v_out, grads, landing, stage, sems):
    NR, NF, S, D, rows = sizes
    N = NR * NF
    step = pl.program_id(0)
    block = w.shape[0]

    @pl.when(step == 0)
    def _():
        start_row = lax.axis_index("fsdp") * rows

        def fetch(s):
            return pltpu.make_async_copy(ge.at[s], landing.at[lax.rem(s, 4)], sems.at[lax.rem(s, 4)])

        for s in range(3):
            fetch(s).start()

        def clear(i, carry):
            grads[pl.ds(pl.multiple_of(i * block, 8), block), :] = jnp.zeros((block, D), F32)
            return carry

        lax.fori_loop(0, grads.shape[0] // block, clear, 0)

        def sequence(s, carry):
            pl.when(s + 3 < N)(lambda: fetch(s + 3).start())
            fetch(s).wait()
            stage[...] = landing[lax.rem(s, 4)].astype(F32)

            def token(j, inner):
                wanted = ids[s, 0, j] - start_row

                @pl.when((wanted >= 0) & (wanted < rows))
                def _():
                    at = pl.ds(wanted, 1)
                    grads[at, :] = grads[at, :] + stage[pl.ds(j, 1), :]

                return inner

            return lax.fori_loop(0, S, token, carry)

        lax.fori_loop(0, N, sequence, 0)

    grad = grads[pl.ds(pl.multiple_of(step * block, 8), block), :] * factor[0:1, 0:1]
    w_out[...], m_out[...], v_out[...] = adamw(w[...], grad, m[...], v[...], learn_rate)


def update_table(sizes, ids, ge, factor, w, m, v):
    NR, NF, S, D, rows = sizes
    block = 424
    steps = pl.cdiv(rows, block)
    part = pl.BlockSpec((block, D), lambda i: (i, 0))
    return pl.pallas_call(
        functools.partial(table_kernel, sizes),
        name="table",
        grid=(steps,),
        out_shape=(jax.ShapeDtypeStruct((rows, D), F32),) * 3,
        in_specs=[
            pl.BlockSpec(memory_space=pltpu.SMEM), pl.BlockSpec(memory_space=pl.ANY),
            pl.BlockSpec((8, 128), lambda i: (0, 0)), part, part, part,
        ],
        out_specs=(part, part, part),
        scratch_shapes=[
            pltpu.VMEM((steps * block, D), F32), pltpu.VMEM((4, S, D), BF), pltpu.VMEM((S, D), F32),
            pltpu.SemaphoreType.DMA((4,)),
        ],
        compiler_params=pltpu.CompilerParams(vmem_limit_bytes=60_000_000),
    )(ids, ge, factor, w, m, v)


def local(
    sizes,
    token_ids,
    lengths,
    slot_order,
    pair_labels,
    embedding,
    attend_weight,
    attention_output_matrix,
    gate_up,
    contract_kernel,
    norm_params,
    embedding_first,
    embedding_second,
    attend_first,
    attend_second,
    output_first,
    output_second,
    gate_up_first,
    gate_up_second,
    down_first,
    down_second,
    norm_first,
    norm_second,
):
    NR, NF, S, D, rows = sizes
    nr = D // NF
    f = lax.axis_index("fsdp")
    N = NR * NF
    positions = jnp.arange(S)
    angles = (
        positions.astype(F32)[:, None]
        * (1000.0 ** (-2.0 * jnp.arange(HD // 2).astype(F32) / HD))[None, :]
    )
    cosine, sine = jnp.tile(jnp.cos(angles), (1, 128 * 2 // HD)), jnp.tile(jnp.sin(angles), (1, 128 * 2 // HD))
    ids, ffn, att, norms, stats, lists, ge = run_step(
        sizes,
        lengths,
        token_ids,
        norm_params,
        slot_order.reshape(1, N),
        pair_labels.reshape(1, N),
        cosine,
        sine,
        attend_weight,
        attention_output_matrix,
        gate_up,
        contract_kernel,
        embedding,
    )
    loss_value, grad_norm = stats[0, 0], stats[1, 0]
    if rows % CHUNK == 0:
        norm_next, *rest = split_three(
            finish(
                sizes, lists, ge, ffn, att, norms, stats, (norm_params, norm_first, norm_second),
                (
                    (embedding, embedding_first, embedding_second),
                    (attend_weight, attend_first, attend_second),
                    (attention_output_matrix, output_first, output_second),
                    (gate_up, gate_up_first, gate_up_second),
                    (contract_kernel, down_first, down_second),
                ),
            )
        )
        return (loss_value, grad_norm, *(item for state in rest for item in state), *norm_next)
    factor = jnp.minimum(1.0, clip_level / (grad_norm + 1e-06))
    factor_tile = jnp.broadcast_to(factor, (8, 128))
    emb_next = update_table(sizes, ids, ge, factor_tile, embedding, embedding_first, embedding_second)
    fin = ffn.reshape(TP, 3, nr, D)
    grad_attend = att[:3].transpose(1, 0, 2).reshape(nr, 3 * D).astype(F32)
    grad_output = att[3].astype(F32)
    grad_hidden = (
        fin[:, :2].reshape(TP, 2, nr, NF, nr).transpose(2, 1, 3, 0, 4).reshape(nr, 8 * D).astype(F32)
    )
    grad_down = fin[:, 2].reshape(TP * nr, D).astype(F32)
    grad_norms = lax.dynamic_slice(norms, (0, f * nr), (6, nr))
    att_next = adamw(attend_weight, grad_attend * factor, attend_first, attend_second, learn_rate)
    out_next = adamw(
        attention_output_matrix, grad_output * factor, output_first, output_second, learn_rate
    )
    gate_next = adamw(gate_up, grad_hidden * factor, gate_up_first, gate_up_second, learn_rate)
    down_next = adamw(contract_kernel, grad_down * factor, down_first, down_second, learn_rate)
    norm_next = adamw(norm_params, grad_norms * factor, norm_first, norm_second, norm_rate)
    return (
        loss_value, grad_norm, *emb_next, *att_next, *out_next, *gate_next, *down_next, *norm_next
    )


def split_three(flat):
    return [flat[i : i + 3] for i in range(0, len(flat), 3)]


def solution(mesh):
    NR, NF = mesh.shape["rep"], mesh.shape["fsdp"]
    rows_spec, cols_spec = P("fsdp", None), P(None, "fsdp")

    def step(*args):
        S, D, rows = args[0].shape[1], args[4].shape[1], args[4].shape[0] // NF
        run = jax.shard_map(
            functools.partial(local, (NR, NF, S, D, rows)),
            mesh=mesh,
            in_specs=(P(("rep", "fsdp"), None), P(("rep", "fsdp")), P(), P())
            + (rows_spec,) * 5 + (cols_spec,) + (rows_spec,) * 10 + (cols_spec,) * 2,
            out_specs=(P(), P()) + (rows_spec,) * 15 + (cols_spec,) * 3,
            check_vma=False,
        )
        return run(*args)

    return step
```

```python
import functools
import types

import jax
import jax.numpy as jnp
from jax import lax
from jax.experimental import pallas as pl
from jax.experimental.pallas import tpu as pltpu
from jax.sharding import PartitionSpec as P

H = 12
HD = 64
STEP = 4
TP = 4
MESH = pl.DeviceIdType.MESH
BF = jnp.bfloat16
F32 = jnp.float32

logit_divisor = 0.05
clip_level = 0.001
learn_rate = 0.02
norm_rate = 0.3
weight_decay = 0.01
beta_first = 0.5
beta_second = 0.75
adam_floor = 1e-08


def dot(a, b):
    return lax.dot_general(a, b, (((1,), (0,)), ((), ())), preferred_element_type=F32)


def dot_nt(a, b):
    return lax.dot_general(a, b, (((1,), (1,)), ((), ())), preferred_element_type=F32)


def dot_tn(a, b):
    return lax.dot_general(a, b, (((0,), (0,)), ((), ())), preferred_element_type=F32)


def layer_norm(values, gain, shift):
    centred = values - jnp.mean(values, axis=-1, keepdims=True)
    inverse = lax.rsqrt(jnp.mean(centred * centred, axis=-1, keepdims=True) + 1e-06)
    normed = centred * inverse
    return normed * gain + shift, normed, inverse


def norm_back(upstream, normed, inverse, gain):
    scaled = upstream * gain
    inner = (
        scaled
        - jnp.mean(scaled, axis=-1, keepdims=True)
        - normed * jnp.mean(scaled * normed, axis=-1, keepdims=True)
    )
    return (
        inner * inverse,
        jnp.sum(upstream * normed, axis=0, keepdims=True),
        jnp.sum(upstream, axis=0, keepdims=True),
    )


def step_layout(sizes):
    NR, NF, S, D, rows = sizes
    NZ, NG = NF // 2, NR // TP
    N, nr = NR * NF, D // NF
    block = (S, D)
    buffers = dict(
        pool=((max(0 if rows % 8 else rows, 30 * S), D), F32),
        table=((rows, D) if rows % 8 else (8, 128), F32),
        stage=(block, F32),
        W7=((7, D, D), BF),
        GW=((4, D, D), BF),
        EX=((4, NZ, S, D), BF),
        GNB=((NF, 8, 128), F32),
        H0B=(block, BF), QKV=((3, S, D), BF), ATT=(block, BF), PS=((D // HD, S, S), F32),
        H1=((TP, S, D), BF), MIX=((TP, S, D), BF), DF=((TP, S, D), BF), DG=((2, TP, S, D), BF),
        LX=((TP, S, D), BF), RX=((TP, S, D), BF), DQB=((3, S, D), BF), DB=((3, S, D), BF),
        INV=((3, S, 1), F32), YS=((2, S, D), BF), YR=((2, S, D), BF),
        PB=((N, 1, D), F32), PROW=((1, 1, D), F32), PM=((N, D), F32),
        XR=((4, NZ, nr, D), BF), ZS=((4, NZ, nr, D), BF), ZR=((4, NZ, nr, D), BF),
        NGS=((4, 8, D), F32), NGR=((3, 8, D), F32), NGZ=((NZ, 8, D), F32),
        SQ=((1, 1, 128), F32), SQS=((N, 1, 128), F32),
        PA=((nr, D), F32), PD=((nr, D), F32), PG=((nr, 8 * D), F32), IDF=((N, S), F32), RANK=((2, N, S), F32),
        FG=((NG, 4 * nr, D) if NG > 1 else (1, 16, 128), BF),
    )
    copies = dict(
        ids=1, gn=1, ex=NZ, ez=NZ, wu=3 * NZ, wd=3 * NZ, wx0=NZ, wx1=NZ, wx2=NZ, wx3=NZ, vu=2 * NZ, vd=2 * NZ, ay=NF, ac=2 * NF,
        h1=3, fc=2, fy=1, pool=1, df=3, bc=2, by=1, lx=TP, rx=TP, gx=4 * NZ, gz=4 * NZ, nc=1, ny=1, nx=1,
        nz=NZ, ff=3, fa=3, gg=2 * NG, sq=1, eu=2 * NZ, ed=2 * NZ, e0x=NZ, e0y=NF, e0c=2 * NF, e1x=2 * NZ, e1y=NZ,
        e1c=2 * NF, eg=NG,
    )
    return buffers, copies


def step_kernel(sizes, *refs):
    NR, NF, S, D, rows = sizes
    NX, NZ, NG = 2, NF // 2, NR // TP
    N, nr = NR * NF, D // NF
    HI = lax.Precision.HIGHEST
    buffers, copies = step_layout(sizes)
    given = (
        "length_in", "ids_in", "gn_in", "order_in", "labels_in", "cos_in", "sin_in", "qkv_in", "o_in", "gu_in", "down_in",
        "w_in", "ids_out", "ff_out", "fa_out", "ng_out", "stats_out", "list_out", "ge_out",
    )
    v = types.SimpleNamespace(**dict(zip((*given, *buffers, "sids", "ssem", "rsem", "lsem"), refs, strict=True)))
    pool, W7, GW, DB, DQB, QKV = v.pool, v.W7, v.GW, v.DB, v.DQB, v.QKV
    ssem, rsem, lsem, ids_out, ge_out = v.ssem, v.rsem, v.lsem, v.ids_out, v.ge_out
    r = lax.axis_index("rep")
    f = lax.axis_index("fsdp")
    d = r * NF + f
    z, x = lax.div(f, NX), lax.rem(f, NX)
    g, t = lax.div(r, TP), lax.rem(r, TP)
    y, c = lax.div(t, 2), lax.rem(t, 2)
    ty = (1 - y) * 2 + c
    tc = y * 2 + 1 - c
    tyc = (1 - y) * 2 + 1 - c
    dev_x = (r, z * NX + 1 - x)
    dev_y = (g * TP + ty, f)
    dev_c = (g * TP + tc, f)

    GATE, UP, PT, PT2 = 0, 4 * S, 8 * S, 12 * S
    CR, CR2 = 16 * S, 18 * S
    H0F, H1F, HAT, DS2, DS1, DQ = 20 * S, 21 * S, 22 * S, 25 * S, 26 * S, 27 * S

    def blk(offset, index=0):
        return pl.ds(pl.multiple_of(offset + index * S, 128), S)

    sem_at, used = {}, 0
    for name, many in copies.items():
        sem_at[name] = used
        used += many
    later = []

    def copy(name, index, src, dst, dev, landing=None):
        base = sem_at[name]
        return pltpu.make_async_remote_copy(
            src_ref=src, dst_ref=dst, send_sem=ssem.at[base + index],
            recv_sem=rsem.at[base + (index if landing is None else landing)],
            device_id=dev, device_id_type=MESH,
        )

    def send(name, index, src, dst, dev, only=None, landing=None):
        def start():
            copy(name, index, src, dst, dev, landing).start()

        def finish():
            copy(name, index, src, dst, dev, landing).wait_send()

        if only is None:
            start()
            later.append(finish)
        else:
            pl.when(only)(start)
            later.append(lambda: pl.when(only)(finish))

    def arrive(name, index, dst, only=None):
        def wait():
            pltpu.make_async_copy(dst, dst, rsem.at[sem_at[name] + index]).wait()

        if only is None:
            wait()
        else:
            pl.when(only)(wait)

    def spread(name, src, dst):
        base = sem_at[name]

        def one(k, carry):
            to = lax.rem(d + k, N)
            pltpu.make_async_remote_copy(
                src_ref=src, dst_ref=dst.at[d], send_sem=ssem.at[base], recv_sem=rsem.at[base],
                device_id=(lax.div(to, NF), lax.rem(to, NF)), device_id_type=MESH,
            ).start()
            return carry

        lax.fori_loop(1, N, one, 0)
        rest = dst.at[pl.ds(0, N - 1)]
        later.append(lambda: pltpu.make_async_copy(rest, rest, ssem.at[base]).wait())

    def gather_all(name, dst):
        rest = dst.at[pl.ds(0, N - 1)]
        pltpu.make_async_copy(rest, rest, rsem.at[sem_at[name]]).wait()

    def keep(only, ref, at, value):
        @pl.when(only)
        def _():
            ref[at] = value

    def load(src, dst, sem):
        done = pltpu.make_async_copy(src, dst, lsem.at[sem])
        done.start()
        return done

    table = v.table if rows % 8 else pool.at[pl.ds(0, rows)]
    slots = [t, 4, 5, 6]

    def wrow(index):
        return pl.ds(pl.multiple_of(index * nr, 16), nr)

    got_gate = load(v.gu_in, v.PG, 1)
    got_down = load(v.down_in.at[wrow(t)], v.PD, 2)

    @pl.when(t < 3)
    def _():
        load(v.qkv_in.at[:, pl.ds(pl.multiple_of(jnp.minimum(t, 2) * D, 128), D)], v.PA, 3)

    @pl.when(t == 3)
    def _():
        load(v.o_in, v.PA, 3)

    length = v.length_in[0]
    ids_out[d, :, pl.ds(0, S)] = v.ids_in[...]
    ids_out[d, :, pl.ds(S, S)] = jnp.zeros((1, S), jnp.int32) + length
    v.GNB[f] = jnp.zeros((8, 128), F32)
    v.GNB[f, 0:6, 0:nr] = v.gn_in[...].astype(BF).astype(F32)
    barrier = pltpu.get_barrier_semaphore()

    def greet(k, carry):
        to = lax.rem(d + k, N)
        pl.semaphore_signal(
            barrier, inc=1, device_id=(lax.div(to, NF), lax.rem(to, NF)), device_id_type=MESH
        )
        return carry

    lax.fori_loop(1, N, greet, 0)
    pltpu.make_async_copy(v.o_in, v.PA, lsem.at[3]).wait()
    W7[t, wrow(f), :] = v.PA[...].astype(BF)
    got_down.wait()
    W7[6, wrow(f), :] = v.PD[...].astype(BF)
    got_gate.wait()
    got_table = load(v.w_in, table, 0)
    quarter, span = D // TP, D // 3
    unit_row = lax.broadcasted_iota(jnp.int32, (D, span), 0)
    unit_col = lax.broadcasted_iota(jnp.int32, (D, span), 1)
    unit_group = lax.div(unit_row, nr)
    unit_at = lax.div(unit_group, TP) * nr + (unit_row - unit_group * nr)
    unit_mine = lax.rem(unit_group, TP) == t
    tiles = [jnp.zeros((2 * nr, 128), F32) for _ in range(D // 128)]
    for b in range(TP):
        first = quarter * b // 128 * 128
        choose = unit_mine & (unit_at + (quarter * b - first) == unit_col)
        both = jnp.concatenate(
            [v.PG[:, pl.ds(b * D, D)], v.PG[:, pl.ds((TP + b) * D, D)]], axis=0
        ).astype(BF)
        found = dot(both, jnp.where(choose, 1.0, 0.0).astype(BF))
        for i in range(span // 128):
            tiles[first // 128 + i] = tiles[first // 128 + i] + found[:, i * 128 : (i + 1) * 128]
    hidden = jnp.concatenate(tiles, axis=1).astype(BF)
    W7[4, wrow(f), :] = hidden[:nr]
    W7[5, wrow(f), :] = hidden[nr:]
    pl.semaphore_wait(barrier, N - 1)

    spread("ids", ids_out.at[d], ids_out)

    def piece(m, origin_z, origin_x):
        return W7.at[slots[m], wrow(origin_z * NX + origin_x)]

    def up_to(m, origin, only, which):
        here = piece(m, origin, which)
        if m < 3:
            send("wu", m * NZ + origin, here, here, (r, f + NX), only)
        else:
            send("vu", which * NZ + origin, here, here, (r, f + NX), only)

    def down_to(m, origin, only, which):
        here = piece(m, origin, which)
        if m < 3:
            send("wd", m * NZ + origin, here, here, (r, f - NX), only)
        else:
            send("vd", which * NZ + origin, here, here, (r, f - NX), only)

    def across(m, origin, only=None):
        here = piece(m, origin, x)
        send(f"wx{m}", origin, here, here, dev_x, only)

    def publish(index, only=None):
        here = W7.at[t, wrow(index)]
        send("ay", index, here, here, dev_y, only)
        send("ac", index, here, here, dev_c, only)

    def own_pieces(m):
        up_to(m, z, z + 1 < NZ, x)
        down_to(m, z, z >= 1, x)
        across(m, z)

    def relay(m, k):
        low, high = z - k, z + k
        below, above = jnp.maximum(low, 0), jnp.minimum(high, NZ - 1)
        for which in (x,) if m < 3 else (x, 1 - x):
            first = m * NZ if m < 3 else which * NZ
            arrive("wu" if m < 3 else "vu", first + below, piece(m, below, which), low >= 0)
            up_to(m, below, (low >= 0) & (z + 1 < NZ), which)
            if m < 3:
                across(m, below, low >= 0)
            if m == 0:
                publish(below * NX + x, low >= 0)
            arrive("wd" if m < 3 else "vd", first + above, piece(m, above, which), high < NZ)
            down_to(m, above, (high < NZ) & (z >= 1), which)
            if m < 3:
                across(m, above, high < NZ)
            if m == 0:
                publish(above * NX + x, high < NZ)

    own_pieces(0)
    publish(f)
    base_gn = sem_at["gn"]

    def gn_one(k, carry):
        pltpu.make_async_remote_copy(
            src_ref=v.GNB.at[f], dst_ref=v.GNB.at[f], send_sem=ssem.at[base_gn], recv_sem=rsem.at[base_gn],
            device_id=(r, lax.rem(f + k, NF)), device_id_type=MESH,
        ).start()
        return carry

    lax.fori_loop(1, NF, gn_one, 0)
    gn_rest = v.GNB.at[pl.ds(0, NF - 1)]
    later.append(lambda: pltpu.make_async_copy(gn_rest, gn_rest, ssem.at[base_gn]).wait())
    for m in (1, 2, 3):
        own_pieces(m)

    gather_all("ids", ids_out)
    got_sids = load(ids_out.at[pl.ds(pl.multiple_of(r * NF, NF), NF)], v.sids, 5)
    got_sids.wait()
    got_table.wait()
    start_row = f * rows
    EXS, EXO, EXR, EZR = (v.EX.at[i] for i in range(4))

    def rows_of(i, other):
        owner = i * NX + other

        def token(j, inner):
            wanted = v.sids[owner, 0, j] - start_row
            inside = (wanted >= 0) & (wanted < rows)
            row = table[pl.ds(jnp.clip(wanted, 0, rows - 1), 1), :]
            v.stage[pl.ds(j, 1), :] = jnp.where(inside, row, 0.0)
            return inner

        lax.fori_loop(0, S, token, 0, unroll=8)
        return v.stage[...].astype(BF)

    steps = [(m, k) for k in range(1, NZ) for m in (0, 1, 2, 3)]
    jobs = [(i, True) for i in range(NZ)] + [(i, False) for i in range(NZ)]
    at_step = 0
    for number, (i, away) in enumerate(jobs):
        if away:
            EXS[i] = rows_of(i, 1 - x)
            send("ex", i, EXS.at[i], EXR.at[i], dev_x)
        else:
            EXO[i] = rows_of(i, x)
        if number == 1:
            arrive("wx3", z, piece(3, z, 1 - x))
            up_to(3, z, z + 1 < NZ, 1 - x)
            down_to(3, z, z >= 1, 1 - x)
        while at_step < len(steps) * (number + 1) // len(jobs):
            relay(*steps[at_step])
            at_step += 1

    for i in range(NZ):
        arrive("ex", i, EXR.at[i])
        total = EXO[i] + EXR[i]
        EXO[i] = total
        keep(z == i, EZR, i, total)
        send("ez", i, EXO.at[i], EZR.at[z], (r, i * NX + x), z != i, z)
    while at_step < len(steps):
        relay(*steps[at_step])
        at_step += 1

    for i in range(NZ):
        arrive("wx0", i, piece(0, i, 1 - x))
        publish(i * NX + 1 - x)
    for i in range(NF):
        there = W7.at[ty, wrow(i)]
        arrive("ay", i, there)
        send("ac", NF + i, there, there, dev_c)

    arrive("gn", 0, gn_rest)
    tiles = jnp.concatenate([v.GNB[i] for i in range(NF)], axis=1).astype(BF)
    at_row = lax.broadcasted_iota(jnp.int32, (NF * 128, D), 0)
    at_col = lax.broadcasted_iota(jnp.int32, (NF * 128, D), 1)
    lane = lax.bitwise_and(at_row, 127)
    pick = (lane < nr) & (lax.shift_right_logical(at_row, 7) * nr + lane == at_col)
    gains = dot(tiles, jnp.where(pick, 1.0, 0.0).astype(BF))
    gain = [gains[i : i + 1] for i in range(6)]

    for i in range(NZ):
        pl.when(z != i)(functools.partial(arrive, "ez", i, EZR.at[i]))
    embedded = EZR[0].astype(F32)
    for i in range(1, NZ):
        embedded = embedded + EZR[i].astype(F32)
    normed, hat, inverse = layer_norm(embedded, gain[0], gain[1])
    pool[blk(H0F), :] = normed
    pool[blk(HAT, 0), :] = hat
    v.INV[0] = inverse
    v.H0B[...] = normed.astype(BF)

    def to_rank(name, which, src, buffer):
        send(name, which, src, buffer.at[t], (g * TP + which, f), t != which, t)
        keep(t == which, buffer, which, src[...])

    for which in range(3):
        to_rank("lx", which, v.H0B, v.LX)

    for i in range(NF):
        arrive("ac", i, W7.at[tc, wrow(i)])
    for i in range(NF):
        arrive("ac", NF + i, W7.at[tyc, wrow(i)])
    tables = [jnp.concatenate([ref[...]] * (D // 128), axis=1) for ref in (v.cos_in, v.sin_in)]
    in_half = lax.bitwise_and(lax.broadcasted_iota(jnp.int32, (S, D), 1), HD - 1) < HD // 2

    def turn(values, sign):
        partner = jnp.where(
            in_half, pltpu.roll(values, D - HD // 2, 1), pltpu.roll(values, HD // 2, 1)
        )
        signed = jnp.where(in_half, -sign, sign) * tables[1]
        return values * tables[0] + partner * signed

    for j in range(3):
        projected = dot(v.H0B[...], W7[j])
        QKV[j] = (turn(projected, 1.0) if j < 2 else projected).astype(BF)
    allowed = lax.broadcasted_iota(jnp.int32, (1, S), 1) < length
    scaling = HD ** (-0.5)
    first_half = lax.broadcasted_iota(jnp.int32, (S, 128), 1) < HD

    def half(values, which):
        keep = first_half if which == 0 else jnp.logical_not(first_half)
        return jnp.where(keep, values, jnp.zeros_like(values))

    def attend(p, carry):
        lanes = pl.ds(pl.multiple_of(p * 128, 128), 128)
        query, keys, values = QKV[0, :, lanes], QKV[1, :, lanes], QKV[2, :, lanes]
        result = jnp.zeros((S, 128), F32)
        for which in range(2):
            scores = dot_nt(query, half(keys, which)) * scaling
            scores = jnp.where(allowed, scores, -1000000000.0)
            raised = jnp.exp(scores - jnp.max(scores, axis=-1, keepdims=True))
            chances = raised / jnp.sum(raised, axis=-1, keepdims=True)
            v.PS[2 * p + which] = chances
            result = result + dot(chances.astype(BF), half(values, which))
        v.ATT[:, lanes] = result.astype(BF)
        return carry

    lax.fori_loop(0, D // 128, attend, 0)
    branch = dot(v.ATT[...], W7[3])
    normed, hat, inverse = layer_norm(pool[blk(H0F), :] + branch, gain[2], gain[3])
    pool[blk(H1F), :] = normed
    pool[blk(HAT, 1), :] = hat
    v.INV[1] = inverse
    v.H1[t] = normed.astype(BF)

    def share(name, buffer):
        send(name, 0, buffer.at[t], buffer.at[t], dev_y)
        send(name, 1, buffer.at[t], buffer.at[t], dev_c)
        arrive(name, 0, buffer.at[ty])
        send(name, 2, buffer.at[ty], buffer.at[ty], dev_c)
        arrive(name, 1, buffer.at[tc])
        arrive(name, 2, buffer.at[tyc])

    def reduce(names, offset, landing, which):
        for i in range(2):
            send(names[0], i, pool.at[blk(offset, i * 2 + 1 - c)], pool.at[blk(landing, i)], dev_c)
        for i in range(2):
            arrive(names[0], i, pool.at[blk(landing, i)])
        away = pool[blk(offset, (1 - y) * 2 + c), :] + pool[blk(landing, 1 - y), :]
        v.YS[which] = away.astype(BF)
        send(names[1], 0, v.YS.at[which], v.YR.at[which], dev_y)
        mine = pool[blk(offset, t), :] + pool[blk(landing, y), :]
        arrive(names[1], 0, v.YR.at[which])
        return mine + v.YR[which].astype(F32)

    share("h1", v.H1)
    to_rank("lx", 3, v.ATT, v.LX)
    for m in range(1, 3):
        for i in range(NZ):
            arrive(f"wx{m}", i, piece(m, i, 1 - x))

    def forward(b, carry):
        gate, up = dot(v.H1[b], W7[4]), dot(v.H1[b], W7[5])
        pool[blk(GATE, b), :] = gate
        pool[blk(UP, b), :] = up
        mixed = (gate / (1.0 + jnp.exp(-gate)) * up).astype(BF)
        v.MIX[b] = mixed
        pool[blk(PT, b), :] = dot(mixed, W7[6])
        return carry

    lax.fori_loop(0, TP, forward, 0)
    feed = reduce(("fc", "fy"), PT, CR, 0)
    normed, hat, inverse = layer_norm(pool[blk(H1F), :] + feed, gain[4], gain[5])
    pool[blk(HAT, 2), :] = hat
    v.INV[2] = inverse
    present = jnp.where(lax.broadcasted_iota(jnp.int32, (S, 1), 0) < length, 1.0, 0.0)
    share_of = length.astype(F32)
    v.PROW[0] = jnp.sum(normed * present, axis=0, keepdims=True) / share_of

    spread("pool", v.PROW.at[0], v.PB)
    v.PB[d] = v.PROW[0]
    gather_all("pool", v.PB)
    for i in range(N):
        v.PM[pl.ds(i, 1), :] = v.PB[i]
    pooled = v.PM[...]
    wide = lax.broadcasted_iota(jnp.int32, (N, D), 1)
    row_at = lax.broadcasted_iota(jnp.int32, (N, N), 0)
    col_at = lax.broadcasted_iota(jnp.int32, (N, N), 1)
    order, labels = v.order_in[...].astype(F32), v.labels_in[...].astype(F32)

    def column(row):
        return jnp.sum(jnp.where(row_at == col_at, row, 0.0), axis=1, keepdims=True)

    slot_has = jnp.where(column(order) == col_at.astype(F32), 1.0, 0.0).astype(BF)
    label_is = jnp.where(column(labels) == order, 1.0, 0.0).astype(BF)
    paired = dot(slot_has, label_is)
    loss_value = jnp.zeros((1, 1), F32)
    d_pooled = jnp.zeros((N, D), F32)
    for width in (D // 12, D // 3, D):
        portion = jnp.where(wide < width, pooled, 0.0)
        inverse = lax.rsqrt(jnp.sum(portion * portion, axis=1, keepdims=True) + 1e-06)
        unit = portion * inverse
        similar = lax.dot_general(
            unit, unit, (((1,), (1,)), ((), ())), precision=HI, preferred_element_type=F32
        ) / logit_divisor
        similar = jnp.where(row_at == col_at, -1000000000.0, similar)
        row_max = jnp.max(similar, axis=1, keepdims=True)
        raised = jnp.exp(similar - row_max)
        total = jnp.sum(raised, axis=1, keepdims=True)
        target = jnp.sum(jnp.where(paired > 0.0, similar, 0.0), axis=1, keepdims=True)
        term = row_max + jnp.log(total) - target
        loss_value = loss_value + jnp.sum(term, axis=0, keepdims=True) / N
        col_max = jnp.max(similar, axis=0, keepdims=True)
        raised_t = jnp.exp(similar - col_max)
        turned = raised_t / jnp.sum(raised_t, axis=0, keepdims=True)
        d_similar = (raised / total + turned - 2.0 * paired) / (3.0 * N) / logit_divisor
        d_unit = lax.dot_general(
            d_similar, unit, (((1,), (0,)), ((), ())), precision=HI, preferred_element_type=F32
        )
        inner = jnp.sum(d_unit * unit, axis=1, keepdims=True)
        d_pooled = d_pooled + inverse * (d_unit - unit * inner)
    loss_value = loss_value / 3.0
    own_row = lax.broadcasted_iota(jnp.int32, (N, D), 0) == d
    d_mine = jnp.sum(jnp.where(own_row, d_pooled, 0.0), axis=0, keepdims=True)

    d_two = d_mine * present / share_of
    d_sum, d_gain_two, d_shift_two = norm_back(d_two, pool[blk(HAT, 2), :], v.INV[2], gain[4])
    pool[blk(DS2), :] = d_sum
    v.DF[t] = d_sum.astype(BF)
    share("df", v.DF)

    def back(b, carry):
        d_mixed = dot_nt(v.DF[b], W7[6])
        gate, up = pool[blk(GATE, b), :], pool[blk(UP, b), :]
        logistic = 1.0 / (1.0 + jnp.exp(-gate))
        d_gate = (d_mixed * up * (logistic * (1.0 + gate * (1.0 - logistic)))).astype(BF)
        d_up = (d_mixed * (gate * logistic)).astype(BF)
        v.DG[0, b] = d_gate
        v.DG[1, b] = d_up
        pool[blk(PT2, b), :] = dot_nt(d_gate, W7[4]) + dot_nt(d_up, W7[5])
        return carry

    TILE = 256

    def product(left, right, m):
        def tile(i, carry):
            at = pl.ds(pl.multiple_of(i * TILE, TILE), TILE)
            GW[m, at, :] = dot_tn(left(at), right()).astype(BF)
            return carry

        lax.fori_loop(0, D // TILE, tile, 0)

    def part(m, i, other):
        return GW.at[m, wrow(i * NX + other)]

    def give(m):
        for i in range(NZ):
            send("gx", m * NZ + i, part(m, i, 1 - x), v.XR.at[m, i], dev_x)

    def pass_on(m):
        for i in range(NZ):
            arrive("gx", m * NZ + i, v.XR.at[m, i])
            total = (part(m, i, x)[...].astype(F32) + v.XR[m, i].astype(F32)).astype(BF)
            v.ZS[m, i] = total
            keep(z == i, v.ZR, (m, i), total)
            send("gz", m * NZ + i, v.ZS.at[m, i], v.ZR.at[m, z], (r, i * NX + x), z != i, m * NZ + z)

    def product_rows(buffer):
        return lambda at: buffer[:, :, at].reshape(TP * S, TILE)

    product(product_rows(v.MIX), lambda: v.DF[...].reshape(TP * S, D), 3)
    give(3)
    lax.fori_loop(0, TP, back, 0)
    for i in range(2):
        send("bc", i, pool.at[blk(PT2, i * 2 + 1 - c)], pool.at[blk(CR2, i)], dev_c)
    product(product_rows(v.H1), lambda: v.DG[0].reshape(TP * S, D), 1)
    give(1)
    for i in range(2):
        arrive("bc", i, pool.at[blk(CR2, i)])
    away = pool[blk(PT2, (1 - y) * 2 + c), :] + pool[blk(CR2, 1 - y), :]
    v.YS[1] = away.astype(BF)
    send("by", 0, v.YS.at[1], v.YR.at[1], dev_y)
    product(product_rows(v.H1), lambda: v.DG[1].reshape(TP * S, D), 2)
    give(2)
    pass_on(3)
    mine = pool[blk(PT2, t), :] + pool[blk(CR2, y), :]
    arrive("by", 0, v.YR.at[1])
    d_one = pool[blk(DS2), :] + (mine + v.YR[1].astype(F32))

    d_sum, d_gain_one, d_shift_one = norm_back(d_one, pool[blk(HAT, 1), :], v.INV[1], gain[2])
    pool[blk(DS1), :] = d_sum
    DB[0] = d_sum.astype(BF)
    to_rank("rx", 3, DB.at[0], v.RX)
    DB[1] = dot_nt(DB[0], W7[3]).astype(BF)
    pass_on(1)

    def attend_back(p, carry):
        lanes = pl.ds(pl.multiple_of(p * 128, 128), 128)
        query, keys, values = QKV[0, :, lanes], QKV[1, :, lanes], QKV[2, :, lanes]
        grad = DB[1, :, lanes]
        d_query = jnp.zeros((S, 128), F32)
        d_keys = jnp.zeros((S, 128), F32)
        d_values = jnp.zeros((S, 128), F32)
        for which in range(2):
            chances = v.PS[2 * p + which]
            d_values = d_values + dot_tn(chances.astype(BF), half(grad, which))
            d_chances = dot_nt(grad, half(values, which))
            inner = jnp.sum(chances * d_chances, axis=-1, keepdims=True)
            d_scores = (chances * (d_chances - inner)).astype(BF)
            d_query = d_query + dot(d_scores, half(keys, which)) * scaling
            d_keys = d_keys + dot_tn(d_scores, half(query, which)) * scaling
        pool[blk(DQ, 0), lanes] = d_query
        pool[blk(DQ, 1), lanes] = d_keys
        DQB[2, :, lanes] = d_values.astype(BF)
        return carry

    lax.fori_loop(0, D // 128, attend_back, 0)
    for j in range(2):
        DQB[j] = turn(pool[blk(DQ, j), :], -1.0).astype(BF)

    for which in range(3):
        to_rank("rx", which, DQB.at[which], v.RX)
    d_zero = pool[blk(DS1), :]
    for j in range(3):
        d_zero = d_zero + dot_nt(DQB[j], W7[j])
    d_embedded, d_gain_zero, d_shift_zero = norm_back(d_zero, pool[blk(HAT, 0), :], v.INV[0], gain[0])
    DB[2] = d_embedded.astype(BF)

    got_own = load(DB.at[2], ge_out.at[d], 0)
    cut = D // 2
    cols = [pl.ds(0, cut), pl.ds(cut, D - cut)]

    def line(rep, which_x, order, i):
        return ge_out.at[rep * NF + i * NX + which_x, :, cols[order]]

    def all_of(rep, order):
        return ge_out.at[pl.ds(pl.multiple_of(rep * NF, NF), NF), :, cols[order]]

    def ge_up(order, origin, src, only):
        send("eu", order * NZ + origin, src, line(r, x, order, origin), (r, f + NX), only)

    def ge_down(order, origin, src, only):
        send("ed", order * NZ + origin, src, line(r, x, order, origin), (r, f - NX), only)

    ry, rc, ryc = g * TP + ty, g * TP + tc, g * TP + tyc

    def ge_line(order, i, only=None, src=None):
        here = line(r, x, order, i)
        src = here if src is None else src
        if order == 0:
            send("e0x", i, src, here, dev_x, only)
            send("e0y", i * NX + x, src, here, dev_y, only)
            send("e0c", i * NX + x, src, here, dev_c, only)
        else:
            send("e1y", i, src, here, dev_y, only)
            send("e1x", i, src, here, dev_x, only)
            send("e1c", i * NX + x, src, here, dev_c, only)

    def ge_second(i, only):
        here = line(r, 1 - x, 0, i)
        arrive("e0x", i, here, only)
        send("e0y", i * NX + 1 - x, here, here, dev_y, only)
        send("e0c", i * NX + 1 - x, here, here, dev_c, only)
        here = line(ry, x, 1, i)
        arrive("e1y", i, here, only)
        send("e1x", NZ + i, here, here, dev_x, only)
        send("e1c", NF + i * NX + x, here, here, dev_c, only)

    def ge_third(i, only):
        for which_x in (x, 1 - x):
            here = line(ry, which_x, 0, i)
            arrive("e0y", i * NX + which_x, here, only)
            send("e0c", NF + i * NX + which_x, here, here, dev_c, only)
        for which, rep in enumerate((r, ry)):
            here = line(rep, 1 - x, 1, i)
            arrive("e1x", which * NZ + i, here, only)
            send("e1c", which * NF + i * NX + 1 - x, here, here, dev_c, only)

    def at_distance(step, k):
        low, high = z - k, z + k
        step(jnp.maximum(low, 0), low >= 0)
        if k:
            step(jnp.minimum(high, NZ - 1), high < NZ)

    for order in range(2):
        own_cols = DB.at[2, :, cols[order]]
        ge_up(order, z, own_cols, z + 1 < NZ)
        ge_down(order, z, own_cols, z >= 1)
        ge_line(order, z, None, own_cols)

    def ge_relay(k):
        low, high = z - k, z + k
        below, above = jnp.maximum(low, 0), jnp.minimum(high, NZ - 1)
        for order in range(2):
            arrive("eu", order * NZ + below, line(r, x, order, below), low >= 0)
            ge_up(order, below, line(r, x, order, below), (low >= 0) & (z + 1 < NZ))
            ge_line(order, below, low >= 0)
            arrive("ed", order * NZ + above, line(r, x, order, above), high < NZ)
            ge_down(order, above, line(r, x, order, above), (high < NZ) & (z >= 1))
            ge_line(order, above, high < NZ)

    def own_lists():
        for i in range(N):
            v.IDF[pl.ds(i, 1), :] = ids_out[i, :, pl.ds(0, S)].astype(F32)
            v.PM[pl.ds(i, 1), pl.ds(0, S)] = ids_out[i, :, pl.ds(S, S)].astype(F32)
        local_row = v.IDF[...] - (f * rows).astype(F32)
        valid = lax.broadcasted_iota(jnp.int32, (N, S), 1).astype(F32) < v.PM[:, 0:S]
        mine = valid & (local_row >= 0.0) & (local_row < 1.0 * rows)
        marks = jnp.where(mine, 1.0, 0.0).astype(BF)
        before = lax.broadcasted_iota(jnp.int32, (S, S), 0) < lax.broadcasted_iota(jnp.int32, (S, S), 1)
        prefix = dot(marks, jnp.where(before, 1.0, 0.0).astype(BF))
        counts = jnp.zeros((N, S), F32) + jnp.sum(marks.astype(F32), axis=1, keepdims=True)
        offsets = dot(jnp.where(row_at > col_at, 1.0, 0.0).astype(BF), counts.astype(BF))
        place = prefix + offsets
        high = jnp.floor(place * (1.0 / S))
        v.RANK[0] = high
        v.RANK[1] = jnp.where(mine, place - high * S, -1.0)
        v.IDF[...] = jnp.where(mine, local_row, 0.0)
        slot_at = lax.broadcasted_iota(jnp.int32, (N, S), 0).astype(F32)
        low_at = lax.broadcasted_iota(jnp.int32, (S, S), 0).astype(F32)
        token_at = lax.broadcasted_iota(jnp.int32, (1, S), 1).astype(F32)

        def one(i, carry):
            at = pl.ds(i, 1)
            row = v.IDF[at, :]
            row_high = jnp.floor(row * (1.0 / 64))
            spot = v.RANK[0, at, :] == slot_at
            left = jnp.concatenate(
                [jnp.where(spot, item, 0.0) for item in (row_high, row - row_high * 64.0, token_at)], axis=0
            ).astype(BF)
            right = jnp.where(v.RANK[1, at, :] == low_at, 1.0, 0.0).astype(BF)
            return carry + dot_nt(left, right)

        found = lax.fori_loop(0, N, one, jnp.zeros((3 * N, S), F32))
        v.list_out[0] = (found[:N] * 64.0 + found[N : 2 * N]).astype(jnp.int32)
        v.list_out[1] = found[2 * N :].astype(jnp.int32)
        v.list_out[2] = offsets.astype(jnp.int32)
        v.list_out[3] = (offsets + counts).astype(jnp.int32)

    v.NGS[0] = jnp.concatenate(
        [d_gain_zero, d_shift_zero, d_gain_one, d_shift_one, d_gain_two, d_shift_two,
         jnp.zeros((2, D), F32)], axis=0)
    stages = (("nc", dev_c), ("ny", dev_y), ("nx", dev_x))

    def norm_send(i):
        send(stages[i][0], 0, v.NGS.at[i], v.NGR.at[i], stages[i][1])

    def norm_add(i):
        arrive(stages[i][0], 0, v.NGR.at[i])
        v.NGS[i + 1] = v.NGS[i] + v.NGR[i]

    def settle(m, out, at):
        for i in range(NZ):
            arrive("gz", m * NZ + i, v.ZR.at[m, i], z != i)
        total = v.ZR[m, 0].astype(F32)
        for i in range(1, NZ):
            total = total + v.ZR[m, i].astype(F32)
        out[t, at, :] = total.astype(BF)

    def group_sum(out, first, size):
        own = v.FG.at[g, pl.ds(first, size)]
        own[...] = out[t]
        for k in range(1, NG):
            other = lax.rem(g + k, NG)
            index = (0 if first else NG) + k
            send("gg", index, own, own, (other * TP + t, f), None, (0 if first else NG) + g)
        for k in range(1, NG):
            other = lax.rem(g + k, NG)
            arrive("gg", (0 if first else NG) + other, v.FG.at[other, pl.ds(first, size)])
        total = v.FG[0, pl.ds(first, size)].astype(F32)
        for k in range(1, NG):
            total = total + v.FG[k, pl.ds(first, size)].astype(F32)
        out[t] = total.astype(BF)

    def share_start(name, buffer):
        send(name, 0, buffer.at[t], buffer.at[t], dev_y)
        send(name, 1, buffer.at[t], buffer.at[t], dev_c)

    def share_pass(name, buffer):
        arrive(name, 0, buffer.at[ty])
        send(name, 2, buffer.at[ty], buffer.at[ty], dev_c)

    def share_end(name, buffer):
        arrive(name, 1, buffer.at[tc])
        arrive(name, 2, buffer.at[tyc])

    norm_send(0)
    pass_on(2)
    for which in range(TP):
        arrive("lx", which, v.LX.at[which], t != which)
        arrive("rx", which, v.RX.at[which], t != which)
    product(product_rows(v.LX), lambda: v.RX[...].reshape(TP * S, D), 0)
    give(0)
    norm_add(0)
    norm_send(1)
    got_own.wait()
    ge_relay(1)
    at_distance(ge_second, 0)
    settle(3, v.ff_out, pl.ds(2 * nr, nr))
    settle(1, v.ff_out, pl.ds(0, nr))
    norm_add(1)
    norm_send(2)
    settle(2, v.ff_out, pl.ds(nr, nr))
    if NG > 1:
        group_sum(v.ff_out, nr, 3 * nr)
    share_start("ff", v.ff_out)
    pass_on(0)
    for k in range(2, NZ):
        ge_relay(k)
        at_distance(ge_second, k - 1)
    at_distance(ge_second, NZ - 1)
    norm_add(2)
    for i in range(NZ):
        send("nz", i, v.NGS.at[3], v.NGZ.at[z], (r, i * NX + x), z != i, z)
        keep(z == i, v.NGZ, i, v.NGS[3])
    own = v.ff_out[t].astype(F32)
    squares = jnp.sum(own * own)
    settle(0, v.fa_out, pl.ds(0, nr))
    if NG > 1:
        group_sum(v.fa_out, 0, nr)
    share_start("fa", v.fa_out)
    own = v.fa_out[t].astype(F32)
    squares = squares + jnp.sum(own * own)
    squares = jnp.where(g == 0, squares, 0.0)
    own_lists()
    for k in range(NZ):
        at_distance(ge_third, k)
    for name, buffer in (("ff", v.ff_out), ("fa", v.fa_out)):
        share_pass(name, buffer)
    for i in range(NZ):
        arrive("nz", i, v.NGZ.at[i], z != i)
    total_norms = v.NGZ[0]
    for i in range(1, NZ):
        total_norms = total_norms + v.NGZ[i]
    for name, buffer in (("ff", v.ff_out), ("fa", v.fa_out)):
        share_end(name, buffer)
    for order, name in enumerate(("e0c", "e1c")):
        for which, rep in enumerate((rc, ryc)):
            for i in range(NF):
                arrive(name, which * NF + i, ge_out.at[rep * NF + i, :, cols[order]])
    if NG > 1:

        def group(which):
            return ge_out.at[pl.ds(pl.multiple_of(which * TP * NF, TP * NF), TP * NF)]

        for k in range(1, NG):
            other = lax.rem(g + k, NG)
            send("eg", k, group(g), group(g), (other * TP + t, f), None, g)
        for k in range(1, NG):
            other = lax.rem(g + k, NG)
            arrive("eg", other, group(other))

    def fetch(b):
        return pltpu.make_async_copy(
            ge_out.at[pl.ds(b * NZ, NZ)], v.EX.at[2 + lax.rem(b, 2)], lsem.at[1 + lax.rem(b, 2)]
        )

    fetch(0).start()
    same = lax.broadcasted_iota(jnp.int32, (S, S), 0) == lax.broadcasted_iota(jnp.int32, (S, S), 1)
    own_ids = jnp.sum(
        jnp.where(same, ids_out[d, :, pl.ds(0, S)].astype(F32), 0.0), axis=1, keepdims=True
    )

    def pairs_of(b, carry):
        pl.when(b + 1 < N // NZ)(lambda: fetch(b + 1).start())
        fetch(b).wait()
        for i in range(NZ):
            both = dot_nt(DB[2], v.EX[2 + lax.rem(b, 2), i])
            theirs = ids_out[b * NZ + i, :, pl.ds(0, S)].astype(F32)
            carry = carry + jnp.where(own_ids == theirs, both, 0.0)
        return carry

    both = lax.fori_loop(0, N // NZ, pairs_of, jnp.zeros((S, S), F32))
    squares = squares + jnp.sum(both)
    squares = squares + jnp.where(d == 0, jnp.sum(total_norms * total_norms), 0.0)
    v.SQ[0] = jnp.zeros((1, 128), F32) + squares
    spread("sq", v.SQ.at[0], v.SQS)
    v.SQS[d] = v.SQ[0]
    v.ng_out[...] = total_norms
    gather_all("sq", v.SQS)
    all_squares = v.SQS[0]
    for i in range(1, N):
        all_squares = all_squares + v.SQS[i]
    v.stats_out[...] = jnp.concatenate(
        [jnp.zeros((1, 128), F32) + loss_value, jnp.sqrt(all_squares), jnp.zeros((6, 128), F32)], axis=0
    )
    for finish in later:
        finish()


def run_step(sizes, *args):
    NR, NF, S, D, rows = sizes
    N, nr = NR * NF, D // NF
    vmem = pl.BlockSpec(memory_space=pltpu.VMEM)
    smem = pl.BlockSpec(memory_space=pltpu.SMEM)
    hbm = pl.BlockSpec(memory_space=pl.ANY)
    buffers, copies = step_layout(sizes)
    many = sum(copies.values())
    return pl.pallas_call(
        functools.partial(step_kernel, sizes),
        name="step",
        out_shape=(
            jax.ShapeDtypeStruct((N, 1, 2 * S), jnp.int32),
            jax.ShapeDtypeStruct((TP, 3 * nr, D), BF),
            jax.ShapeDtypeStruct((TP, nr, D), BF),
            jax.ShapeDtypeStruct((8, D), F32),
            jax.ShapeDtypeStruct((8, 128), F32),
            jax.ShapeDtypeStruct((4, N, S), jnp.int32),
            jax.ShapeDtypeStruct((N, S, D), BF),
        ),
        in_specs=[smem] + [vmem] * 6 + [hbm] * 5,
        out_specs=(vmem,) * 6 + (hbm,),
        scratch_shapes=[pltpu.VMEM(*item) for item in buffers.values()]
        + [
            pltpu.SMEM((NF, 1, 2 * S), jnp.int32), pltpu.SemaphoreType.DMA((many,)),
            pltpu.SemaphoreType.DMA((many,)), pltpu.SemaphoreType.DMA((8,)),
        ],
        compiler_params=pltpu.CompilerParams(
            collective_id=0, has_side_effects=True, vmem_limit_bytes=67_000_000
        ),
    )(*args)


def adamw(weight, grad, first, second, rate):
    first_new = beta_first * first + (1.0 - beta_first) * grad
    second_new = beta_second * second + (1.0 - beta_second) * grad * grad
    first_fix = 1.0 - beta_first**STEP
    second_fix = 1.0 - beta_second**STEP
    update = first_new / first_fix / (jnp.sqrt(second_new / second_fix) + adam_floor)
    return (weight - rate * (update + weight_decay * weight), first_new, second_new)


CHUNK, SLOTS = 424, 7


def finish_kernel(sizes, *refs):
    NR, NF, S, D, rows = sizes
    N, nr = NR * NF, D // NF
    names = ("lists", "ge", "ff", "fa", "norms", "stats", "pw", "pm", "pv") + tuple(
        f"{kind}{which}" for kind in "eaogd" for which in range(3)
    )
    results = ("qw", "qm", "qv") + tuple(f"{kind}{which}_new" for kind in "eaogd" for which in range(3))
    scratch = (
        "grads", "landing", "stage", "TB", "LA", "LO", "LG", "LD", "sems",
        "ins", "outs", "tin", "tout",
    )
    v = types.SimpleNamespace(**dict(zip((*names, *results, *scratch), refs, strict=True)))
    n_chunks = rows // CHUNK

    def fetch(s):
        return pltpu.make_async_copy(v.ge.at[s], v.landing.at[lax.rem(s, 4)], v.sems.at[lax.rem(s, 4)])

    for s in range(3):
        fetch(s).start()
    layers = (("a", v.LA), ("o", v.LO), ("d", v.LD), ("g", v.LG))

    def layer(index, inward):
        kind, buffer = layers[index]
        for which in range(3):
            if inward:
                yield pltpu.make_async_copy(
                    getattr(v, f"{kind}{which}"), buffer.at[which], v.ins.at[index * 3 + which]
                )
            else:
                yield pltpu.make_async_copy(
                    buffer.at[which], getattr(v, f"{kind}{which}_new"), v.outs.at[index * 3 + which]
                )

    def chunk(k, inward):
        at, slot = pl.ds(k * CHUNK, CHUNK), k % SLOTS
        for which in range(3):
            old, new = getattr(v, f"e{which}"), getattr(v, f"e{which}_new")
            if inward:
                yield pltpu.make_async_copy(old.at[at], v.TB.at[slot, which], v.tin.at[slot, which])
            else:
                yield pltpu.make_async_copy(v.TB.at[slot, which], new.at[at], v.tout.at[slot, which])

    for index in range(4):
        for item in layer(index, True):
            item.start()
    for k in range(min(SLOTS, n_chunks)):
        for item in chunk(k, True):
            item.start()

    factor = jnp.minimum(1.0, clip_level / (v.stats[1:2, 0:1] + 1e-06))

    def apply(buffer, at, grad):
        index = tuple(at)
        new = adamw(
            buffer[(0, *index)], grad * factor, buffer[(1, *index)], buffer[(2, *index)], learn_rate
        )
        for which in range(3):
            buffer[(which, *index)] = new[which]

    def finish_layer(index):
        for item in layer(index, False):
            item.start()

    whole = pl.ds(0, nr)
    for item in layer(0, True):
        item.wait()
    for q in range(3):
        apply(v.LA, (whole, pl.ds(q * D, D)), v.fa[q].astype(F32))
    finish_layer(0)
    for item in layer(1, True):
        item.wait()
    apply(v.LO, (whole, pl.ds(0, D)), v.fa[3].astype(F32))
    finish_layer(1)
    for item in layer(2, True):
        item.wait()

    def down(q, carry):
        at = pl.ds(pl.multiple_of(q * nr, 16), nr)
        apply(v.LD, (at, pl.ds(0, D)), v.ff[q, pl.ds(2 * nr, nr), :].astype(F32))
        return carry

    lax.fori_loop(0, TP, down, 0)
    finish_layer(2)
    for item in layer(3, True):
        item.wait()
    quarter, span = D // TP, 2 * D // 6
    at_row = lax.broadcasted_iota(jnp.int32, (span, D), 0)
    at_col = lax.broadcasted_iota(jnp.int32, (span, D), 1)
    group = lax.div(at_col, nr)
    unit = lax.div(group, TP) * nr + (at_col - group * nr)
    holder = lax.rem(group, TP)
    for b in range(TP):
        first = quarter * b // 128 * 128
        total = jnp.zeros((2 * nr, D), F32)
        for q in range(TP):
            pick = (at_row + (first - quarter * b) == unit) & (holder == q)
            total = total + dot(
                v.ff[q, pl.ds(0, 2 * nr), pl.ds(first, span)], jnp.where(pick, 1.0, 0.0).astype(BF)
            )
        apply(v.LG, (whole, pl.ds(b * D, D)), total[:nr])
        apply(v.LG, (whole, pl.ds((TP + b) * D, D)), total[nr:])
    finish_layer(3)
    at_row = lax.broadcasted_iota(jnp.int32, (D, 128), 0)
    at_col = lax.broadcasted_iota(jnp.int32, (D, 128), 1)
    pick = (at_row - lax.axis_index("fsdp") * nr == at_col) & (at_col < nr)
    mine = lax.dot_general(
        v.norms[...], jnp.where(pick, 1.0, 0.0), (((1,), (0,)), ((), ())),
        precision=lax.Precision.HIGHEST, preferred_element_type=F32,
    )
    v.qw[...], v.qm[...], v.qv[...] = adamw(
        v.pw[...], mine[:6, :nr] * factor, v.pm[...], v.pv[...], norm_rate
    )

    def clear(i, carry):
        v.grads[pl.ds(pl.multiple_of(i * CHUNK, 8), CHUNK), :] = jnp.zeros((CHUNK, D), F32)
        return carry

    lax.fori_loop(0, n_chunks, clear, 0)

    def sequence(s, carry):
        pl.when(s + 3 < N)(lambda: fetch(s + 3).start())
        fetch(s).wait()
        v.stage[...] = v.landing[lax.rem(s, 4)].astype(F32)

        def token(k, inner):
            high, low = lax.shift_right_logical(k, shift), lax.bitwise_and(k, S - 1)
            at = pl.ds(v.lists[0, high, low], 1)
            v.grads[at, :] = v.grads[at, :] + v.stage[pl.ds(v.lists[1, high, low], 1), :]
            return inner

        return lax.fori_loop(v.lists[2, s, 0], v.lists[3, s, 0], token, carry)

    shift = S.bit_length() - 1
    lax.fori_loop(0, N, sequence, 0)

    for k in range(n_chunks):
        for item in chunk(k, True):
            item.wait()
        slot = k % SLOTS

        def part(first, size, k=k, slot=slot):
            at = pl.ds(pl.multiple_of(k * CHUNK + first, 8), size)
            grad = v.grads[at, :]
            apply(v.TB.at[slot], (pl.ds(pl.multiple_of(first, 8), size), pl.ds(0, D)), grad)

        def tile(i, carry, part=part):
            part(i * 32, 32)
            return carry

        lax.fori_loop(0, CHUNK // 32, tile, 0)
        if CHUNK % 32:
            part(CHUNK // 32 * 32, CHUNK % 32)
        for item in chunk(k, False):
            item.start()
        if k >= 1 and k - 1 + SLOTS < n_chunks:
            for item in chunk(k - 1, False):
                item.wait()
            for item in chunk(k - 1 + SLOTS, True):
                item.start()
    for k in range(n_chunks):
        if k + SLOTS >= n_chunks or k == n_chunks - 1:
            for item in chunk(k, False):
                item.wait()
    for index in range(4):
        for item in layer(index, False):
            item.wait()


def finish(sizes, lists, ge, ff, fa, norms, stats, norm_state, states):
    NR, NF, S, D, rows = sizes
    N, nr = NR * NF, D // NF
    hbm = pl.BlockSpec(memory_space=pl.ANY)
    vmem = pl.BlockSpec(memory_space=pltpu.VMEM)
    smem = pl.BlockSpec(memory_space=pltpu.SMEM)
    flat = [item for state in states for item in state]
    shapes = [jax.ShapeDtypeStruct(item.shape, F32) for item in (*norm_state, *flat)]
    return pl.pallas_call(
        functools.partial(finish_kernel, sizes),
        name="finish",
        out_shape=tuple(shapes),
        in_specs=[smem, hbm] + [vmem] * 7 + [hbm] * 15,
        out_specs=(vmem,) * 3 + (hbm,) * 15,
        scratch_shapes=[
            pltpu.VMEM((rows, D), F32), pltpu.VMEM((4, S, D), BF), pltpu.VMEM((S, D), F32),
            pltpu.VMEM((SLOTS, 3, CHUNK, D), F32),
            pltpu.VMEM((3, nr, 3 * D), F32), pltpu.VMEM((3, nr, D), F32), pltpu.VMEM((3, nr, 8 * D), F32),
            pltpu.VMEM((3, 4 * nr, D), F32),
            pltpu.SemaphoreType.DMA((4,)), pltpu.SemaphoreType.DMA((12,)),
            pltpu.SemaphoreType.DMA((12,)), pltpu.SemaphoreType.DMA((SLOTS, 3)),
            pltpu.SemaphoreType.DMA((SLOTS, 3)),
        ],
        compiler_params=pltpu.CompilerParams(vmem_limit_bytes=62_000_000),
    )(lists, ge, ff, fa, norms, stats, *norm_state, *flat)


def table_kernel(sizes, ids, ge, factor, w, m, v, w_out, m_out, v_out, grads, landing, stage, sems):
    NR, NF, S, D, rows = sizes
    N = NR * NF
    step = pl.program_id(0)
    block = w.shape[0]

    @pl.when(step == 0)
    def _():
        start_row = lax.axis_index("fsdp") * rows

        def fetch(s):
            return pltpu.make_async_copy(ge.at[s], landing.at[lax.rem(s, 4)], sems.at[lax.rem(s, 4)])

        for s in range(3):
            fetch(s).start()

        def clear(i, carry):
            grads[pl.ds(pl.multiple_of(i * block, 8), block), :] = jnp.zeros((block, D), F32)
            return carry

        lax.fori_loop(0, grads.shape[0] // block, clear, 0)

        def sequence(s, carry):
            pl.when(s + 3 < N)(lambda: fetch(s + 3).start())
            fetch(s).wait()
            stage[...] = landing[lax.rem(s, 4)].astype(F32)

            def token(j, inner):
                wanted = ids[s, 0, j] - start_row

                @pl.when((wanted >= 0) & (wanted < rows))
                def _():
                    at = pl.ds(wanted, 1)
                    grads[at, :] = grads[at, :] + stage[pl.ds(j, 1), :]

                return inner

            return lax.fori_loop(0, S, token, carry)

        lax.fori_loop(0, N, sequence, 0)

    grad = grads[pl.ds(pl.multiple_of(step * block, 8), block), :] * factor[0:1, 0:1]
    w_out[...], m_out[...], v_out[...] = adamw(w[...], grad, m[...], v[...], learn_rate)


def update_table(sizes, ids, ge, factor, w, m, v):
    NR, NF, S, D, rows = sizes
    block = 424
    steps = pl.cdiv(rows, block)
    part = pl.BlockSpec((block, D), lambda i: (i, 0))
    return pl.pallas_call(
        functools.partial(table_kernel, sizes),
        name="table",
        grid=(steps,),
        out_shape=(jax.ShapeDtypeStruct((rows, D), F32),) * 3,
        in_specs=[
            pl.BlockSpec(memory_space=pltpu.SMEM), pl.BlockSpec(memory_space=pl.ANY),
            pl.BlockSpec((8, 128), lambda i: (0, 0)), part, part, part,
        ],
        out_specs=(part, part, part),
        scratch_shapes=[
            pltpu.VMEM((steps * block, D), F32), pltpu.VMEM((4, S, D), BF), pltpu.VMEM((S, D), F32),
            pltpu.SemaphoreType.DMA((4,)),
        ],
        compiler_params=pltpu.CompilerParams(vmem_limit_bytes=60_000_000),
    )(ids, ge, factor, w, m, v)


def local(
    sizes,
    token_ids,
    lengths,
    slot_order,
    pair_labels,
    embedding,
    attend_weight,
    attention_output_matrix,
    gate_up,
    contract_kernel,
    norm_params,
    embedding_first,
    embedding_second,
    attend_first,
    attend_second,
    output_first,
    output_second,
    gate_up_first,
    gate_up_second,
    down_first,
    down_second,
    norm_first,
    norm_second,
):
    NR, NF, S, D, rows = sizes
    nr = D // NF
    f = lax.axis_index("fsdp")
    N = NR * NF
    positions = jnp.arange(S)
    angles = (
        positions.astype(F32)[:, None]
        * (1000.0 ** (-2.0 * jnp.arange(HD // 2).astype(F32) / HD))[None, :]
    )
    cosine, sine = jnp.tile(jnp.cos(angles), (1, 128 * 2 // HD)), jnp.tile(jnp.sin(angles), (1, 128 * 2 // HD))
    ids, ffn, att, norms, stats, lists, ge = run_step(
        sizes,
        lengths,
        token_ids,
        norm_params,
        slot_order.reshape(1, N),
        pair_labels.reshape(1, N),
        cosine,
        sine,
        attend_weight,
        attention_output_matrix,
        gate_up,
        contract_kernel,
        embedding,
    )
    loss_value, grad_norm = stats[0, 0], stats[1, 0]
    if rows % CHUNK == 0:
        norm_next, *rest = split_three(
            finish(
                sizes, lists, ge, ffn, att, norms, stats, (norm_params, norm_first, norm_second),
                (
                    (embedding, embedding_first, embedding_second),
                    (attend_weight, attend_first, attend_second),
                    (attention_output_matrix, output_first, output_second),
                    (gate_up, gate_up_first, gate_up_second),
                    (contract_kernel, down_first, down_second),
                ),
            )
        )
        return (loss_value, grad_norm, *(item for state in rest for item in state), *norm_next)
    factor = jnp.minimum(1.0, clip_level / (grad_norm + 1e-06))
    factor_tile = jnp.broadcast_to(factor, (8, 128))
    emb_next = update_table(sizes, ids, ge, factor_tile, embedding, embedding_first, embedding_second)
    fin = ffn.reshape(TP, 3, nr, D)
    grad_attend = att[:3].transpose(1, 0, 2).reshape(nr, 3 * D).astype(F32)
    grad_output = att[3].astype(F32)
    grad_hidden = (
        fin[:, :2].reshape(TP, 2, nr, NF, nr).transpose(2, 1, 3, 0, 4).reshape(nr, 8 * D).astype(F32)
    )
    grad_down = fin[:, 2].reshape(TP * nr, D).astype(F32)
    grad_norms = lax.dynamic_slice(norms, (0, f * nr), (6, nr))
    att_next = adamw(attend_weight, grad_attend * factor, attend_first, attend_second, learn_rate)
    out_next = adamw(
        attention_output_matrix, grad_output * factor, output_first, output_second, learn_rate
    )
    gate_next = adamw(gate_up, grad_hidden * factor, gate_up_first, gate_up_second, learn_rate)
    down_next = adamw(contract_kernel, grad_down * factor, down_first, down_second, learn_rate)
    norm_next = adamw(norm_params, grad_norms * factor, norm_first, norm_second, norm_rate)
    return (
        loss_value, grad_norm, *emb_next, *att_next, *out_next, *gate_next, *down_next, *norm_next
    )


def split_three(flat):
    return [flat[i : i + 3] for i in range(0, len(flat), 3)]


def solution(mesh):
    NR, NF = mesh.shape["rep"], mesh.shape["fsdp"]
    rows_spec, cols_spec = P("fsdp", None), P(None, "fsdp")

    def step(*args):
        S, D, rows = args[0].shape[1], args[4].shape[1], args[4].shape[0] // NF
        run = jax.shard_map(
            functools.partial(local, (NR, NF, S, D, rows)),
            mesh=mesh,
            in_specs=(P(("rep", "fsdp"), None), P(("rep", "fsdp")), P(), P())
            + (rows_spec,) * 5 + (cols_spec,) + (rows_spec,) * 10 + (cols_spec,) * 2,
            out_specs=(P(), P()) + (rows_spec,) * 15 + (cols_spec,) * 3,
            check_vma=False,
        )
        return run(*args)

    return step
```

```python
import functools
import types

import jax
import jax.numpy as jnp
from jax import lax
from jax.experimental import pallas as pl
from jax.experimental.pallas import tpu as pltpu
from jax.sharding import PartitionSpec as P

H = 12
HD = 64
STEP = 4
TP = 4
MESH = pl.DeviceIdType.MESH
BF = jnp.bfloat16
F32 = jnp.float32

logit_divisor = 0.05
clip_level = 0.001
learn_rate = 0.02
norm_rate = 0.3
weight_decay = 0.01
beta_first = 0.5
beta_second = 0.75
adam_floor = 1e-08


def dot(a, b):
    return lax.dot_general(a, b, (((1,), (0,)), ((), ())), preferred_element_type=F32)


def dot_nt(a, b):
    return lax.dot_general(a, b, (((1,), (1,)), ((), ())), preferred_element_type=F32)


def dot_tn(a, b):
    return lax.dot_general(a, b, (((0,), (0,)), ((), ())), preferred_element_type=F32)


def layer_norm(values, gain, shift):
    centred = values - jnp.mean(values, axis=-1, keepdims=True)
    inverse = lax.rsqrt(jnp.mean(centred * centred, axis=-1, keepdims=True) + 1e-06)
    normed = centred * inverse
    return normed * gain + shift, normed, inverse


def norm_back(upstream, normed, inverse, gain):
    scaled = upstream * gain
    inner = (
        scaled
        - jnp.mean(scaled, axis=-1, keepdims=True)
        - normed * jnp.mean(scaled * normed, axis=-1, keepdims=True)
    )
    return (
        inner * inverse,
        jnp.sum(upstream * normed, axis=0, keepdims=True),
        jnp.sum(upstream, axis=0, keepdims=True),
    )


def step_layout(sizes):
    NR, NF, S, D, rows = sizes
    NZ, NG = NF // 2, NR // TP
    N, nr = NR * NF, D // NF
    block = (S, D)
    buffers = dict(
        pool=((max(0 if rows % 8 else rows, 30 * S), D), F32),
        table=((rows, D) if rows % 8 else (8, 128), F32),
        stage=(block, F32),
        W7=((7, D, D), BF),
        GW=((4, D, D), BF),
        EX=((4, NZ, S, D), BF),
        GNB=((NF, 8, 128), F32),
        H0B=(block, BF), QKV=((3, S, D), BF), ATT=(block, BF), PS=((D // HD, S, S), F32),
        H1=((TP, S, D), BF), MIX=((TP, S, D), BF), DF=((TP, S, D), BF), DG=((2, TP, S, D), BF),
        LX=((TP, S, D), BF), RX=((TP, S, D), BF), DQB=((3, S, D), BF), DB=((3, S, D), BF),
        INV=((3, S, 1), F32), YS=((2, S, D), BF), YR=((2, S, D), BF),
        PB=((N, 1, D), F32), PROW=((1, 1, D), F32), PM=((N, D), F32),
        XR=((4, NZ, nr, D), BF), ZS=((4, NZ, nr, D), BF), ZR=((4, NZ, nr, D), BF),
        NGS=((4, 8, D), F32), NGR=((3, 8, D), F32), NGZ=((NZ, 8, D), F32),
        SQ=((1, 1, 128), F32), SQS=((N, 1, 128), F32),
        PA=((nr, D), F32), PD=((nr, D), F32), PG=((nr, 8 * D), F32), IDF=((N, S), F32), RANK=((2, N, S), F32),
        FG=((NG, 4 * nr, D) if NG > 1 else (1, 16, 128), BF),
    )
    copies = dict(
        ids=1, gn=1, ex=NZ, ez=NZ, wu=3 * NZ, wd=3 * NZ, wx0=NZ, wx1=NZ, wx2=NZ, wx3=NZ, vu=2 * NZ, vd=2 * NZ, ay=NF, ac=2 * NF,
        h1=3, fc=2, fy=1, pool=1, df=3, bc=2, by=1, lx=TP, rx=TP, gx=4 * NZ, gz=4 * NZ, nc=1, ny=1, nx=1,
        nz=NZ, ff=3, fa=3, gg=2 * NG, sq=1, eu=2 * NZ, ed=2 * NZ, e0x=NZ, e0y=NF, e0c=2 * NF, e1x=2 * NZ, e1y=NZ,
        e1c=2 * NF, eg=NG,
    )
    return buffers, copies


def step_kernel(sizes, *refs):
    NR, NF, S, D, rows = sizes
    NX, NZ, NG = 2, NF // 2, NR // TP
    N, nr = NR * NF, D // NF
    HI = lax.Precision.HIGHEST
    buffers, copies = step_layout(sizes)
    given = (
        "length_in", "ids_in", "gn_in", "order_in", "labels_in", "cos_in", "sin_in", "qkv_in", "o_in", "gu_in", "down_in",
        "w_in", "ids_out", "ff_out", "fa_out", "ng_out", "stats_out", "list_out", "ge_out",
    )
    v = types.SimpleNamespace(**dict(zip((*given, *buffers, "sids", "ssem", "rsem", "lsem"), refs, strict=True)))
    pool, W7, GW, DB, DQB, QKV = v.pool, v.W7, v.GW, v.DB, v.DQB, v.QKV
    ssem, rsem, lsem, ids_out, ge_out = v.ssem, v.rsem, v.lsem, v.ids_out, v.ge_out
    r = lax.axis_index("rep")
    f = lax.axis_index("fsdp")
    d = r * NF + f
    z, x = lax.div(f, NX), lax.rem(f, NX)
    g, t = lax.div(r, TP), lax.rem(r, TP)
    y, c = lax.div(t, 2), lax.rem(t, 2)
    ty = (1 - y) * 2 + c
    tc = y * 2 + 1 - c
    tyc = (1 - y) * 2 + 1 - c
    dev_x = (r, z * NX + 1 - x)
    dev_y = (g * TP + ty, f)
    dev_c = (g * TP + tc, f)

    GATE, UP, PT, PT2 = 0, 4 * S, 8 * S, 12 * S
    CR, CR2 = 16 * S, 18 * S
    H0F, H1F, HAT, DS2, DS1, DQ = 20 * S, 21 * S, 22 * S, 25 * S, 26 * S, 27 * S

    def blk(offset, index=0):
        return pl.ds(pl.multiple_of(offset + index * S, 128), S)

    sem_at, used = {}, 0
    for name, many in copies.items():
        sem_at[name] = used
        used += many
    later = []

    def copy(name, index, src, dst, dev, landing=None):
        base = sem_at[name]
        return pltpu.make_async_remote_copy(
            src_ref=src, dst_ref=dst, send_sem=ssem.at[base + index],
            recv_sem=rsem.at[base + (index if landing is None else landing)],
            device_id=dev, device_id_type=MESH,
        )

    def send(name, index, src, dst, dev, only=None, landing=None):
        def start():
            copy(name, index, src, dst, dev, landing).start()

        def finish():
            copy(name, index, src, dst, dev, landing).wait_send()

        if only is None:
            start()
            later.append(finish)
        else:
            pl.when(only)(start)
            later.append(lambda: pl.when(only)(finish))

    def arrive(name, index, dst, only=None):
        def wait():
            pltpu.make_async_copy(dst, dst, rsem.at[sem_at[name] + index]).wait()

        if only is None:
            wait()
        else:
            pl.when(only)(wait)

    def spread(name, src, dst):
        base = sem_at[name]

        def one(k, carry):
            to = lax.rem(d + k, N)
            pltpu.make_async_remote_copy(
                src_ref=src, dst_ref=dst.at[d], send_sem=ssem.at[base], recv_sem=rsem.at[base],
                device_id=(lax.div(to, NF), lax.rem(to, NF)), device_id_type=MESH,
            ).start()
            return carry

        lax.fori_loop(1, N, one, 0)
        rest = dst.at[pl.ds(0, N - 1)]
        later.append(lambda: pltpu.make_async_copy(rest, rest, ssem.at[base]).wait())

    def gather_all(name, dst):
        rest = dst.at[pl.ds(0, N - 1)]
        pltpu.make_async_copy(rest, rest, rsem.at[sem_at[name]]).wait()

    def keep(only, ref, at, value):
        @pl.when(only)
        def _():
            ref[at] = value

    def load(src, dst, sem):
        done = pltpu.make_async_copy(src, dst, lsem.at[sem])
        done.start()
        return done

    table = v.table if rows % 8 else pool.at[pl.ds(0, rows)]
    slots = [t, 4, 5, 6]

    def wrow(index):
        return pl.ds(pl.multiple_of(index * nr, 16), nr)

    got_gate = load(v.gu_in, v.PG, 1)
    got_down = load(v.down_in.at[wrow(t)], v.PD, 2)

    @pl.when(t < 3)
    def _():
        load(v.qkv_in.at[:, pl.ds(pl.multiple_of(jnp.minimum(t, 2) * D, 128), D)], v.PA, 3)

    @pl.when(t == 3)
    def _():
        load(v.o_in, v.PA, 3)

    length = v.length_in[0]
    ids_out[d, :, pl.ds(0, S)] = v.ids_in[...]
    ids_out[d, :, pl.ds(S, S)] = jnp.zeros((1, S), jnp.int32) + length
    v.GNB[f] = jnp.zeros((8, 128), F32)
    v.GNB[f, 0:6, 0:nr] = v.gn_in[...].astype(BF).astype(F32)
    barrier = pltpu.get_barrier_semaphore()

    def greet(k, carry):
        to = lax.rem(d + k, N)
        pl.semaphore_signal(
            barrier, inc=1, device_id=(lax.div(to, NF), lax.rem(to, NF)), device_id_type=MESH
        )
        return carry

    lax.fori_loop(1, N, greet, 0)
    pltpu.make_async_copy(v.o_in, v.PA, lsem.at[3]).wait()
    W7[t, wrow(f), :] = v.PA[...].astype(BF)
    got_down.wait()
    W7[6, wrow(f), :] = v.PD[...].astype(BF)
    got_gate.wait()
    got_table = load(v.w_in, table, 0)
    quarter, span = D // TP, D // 3
    unit_row = lax.broadcasted_iota(jnp.int32, (D, span), 0)
    unit_col = lax.broadcasted_iota(jnp.int32, (D, span), 1)
    unit_group = lax.div(unit_row, nr)
    unit_at = lax.div(unit_group, TP) * nr + (unit_row - unit_group * nr)
    unit_mine = lax.rem(unit_group, TP) == t
    tiles = [jnp.zeros((2 * nr, 128), F32) for _ in range(D // 128)]
    for b in range(TP):
        first = quarter * b // 128 * 128
        choose = unit_mine & (unit_at + (quarter * b - first) == unit_col)
        both = jnp.concatenate(
            [v.PG[:, pl.ds(b * D, D)], v.PG[:, pl.ds((TP + b) * D, D)]], axis=0
        ).astype(BF)
        found = dot(both, jnp.where(choose, 1.0, 0.0).astype(BF))
        for i in range(span // 128):
            tiles[first // 128 + i] = tiles[first // 128 + i] + found[:, i * 128 : (i + 1) * 128]
    hidden = jnp.concatenate(tiles, axis=1).astype(BF)
    W7[4, wrow(f), :] = hidden[:nr]
    W7[5, wrow(f), :] = hidden[nr:]
    pl.semaphore_wait(barrier, N - 1)

    spread("ids", ids_out.at[d], ids_out)

    def piece(m, origin_z, origin_x):
        return W7.at[slots[m], wrow(origin_z * NX + origin_x)]

    def up_to(m, origin, only, which):
        here = piece(m, origin, which)
        if m < 3:
            send("wu", m * NZ + origin, here, here, (r, f + NX), only)
        else:
            send("vu", which * NZ + origin, here, here, (r, f + NX), only)

    def down_to(m, origin, only, which):
        here = piece(m, origin, which)
        if m < 3:
            send("wd", m * NZ + origin, here, here, (r, f - NX), only)
        else:
            send("vd", which * NZ + origin, here, here, (r, f - NX), only)

    def across(m, origin, only=None):
        here = piece(m, origin, x)
        send(f"wx{m}", origin, here, here, dev_x, only)

    def publish(index, only=None):
        here = W7.at[t, wrow(index)]
        send("ay", index, here, here, dev_y, only)
        send("ac", index, here, here, dev_c, only)

    def own_pieces(m):
        up_to(m, z, z + 1 < NZ, x)
        down_to(m, z, z >= 1, x)
        across(m, z)

    def relay(m, k):
        low, high = z - k, z + k
        below, above = jnp.maximum(low, 0), jnp.minimum(high, NZ - 1)
        for which in (x,) if m < 3 else (x, 1 - x):
            first = m * NZ if m < 3 else which * NZ
            arrive("wu" if m < 3 else "vu", first + below, piece(m, below, which), low >= 0)
            up_to(m, below, (low >= 0) & (z + 1 < NZ), which)
            if m < 3:
                across(m, below, low >= 0)
            if m == 0:
                publish(below * NX + x, low >= 0)
            arrive("wd" if m < 3 else "vd", first + above, piece(m, above, which), high < NZ)
            down_to(m, above, (high < NZ) & (z >= 1), which)
            if m < 3:
                across(m, above, high < NZ)
            if m == 0:
                publish(above * NX + x, high < NZ)

    own_pieces(0)
    publish(f)
    base_gn = sem_at["gn"]

    def gn_one(k, carry):
        pltpu.make_async_remote_copy(
            src_ref=v.GNB.at[f], dst_ref=v.GNB.at[f], send_sem=ssem.at[base_gn], recv_sem=rsem.at[base_gn],
            device_id=(r, lax.rem(f + k, NF)), device_id_type=MESH,
        ).start()
        return carry

    lax.fori_loop(1, NF, gn_one, 0)
    gn_rest = v.GNB.at[pl.ds(0, NF - 1)]
    later.append(lambda: pltpu.make_async_copy(gn_rest, gn_rest, ssem.at[base_gn]).wait())
    for m in (1, 2, 3):
        own_pieces(m)

    gather_all("ids", ids_out)
    got_sids = load(ids_out.at[pl.ds(pl.multiple_of(r * NF, NF), NF)], v.sids, 5)
    got_sids.wait()
    got_table.wait()
    start_row = f * rows
    EXS, EXO, EXR, EZR = (v.EX.at[i] for i in range(4))

    def rows_of(i, other):
        owner = i * NX + other

        def token(j, inner):
            wanted = v.sids[owner, 0, j] - start_row
            inside = (wanted >= 0) & (wanted < rows)
            row = table[pl.ds(jnp.clip(wanted, 0, rows - 1), 1), :]
            v.stage[pl.ds(j, 1), :] = jnp.where(inside, row, 0.0)
            return inner

        lax.fori_loop(0, S, token, 0, unroll=8)
        return v.stage[...].astype(BF)

    steps = [(m, k) for k in range(1, NZ) for m in (0, 1, 2, 3)]
    jobs = [(i, True) for i in range(NZ)] + [(i, False) for i in range(NZ)]
    at_step = 0
    for number, (i, away) in enumerate(jobs):
        if away:
            EXS[i] = rows_of(i, 1 - x)
            send("ex", i, EXS.at[i], EXR.at[i], dev_x)
        else:
            EXO[i] = rows_of(i, x)
        if number == 1:
            arrive("wx3", z, piece(3, z, 1 - x))
            up_to(3, z, z + 1 < NZ, 1 - x)
            down_to(3, z, z >= 1, 1 - x)
        while at_step < len(steps) * (number + 1) // len(jobs):
            relay(*steps[at_step])
            at_step += 1

    for i in range(NZ):
        arrive("ex", i, EXR.at[i])
        total = EXO[i] + EXR[i]
        EXO[i] = total
        keep(z == i, EZR, i, total)
        send("ez", i, EXO.at[i], EZR.at[z], (r, i * NX + x), z != i, z)
    while at_step < len(steps):
        relay(*steps[at_step])
        at_step += 1

    for i in range(NZ):
        arrive("wx0", i, piece(0, i, 1 - x))
        publish(i * NX + 1 - x)
    for i in range(NF):
        there = W7.at[ty, wrow(i)]
        arrive("ay", i, there)
        send("ac", NF + i, there, there, dev_c)

    arrive("gn", 0, gn_rest)
    tiles = jnp.concatenate([v.GNB[i] for i in range(NF)], axis=1).astype(BF)
    at_row = lax.broadcasted_iota(jnp.int32, (NF * 128, D), 0)
    at_col = lax.broadcasted_iota(jnp.int32, (NF * 128, D), 1)
    lane = lax.bitwise_and(at_row, 127)
    pick = (lane < nr) & (lax.shift_right_logical(at_row, 7) * nr + lane == at_col)
    gains = dot(tiles, jnp.where(pick, 1.0, 0.0).astype(BF))
    gain = [gains[i : i + 1] for i in range(6)]

    for i in range(NZ):
        pl.when(z != i)(functools.partial(arrive, "ez", i, EZR.at[i]))
    embedded = EZR[0].astype(F32)
    for i in range(1, NZ):
        embedded = embedded + EZR[i].astype(F32)
    normed, hat, inverse = layer_norm(embedded, gain[0], gain[1])
    pool[blk(H0F), :] = normed
    pool[blk(HAT, 0), :] = hat
    v.INV[0] = inverse
    v.H0B[...] = normed.astype(BF)

    def to_rank(name, which, src, buffer):
        send(name, which, src, buffer.at[t], (g * TP + which, f), t != which, t)
        keep(t == which, buffer, which, src[...])


    for i in range(NF):
        arrive("ac", i, W7.at[tc, wrow(i)])
    for i in range(NF):
        arrive("ac", NF + i, W7.at[tyc, wrow(i)])
    tables = [jnp.concatenate([ref[...]] * (D // 128), axis=1) for ref in (v.cos_in, v.sin_in)]
    in_half = lax.bitwise_and(lax.broadcasted_iota(jnp.int32, (S, D), 1), HD - 1) < HD // 2

    def turn(values, sign):
        partner = jnp.where(
            in_half, pltpu.roll(values, D - HD // 2, 1), pltpu.roll(values, HD // 2, 1)
        )
        signed = jnp.where(in_half, -sign, sign) * tables[1]
        return values * tables[0] + partner * signed

    for j in range(3):
        projected = dot(v.H0B[...], W7[j])
        QKV[j] = (turn(projected, 1.0) if j < 2 else projected).astype(BF)
    allowed = lax.broadcasted_iota(jnp.int32, (1, S), 1) < length
    scaling = HD ** (-0.5)
    first_half = lax.broadcasted_iota(jnp.int32, (S, 128), 1) < HD

    def half(values, which):
        keep = first_half if which == 0 else jnp.logical_not(first_half)
        return jnp.where(keep, values, jnp.zeros_like(values))

    def attend(p, carry):
        lanes = pl.ds(pl.multiple_of(p * 128, 128), 128)
        query, keys, values = QKV[0, :, lanes], QKV[1, :, lanes], QKV[2, :, lanes]
        result = jnp.zeros((S, 128), F32)
        for which in range(2):
            scores = dot_nt(query, half(keys, which)) * scaling
            scores = jnp.where(allowed, scores, -1000000000.0)
            raised = jnp.exp(scores - jnp.max(scores, axis=-1, keepdims=True))
            chances = raised / jnp.sum(raised, axis=-1, keepdims=True)
            v.PS[2 * p + which] = chances
            result = result + dot(chances.astype(BF), half(values, which))
        v.ATT[:, lanes] = result.astype(BF)
        return carry

    lax.fori_loop(0, D // 128, attend, 0)
    branch = dot(v.ATT[...], W7[3])
    normed, hat, inverse = layer_norm(pool[blk(H0F), :] + branch, gain[2], gain[3])
    pool[blk(H1F), :] = normed
    pool[blk(HAT, 1), :] = hat
    v.INV[1] = inverse
    v.H1[t] = normed.astype(BF)

    def share(name, buffer):
        send(name, 0, buffer.at[t], buffer.at[t], dev_y)
        send(name, 1, buffer.at[t], buffer.at[t], dev_c)
        arrive(name, 0, buffer.at[ty])
        send(name, 2, buffer.at[ty], buffer.at[ty], dev_c)
        arrive(name, 1, buffer.at[tc])
        arrive(name, 2, buffer.at[tyc])

    def reduce(names, offset, landing, which):
        for i in range(2):
            send(names[0], i, pool.at[blk(offset, i * 2 + 1 - c)], pool.at[blk(landing, i)], dev_c)
        for i in range(2):
            arrive(names[0], i, pool.at[blk(landing, i)])
        away = pool[blk(offset, (1 - y) * 2 + c), :] + pool[blk(landing, 1 - y), :]
        v.YS[which] = away.astype(BF)
        send(names[1], 0, v.YS.at[which], v.YR.at[which], dev_y)
        mine = pool[blk(offset, t), :] + pool[blk(landing, y), :]
        arrive(names[1], 0, v.YR.at[which])
        return mine + v.YR[which].astype(F32)

    share("h1", v.H1)
    for m in range(1, 3):
        for i in range(NZ):
            arrive(f"wx{m}", i, piece(m, i, 1 - x))

    def forward(b, carry):
        gate, up = dot(v.H1[b], W7[4]), dot(v.H1[b], W7[5])
        pool[blk(GATE, b), :] = gate
        pool[blk(UP, b), :] = up
        mixed = (gate / (1.0 + jnp.exp(-gate)) * up).astype(BF)
        v.MIX[b] = mixed
        pool[blk(PT, b), :] = dot(mixed, W7[6])
        return carry

    lax.fori_loop(0, TP, forward, 0)
    feed = reduce(("fc", "fy"), PT, CR, 0)
    for which in range(3):
        to_rank("lx", which, v.H0B, v.LX)
    to_rank("lx", 3, v.ATT, v.LX)
    normed, hat, inverse = layer_norm(pool[blk(H1F), :] + feed, gain[4], gain[5])
    pool[blk(HAT, 2), :] = hat
    v.INV[2] = inverse
    present = jnp.where(lax.broadcasted_iota(jnp.int32, (S, 1), 0) < length, 1.0, 0.0)
    share_of = length.astype(F32)
    v.PROW[0] = jnp.sum(normed * present, axis=0, keepdims=True) / share_of

    spread("pool", v.PROW.at[0], v.PB)
    v.PB[d] = v.PROW[0]
    gather_all("pool", v.PB)
    for i in range(N):
        v.PM[pl.ds(i, 1), :] = v.PB[i]
    pooled = v.PM[...]
    wide = lax.broadcasted_iota(jnp.int32, (N, D), 1)
    row_at = lax.broadcasted_iota(jnp.int32, (N, N), 0)
    col_at = lax.broadcasted_iota(jnp.int32, (N, N), 1)
    order, labels = v.order_in[...].astype(F32), v.labels_in[...].astype(F32)

    def column(row):
        return jnp.sum(jnp.where(row_at == col_at, row, 0.0), axis=1, keepdims=True)

    slot_has = jnp.where(column(order) == col_at.astype(F32), 1.0, 0.0).astype(BF)
    label_is = jnp.where(column(labels) == order, 1.0, 0.0).astype(BF)
    paired = dot(slot_has, label_is)
    loss_value = jnp.zeros((1, 1), F32)
    d_pooled = jnp.zeros((N, D), F32)
    for width in (D // 12, D // 3, D):
        portion = jnp.where(wide < width, pooled, 0.0)
        inverse = lax.rsqrt(jnp.sum(portion * portion, axis=1, keepdims=True) + 1e-06)
        unit = portion * inverse
        similar = lax.dot_general(
            unit, unit, (((1,), (1,)), ((), ())), precision=HI, preferred_element_type=F32
        ) / logit_divisor
        similar = jnp.where(row_at == col_at, -1000000000.0, similar)
        row_max = jnp.max(similar, axis=1, keepdims=True)
        raised = jnp.exp(similar - row_max)
        total = jnp.sum(raised, axis=1, keepdims=True)
        target = jnp.sum(jnp.where(paired > 0.0, similar, 0.0), axis=1, keepdims=True)
        term = row_max + jnp.log(total) - target
        loss_value = loss_value + jnp.sum(term, axis=0, keepdims=True) / N
        col_max = jnp.max(similar, axis=0, keepdims=True)
        raised_t = jnp.exp(similar - col_max)
        turned = raised_t / jnp.sum(raised_t, axis=0, keepdims=True)
        d_similar = (raised / total + turned - 2.0 * paired) / (3.0 * N) / logit_divisor
        d_unit = lax.dot_general(
            d_similar, unit, (((1,), (0,)), ((), ())), precision=HI, preferred_element_type=F32
        )
        inner = jnp.sum(d_unit * unit, axis=1, keepdims=True)
        d_pooled = d_pooled + inverse * (d_unit - unit * inner)
    loss_value = loss_value / 3.0
    own_row = lax.broadcasted_iota(jnp.int32, (N, D), 0) == d
    d_mine = jnp.sum(jnp.where(own_row, d_pooled, 0.0), axis=0, keepdims=True)

    d_two = d_mine * present / share_of
    d_sum, d_gain_two, d_shift_two = norm_back(d_two, pool[blk(HAT, 2), :], v.INV[2], gain[4])
    pool[blk(DS2), :] = d_sum
    v.DF[t] = d_sum.astype(BF)
    share("df", v.DF)

    def back(b, carry):
        d_mixed = dot_nt(v.DF[b], W7[6])
        gate, up = pool[blk(GATE, b), :], pool[blk(UP, b), :]
        logistic = 1.0 / (1.0 + jnp.exp(-gate))
        d_gate = (d_mixed * up * (logistic * (1.0 + gate * (1.0 - logistic)))).astype(BF)
        d_up = (d_mixed * (gate * logistic)).astype(BF)
        v.DG[0, b] = d_gate
        v.DG[1, b] = d_up
        pool[blk(PT2, b), :] = dot_nt(d_gate, W7[4]) + dot_nt(d_up, W7[5])
        return carry

    TILE = 256

    def product(left, right, m):
        def tile(i, carry):
            at = pl.ds(pl.multiple_of(i * TILE, TILE), TILE)
            GW[m, at, :] = dot_tn(left(at), right()).astype(BF)
            return carry

        lax.fori_loop(0, D // TILE, tile, 0)

    def part(m, i, other):
        return GW.at[m, wrow(i * NX + other)]

    def give(m):
        for i in range(NZ):
            send("gx", m * NZ + i, part(m, i, 1 - x), v.XR.at[m, i], dev_x)

    def pass_on(m):
        for i in range(NZ):
            arrive("gx", m * NZ + i, v.XR.at[m, i])
            total = (part(m, i, x)[...].astype(F32) + v.XR[m, i].astype(F32)).astype(BF)
            v.ZS[m, i] = total
            keep(z == i, v.ZR, (m, i), total)
            send("gz", m * NZ + i, v.ZS.at[m, i], v.ZR.at[m, z], (r, i * NX + x), z != i, m * NZ + z)

    def product_rows(buffer):
        return lambda at: buffer[:, :, at].reshape(TP * S, TILE)

    product(product_rows(v.MIX), lambda: v.DF[...].reshape(TP * S, D), 3)
    give(3)
    lax.fori_loop(0, TP, back, 0)
    for i in range(2):
        send("bc", i, pool.at[blk(PT2, i * 2 + 1 - c)], pool.at[blk(CR2, i)], dev_c)
    product(product_rows(v.H1), lambda: v.DG[0].reshape(TP * S, D), 1)
    give(1)
    for i in range(2):
        arrive("bc", i, pool.at[blk(CR2, i)])
    away = pool[blk(PT2, (1 - y) * 2 + c), :] + pool[blk(CR2, 1 - y), :]
    v.YS[1] = away.astype(BF)
    send("by", 0, v.YS.at[1], v.YR.at[1], dev_y)
    product(product_rows(v.H1), lambda: v.DG[1].reshape(TP * S, D), 2)
    give(2)
    pass_on(3)
    mine = pool[blk(PT2, t), :] + pool[blk(CR2, y), :]
    arrive("by", 0, v.YR.at[1])
    d_one = pool[blk(DS2), :] + (mine + v.YR[1].astype(F32))

    d_sum, d_gain_one, d_shift_one = norm_back(d_one, pool[blk(HAT, 1), :], v.INV[1], gain[2])
    pool[blk(DS1), :] = d_sum
    DB[0] = d_sum.astype(BF)
    to_rank("rx", 3, DB.at[0], v.RX)
    DB[1] = dot_nt(DB[0], W7[3]).astype(BF)
    pass_on(1)

    def attend_back(p, carry):
        lanes = pl.ds(pl.multiple_of(p * 128, 128), 128)
        query, keys, values = QKV[0, :, lanes], QKV[1, :, lanes], QKV[2, :, lanes]
        grad = DB[1, :, lanes]
        d_query = jnp.zeros((S, 128), F32)
        d_keys = jnp.zeros((S, 128), F32)
        d_values = jnp.zeros((S, 128), F32)
        for which in range(2):
            chances = v.PS[2 * p + which]
            d_values = d_values + dot_tn(chances.astype(BF), half(grad, which))
            d_chances = dot_nt(grad, half(values, which))
            inner = jnp.sum(chances * d_chances, axis=-1, keepdims=True)
            d_scores = (chances * (d_chances - inner)).astype(BF)
            d_query = d_query + dot(d_scores, half(keys, which)) * scaling
            d_keys = d_keys + dot_tn(d_scores, half(query, which)) * scaling
        pool[blk(DQ, 0), lanes] = d_query
        pool[blk(DQ, 1), lanes] = d_keys
        DQB[2, :, lanes] = d_values.astype(BF)
        return carry

    lax.fori_loop(0, D // 128, attend_back, 0)
    for j in range(2):
        DQB[j] = turn(pool[blk(DQ, j), :], -1.0).astype(BF)

    for which in range(3):
        to_rank("rx", which, DQB.at[which], v.RX)
    d_zero = pool[blk(DS1), :]
    for j in range(3):
        d_zero = d_zero + dot_nt(DQB[j], W7[j])
    d_embedded, d_gain_zero, d_shift_zero = norm_back(d_zero, pool[blk(HAT, 0), :], v.INV[0], gain[0])
    DB[2] = d_embedded.astype(BF)

    got_own = load(DB.at[2], ge_out.at[d], 0)
    cut = D // 2
    cols = [pl.ds(0, cut), pl.ds(cut, D - cut)]

    def line(rep, which_x, order, i):
        return ge_out.at[rep * NF + i * NX + which_x, :, cols[order]]

    def all_of(rep, order):
        return ge_out.at[pl.ds(pl.multiple_of(rep * NF, NF), NF), :, cols[order]]

    def ge_up(order, origin, src, only):
        send("eu", order * NZ + origin, src, line(r, x, order, origin), (r, f + NX), only)

    def ge_down(order, origin, src, only):
        send("ed", order * NZ + origin, src, line(r, x, order, origin), (r, f - NX), only)

    ry, rc, ryc = g * TP + ty, g * TP + tc, g * TP + tyc

    def ge_line(order, i, only=None, src=None):
        here = line(r, x, order, i)
        src = here if src is None else src
        if order == 0:
            send("e0x", i, src, here, dev_x, only)
            send("e0y", i * NX + x, src, here, dev_y, only)
            send("e0c", i * NX + x, src, here, dev_c, only)
        else:
            send("e1y", i, src, here, dev_y, only)
            send("e1x", i, src, here, dev_x, only)
            send("e1c", i * NX + x, src, here, dev_c, only)

    def ge_second(i, only):
        here = line(r, 1 - x, 0, i)
        arrive("e0x", i, here, only)
        send("e0y", i * NX + 1 - x, here, here, dev_y, only)
        send("e0c", i * NX + 1 - x, here, here, dev_c, only)
        here = line(ry, x, 1, i)
        arrive("e1y", i, here, only)
        send("e1x", NZ + i, here, here, dev_x, only)
        send("e1c", NF + i * NX + x, here, here, dev_c, only)

    def ge_third(i, only):
        for which_x in (x, 1 - x):
            here = line(ry, which_x, 0, i)
            arrive("e0y", i * NX + which_x, here, only)
            send("e0c", NF + i * NX + which_x, here, here, dev_c, only)
        for which, rep in enumerate((r, ry)):
            here = line(rep, 1 - x, 1, i)
            arrive("e1x", which * NZ + i, here, only)
            send("e1c", which * NF + i * NX + 1 - x, here, here, dev_c, only)

    def at_distance(step, k):
        low, high = z - k, z + k
        step(jnp.maximum(low, 0), low >= 0)
        if k:
            step(jnp.minimum(high, NZ - 1), high < NZ)

    for order in range(2):
        own_cols = DB.at[2, :, cols[order]]
        ge_up(order, z, own_cols, z + 1 < NZ)
        ge_down(order, z, own_cols, z >= 1)
        ge_line(order, z, None, own_cols)

    def ge_relay(k):
        low, high = z - k, z + k
        below, above = jnp.maximum(low, 0), jnp.minimum(high, NZ - 1)
        for order in range(2):
            arrive("eu", order * NZ + below, line(r, x, order, below), low >= 0)
            ge_up(order, below, line(r, x, order, below), (low >= 0) & (z + 1 < NZ))
            ge_line(order, below, low >= 0)
            arrive("ed", order * NZ + above, line(r, x, order, above), high < NZ)
            ge_down(order, above, line(r, x, order, above), (high < NZ) & (z >= 1))
            ge_line(order, above, high < NZ)

    def own_lists():
        for i in range(N):
            v.IDF[pl.ds(i, 1), :] = ids_out[i, :, pl.ds(0, S)].astype(F32)
            v.PM[pl.ds(i, 1), pl.ds(0, S)] = ids_out[i, :, pl.ds(S, S)].astype(F32)
        local_row = v.IDF[...] - (f * rows).astype(F32)
        valid = lax.broadcasted_iota(jnp.int32, (N, S), 1).astype(F32) < v.PM[:, 0:S]
        mine = valid & (local_row >= 0.0) & (local_row < 1.0 * rows)
        marks = jnp.where(mine, 1.0, 0.0).astype(BF)
        before = lax.broadcasted_iota(jnp.int32, (S, S), 0) < lax.broadcasted_iota(jnp.int32, (S, S), 1)
        prefix = dot(marks, jnp.where(before, 1.0, 0.0).astype(BF))
        counts = jnp.zeros((N, S), F32) + jnp.sum(marks.astype(F32), axis=1, keepdims=True)
        offsets = dot(jnp.where(row_at > col_at, 1.0, 0.0).astype(BF), counts.astype(BF))
        place = prefix + offsets
        high = jnp.floor(place * (1.0 / S))
        v.RANK[0] = high
        v.RANK[1] = jnp.where(mine, place - high * S, -1.0)
        v.IDF[...] = jnp.where(mine, local_row, 0.0)
        slot_at = lax.broadcasted_iota(jnp.int32, (N, S), 0).astype(F32)
        low_at = lax.broadcasted_iota(jnp.int32, (S, S), 0).astype(F32)
        token_at = lax.broadcasted_iota(jnp.int32, (1, S), 1).astype(F32)

        def one(i, carry):
            at = pl.ds(i, 1)
            row = v.IDF[at, :]
            row_high = jnp.floor(row * (1.0 / 64))
            spot = v.RANK[0, at, :] == slot_at
            left = jnp.concatenate(
                [jnp.where(spot, item, 0.0) for item in (row_high, row - row_high * 64.0, token_at)], axis=0
            ).astype(BF)
            right = jnp.where(v.RANK[1, at, :] == low_at, 1.0, 0.0).astype(BF)
            return carry + dot_nt(left, right)

        found = lax.fori_loop(0, N, one, jnp.zeros((3 * N, S), F32))
        v.list_out[0] = (found[:N] * 64.0 + found[N : 2 * N]).astype(jnp.int32)
        v.list_out[1] = found[2 * N :].astype(jnp.int32)
        v.list_out[2] = offsets.astype(jnp.int32)
        v.list_out[3] = (offsets + counts).astype(jnp.int32)

    v.NGS[0] = jnp.concatenate(
        [d_gain_zero, d_shift_zero, d_gain_one, d_shift_one, d_gain_two, d_shift_two,
         jnp.zeros((2, D), F32)], axis=0)
    stages = (("nc", dev_c), ("ny", dev_y), ("nx", dev_x))

    def norm_send(i):
        send(stages[i][0], 0, v.NGS.at[i], v.NGR.at[i], stages[i][1])

    def norm_add(i):
        arrive(stages[i][0], 0, v.NGR.at[i])
        v.NGS[i + 1] = v.NGS[i] + v.NGR[i]

    def settle(m, out, at):
        for i in range(NZ):
            arrive("gz", m * NZ + i, v.ZR.at[m, i], z != i)
        total = v.ZR[m, 0].astype(F32)
        for i in range(1, NZ):
            total = total + v.ZR[m, i].astype(F32)
        out[t, at, :] = total.astype(BF)

    def group_sum(out, first, size):
        own = v.FG.at[g, pl.ds(first, size)]
        own[...] = out[t]
        for k in range(1, NG):
            other = lax.rem(g + k, NG)
            index = (0 if first else NG) + k
            send("gg", index, own, own, (other * TP + t, f), None, (0 if first else NG) + g)
        for k in range(1, NG):
            other = lax.rem(g + k, NG)
            arrive("gg", (0 if first else NG) + other, v.FG.at[other, pl.ds(first, size)])
        total = v.FG[0, pl.ds(first, size)].astype(F32)
        for k in range(1, NG):
            total = total + v.FG[k, pl.ds(first, size)].astype(F32)
        out[t] = total.astype(BF)

    def share_start(name, buffer):
        send(name, 0, buffer.at[t], buffer.at[t], dev_y)
        send(name, 1, buffer.at[t], buffer.at[t], dev_c)

    def share_pass(name, buffer):
        arrive(name, 0, buffer.at[ty])
        send(name, 2, buffer.at[ty], buffer.at[ty], dev_c)

    def share_end(name, buffer):
        arrive(name, 1, buffer.at[tc])
        arrive(name, 2, buffer.at[tyc])

    norm_send(0)
    pass_on(2)
    for which in range(TP):
        arrive("lx", which, v.LX.at[which], t != which)
        arrive("rx", which, v.RX.at[which], t != which)
    product(product_rows(v.LX), lambda: v.RX[...].reshape(TP * S, D), 0)
    give(0)
    norm_add(0)
    norm_send(1)
    got_own.wait()
    ge_relay(1)
    at_distance(ge_second, 0)
    settle(3, v.ff_out, pl.ds(2 * nr, nr))
    settle(1, v.ff_out, pl.ds(0, nr))
    norm_add(1)
    norm_send(2)
    settle(2, v.ff_out, pl.ds(nr, nr))
    if NG > 1:
        group_sum(v.ff_out, nr, 3 * nr)
    share_start("ff", v.ff_out)
    pass_on(0)
    for k in range(2, NZ):
        ge_relay(k)
        at_distance(ge_second, k - 1)
    at_distance(ge_second, NZ - 1)
    norm_add(2)
    for i in range(NZ):
        send("nz", i, v.NGS.at[3], v.NGZ.at[z], (r, i * NX + x), z != i, z)
        keep(z == i, v.NGZ, i, v.NGS[3])
    own = v.ff_out[t].astype(F32)
    squares = jnp.sum(own * own)
    settle(0, v.fa_out, pl.ds(0, nr))
    if NG > 1:
        group_sum(v.fa_out, 0, nr)
    share_start("fa", v.fa_out)
    own = v.fa_out[t].astype(F32)
    squares = squares + jnp.sum(own * own)
    squares = jnp.where(g == 0, squares, 0.0)
    own_lists()
    for k in range(NZ):
        at_distance(ge_third, k)
    for name, buffer in (("ff", v.ff_out), ("fa", v.fa_out)):
        share_pass(name, buffer)
    for i in range(NZ):
        arrive("nz", i, v.NGZ.at[i], z != i)
    total_norms = v.NGZ[0]
    for i in range(1, NZ):
        total_norms = total_norms + v.NGZ[i]
    for name, buffer in (("ff", v.ff_out), ("fa", v.fa_out)):
        share_end(name, buffer)
    for order, name in enumerate(("e0c", "e1c")):
        for which, rep in enumerate((rc, ryc)):
            for i in range(NF):
                arrive(name, which * NF + i, ge_out.at[rep * NF + i, :, cols[order]])
    if NG > 1:

        def group(which):
            return ge_out.at[pl.ds(pl.multiple_of(which * TP * NF, TP * NF), TP * NF)]

        for k in range(1, NG):
            other = lax.rem(g + k, NG)
            send("eg", k, group(g), group(g), (other * TP + t, f), None, g)
        for k in range(1, NG):
            other = lax.rem(g + k, NG)
            arrive("eg", other, group(other))

    def fetch(b):
        return pltpu.make_async_copy(
            ge_out.at[pl.ds(b * NZ, NZ)], v.EX.at[2 + lax.rem(b, 2)], lsem.at[1 + lax.rem(b, 2)]
        )

    fetch(0).start()
    same = lax.broadcasted_iota(jnp.int32, (S, S), 0) == lax.broadcasted_iota(jnp.int32, (S, S), 1)
    own_ids = jnp.sum(
        jnp.where(same, ids_out[d, :, pl.ds(0, S)].astype(F32), 0.0), axis=1, keepdims=True
    )

    def pairs_of(b, carry):
        pl.when(b + 1 < N // NZ)(lambda: fetch(b + 1).start())
        fetch(b).wait()
        for i in range(NZ):
            both = dot_nt(DB[2], v.EX[2 + lax.rem(b, 2), i])
            theirs = ids_out[b * NZ + i, :, pl.ds(0, S)].astype(F32)
            carry = carry + jnp.where(own_ids == theirs, both, 0.0)
        return carry

    both = lax.fori_loop(0, N // NZ, pairs_of, jnp.zeros((S, S), F32))
    squares = squares + jnp.sum(both)
    squares = squares + jnp.where(d == 0, jnp.sum(total_norms * total_norms), 0.0)
    v.SQ[0] = jnp.zeros((1, 128), F32) + squares
    spread("sq", v.SQ.at[0], v.SQS)
    v.SQS[d] = v.SQ[0]
    v.ng_out[...] = total_norms
    gather_all("sq", v.SQS)
    all_squares = v.SQS[0]
    for i in range(1, N):
        all_squares = all_squares + v.SQS[i]
    v.stats_out[...] = jnp.concatenate(
        [jnp.zeros((1, 128), F32) + loss_value, jnp.sqrt(all_squares), jnp.zeros((6, 128), F32)], axis=0
    )
    for finish in later:
        finish()


def run_step(sizes, *args):
    NR, NF, S, D, rows = sizes
    N, nr = NR * NF, D // NF
    vmem = pl.BlockSpec(memory_space=pltpu.VMEM)
    smem = pl.BlockSpec(memory_space=pltpu.SMEM)
    hbm = pl.BlockSpec(memory_space=pl.ANY)
    buffers, copies = step_layout(sizes)
    many = sum(copies.values())
    return pl.pallas_call(
        functools.partial(step_kernel, sizes),
        name="step",
        out_shape=(
            jax.ShapeDtypeStruct((N, 1, 2 * S), jnp.int32),
            jax.ShapeDtypeStruct((TP, 3 * nr, D), BF),
            jax.ShapeDtypeStruct((TP, nr, D), BF),
            jax.ShapeDtypeStruct((8, D), F32),
            jax.ShapeDtypeStruct((8, 128), F32),
            jax.ShapeDtypeStruct((4, N, S), jnp.int32),
            jax.ShapeDtypeStruct((N, S, D), BF),
        ),
        in_specs=[smem] + [vmem] * 6 + [hbm] * 5,
        out_specs=(vmem,) * 6 + (hbm,),
        scratch_shapes=[pltpu.VMEM(*item) for item in buffers.values()]
        + [
            pltpu.SMEM((NF, 1, 2 * S), jnp.int32), pltpu.SemaphoreType.DMA((many,)),
            pltpu.SemaphoreType.DMA((many,)), pltpu.SemaphoreType.DMA((8,)),
        ],
        compiler_params=pltpu.CompilerParams(
            collective_id=0, has_side_effects=True, vmem_limit_bytes=67_000_000
        ),
    )(*args)


def adamw(weight, grad, first, second, rate):
    first_new = beta_first * first + (1.0 - beta_first) * grad
    second_new = beta_second * second + (1.0 - beta_second) * grad * grad
    first_fix = 1.0 - beta_first**STEP
    second_fix = 1.0 - beta_second**STEP
    update = first_new / first_fix / (jnp.sqrt(second_new / second_fix) + adam_floor)
    return (weight - rate * (update + weight_decay * weight), first_new, second_new)


CHUNK, SLOTS = 424, 7


def finish_kernel(sizes, *refs):
    NR, NF, S, D, rows = sizes
    N, nr = NR * NF, D // NF
    names = ("lists", "ge", "ff", "fa", "norms", "stats", "pw", "pm", "pv") + tuple(
        f"{kind}{which}" for kind in "eaogd" for which in range(3)
    )
    results = ("qw", "qm", "qv") + tuple(f"{kind}{which}_new" for kind in "eaogd" for which in range(3))
    scratch = (
        "grads", "landing", "stage", "TB", "LA", "LO", "LG", "LD", "sems",
        "ins", "outs", "tin", "tout",
    )
    v = types.SimpleNamespace(**dict(zip((*names, *results, *scratch), refs, strict=True)))
    n_chunks = rows // CHUNK

    def fetch(s):
        return pltpu.make_async_copy(v.ge.at[s], v.landing.at[lax.rem(s, 4)], v.sems.at[lax.rem(s, 4)])

    for s in range(3):
        fetch(s).start()
    layers = (("a", v.LA), ("o", v.LO), ("d", v.LD), ("g", v.LG))

    def layer(index, inward):
        kind, buffer = layers[index]
        for which in range(3):
            if inward:
                yield pltpu.make_async_copy(
                    getattr(v, f"{kind}{which}"), buffer.at[which], v.ins.at[index * 3 + which]
                )
            else:
                yield pltpu.make_async_copy(
                    buffer.at[which], getattr(v, f"{kind}{which}_new"), v.outs.at[index * 3 + which]
                )

    def chunk(k, inward):
        at, slot = pl.ds(k * CHUNK, CHUNK), k % SLOTS
        for which in range(3):
            old, new = getattr(v, f"e{which}"), getattr(v, f"e{which}_new")
            if inward:
                yield pltpu.make_async_copy(old.at[at], v.TB.at[slot, which], v.tin.at[slot, which])
            else:
                yield pltpu.make_async_copy(v.TB.at[slot, which], new.at[at], v.tout.at[slot, which])

    for index in range(4):
        for item in layer(index, True):
            item.start()
    for k in range(min(SLOTS, n_chunks)):
        for item in chunk(k, True):
            item.start()

    factor = jnp.minimum(1.0, clip_level / (v.stats[1:2, 0:1] + 1e-06))

    def apply(buffer, at, grad):
        index = tuple(at)
        new = adamw(
            buffer[(0, *index)], grad * factor, buffer[(1, *index)], buffer[(2, *index)], learn_rate
        )
        for which in range(3):
            buffer[(which, *index)] = new[which]

    def finish_layer(index):
        for item in layer(index, False):
            item.start()

    whole = pl.ds(0, nr)
    for item in layer(0, True):
        item.wait()
    for q in range(3):
        apply(v.LA, (whole, pl.ds(q * D, D)), v.fa[q].astype(F32))
    finish_layer(0)
    for item in layer(1, True):
        item.wait()
    apply(v.LO, (whole, pl.ds(0, D)), v.fa[3].astype(F32))
    finish_layer(1)
    for item in layer(2, True):
        item.wait()

    def down(q, carry):
        at = pl.ds(pl.multiple_of(q * nr, 16), nr)
        apply(v.LD, (at, pl.ds(0, D)), v.ff[q, pl.ds(2 * nr, nr), :].astype(F32))
        return carry

    lax.fori_loop(0, TP, down, 0)
    finish_layer(2)
    for item in layer(3, True):
        item.wait()
    quarter, span = D // TP, 2 * D // 6
    at_row = lax.broadcasted_iota(jnp.int32, (span, D), 0)
    at_col = lax.broadcasted_iota(jnp.int32, (span, D), 1)
    group = lax.div(at_col, nr)
    unit = lax.div(group, TP) * nr + (at_col - group * nr)
    holder = lax.rem(group, TP)
    for b in range(TP):
        first = quarter * b // 128 * 128
        total = jnp.zeros((2 * nr, D), F32)
        for q in range(TP):
            pick = (at_row + (first - quarter * b) == unit) & (holder == q)
            total = total + dot(
                v.ff[q, pl.ds(0, 2 * nr), pl.ds(first, span)], jnp.where(pick, 1.0, 0.0).astype(BF)
            )
        apply(v.LG, (whole, pl.ds(b * D, D)), total[:nr])
        apply(v.LG, (whole, pl.ds((TP + b) * D, D)), total[nr:])
    finish_layer(3)
    at_row = lax.broadcasted_iota(jnp.int32, (D, 128), 0)
    at_col = lax.broadcasted_iota(jnp.int32, (D, 128), 1)
    pick = (at_row - lax.axis_index("fsdp") * nr == at_col) & (at_col < nr)
    mine = lax.dot_general(
        v.norms[...], jnp.where(pick, 1.0, 0.0), (((1,), (0,)), ((), ())),
        precision=lax.Precision.HIGHEST, preferred_element_type=F32,
    )
    v.qw[...], v.qm[...], v.qv[...] = adamw(
        v.pw[...], mine[:6, :nr] * factor, v.pm[...], v.pv[...], norm_rate
    )

    def clear(i, carry):
        v.grads[pl.ds(pl.multiple_of(i * CHUNK, 8), CHUNK), :] = jnp.zeros((CHUNK, D), F32)
        return carry

    lax.fori_loop(0, n_chunks, clear, 0)

    def sequence(s, carry):
        pl.when(s + 3 < N)(lambda: fetch(s + 3).start())
        fetch(s).wait()
        v.stage[...] = v.landing[lax.rem(s, 4)].astype(F32)

        def token(k, inner):
            high, low = lax.shift_right_logical(k, shift), lax.bitwise_and(k, S - 1)
            at = pl.ds(v.lists[0, high, low], 1)
            v.grads[at, :] = v.grads[at, :] + v.stage[pl.ds(v.lists[1, high, low], 1), :]
            return inner

        return lax.fori_loop(v.lists[2, s, 0], v.lists[3, s, 0], token, carry)

    shift = S.bit_length() - 1
    lax.fori_loop(0, N, sequence, 0)

    for k in range(n_chunks):
        for item in chunk(k, True):
            item.wait()
        slot = k % SLOTS

        def part(first, size, k=k, slot=slot):
            at = pl.ds(pl.multiple_of(k * CHUNK + first, 8), size)
            grad = v.grads[at, :]
            apply(v.TB.at[slot], (pl.ds(pl.multiple_of(first, 8), size), pl.ds(0, D)), grad)

        def tile(i, carry, part=part):
            part(i * 32, 32)
            return carry

        lax.fori_loop(0, CHUNK // 32, tile, 0)
        if CHUNK % 32:
            part(CHUNK // 32 * 32, CHUNK % 32)
        for item in chunk(k, False):
            item.start()
        if k >= 1 and k - 1 + SLOTS < n_chunks:
            for item in chunk(k - 1, False):
                item.wait()
            for item in chunk(k - 1 + SLOTS, True):
                item.start()
    for k in range(n_chunks):
        if k + SLOTS >= n_chunks or k == n_chunks - 1:
            for item in chunk(k, False):
                item.wait()
    for index in range(4):
        for item in layer(index, False):
            item.wait()


def finish(sizes, lists, ge, ff, fa, norms, stats, norm_state, states):
    NR, NF, S, D, rows = sizes
    N, nr = NR * NF, D // NF
    hbm = pl.BlockSpec(memory_space=pl.ANY)
    vmem = pl.BlockSpec(memory_space=pltpu.VMEM)
    smem = pl.BlockSpec(memory_space=pltpu.SMEM)
    flat = [item for state in states for item in state]
    shapes = [jax.ShapeDtypeStruct(item.shape, F32) for item in (*norm_state, *flat)]
    return pl.pallas_call(
        functools.partial(finish_kernel, sizes),
        name="finish",
        out_shape=tuple(shapes),
        in_specs=[smem, hbm] + [vmem] * 7 + [hbm] * 15,
        out_specs=(vmem,) * 3 + (hbm,) * 15,
        scratch_shapes=[
            pltpu.VMEM((rows, D), F32), pltpu.VMEM((4, S, D), BF), pltpu.VMEM((S, D), F32),
            pltpu.VMEM((SLOTS, 3, CHUNK, D), F32),
            pltpu.VMEM((3, nr, 3 * D), F32), pltpu.VMEM((3, nr, D), F32), pltpu.VMEM((3, nr, 8 * D), F32),
            pltpu.VMEM((3, 4 * nr, D), F32),
            pltpu.SemaphoreType.DMA((4,)), pltpu.SemaphoreType.DMA((12,)),
            pltpu.SemaphoreType.DMA((12,)), pltpu.SemaphoreType.DMA((SLOTS, 3)),
            pltpu.SemaphoreType.DMA((SLOTS, 3)),
        ],
        compiler_params=pltpu.CompilerParams(vmem_limit_bytes=62_000_000),
    )(lists, ge, ff, fa, norms, stats, *norm_state, *flat)


def table_kernel(sizes, ids, ge, factor, w, m, v, w_out, m_out, v_out, grads, landing, stage, sems):
    NR, NF, S, D, rows = sizes
    N = NR * NF
    step = pl.program_id(0)
    block = w.shape[0]

    @pl.when(step == 0)
    def _():
        start_row = lax.axis_index("fsdp") * rows

        def fetch(s):
            return pltpu.make_async_copy(ge.at[s], landing.at[lax.rem(s, 4)], sems.at[lax.rem(s, 4)])

        for s in range(3):
            fetch(s).start()

        def clear(i, carry):
            grads[pl.ds(pl.multiple_of(i * block, 8), block), :] = jnp.zeros((block, D), F32)
            return carry

        lax.fori_loop(0, grads.shape[0] // block, clear, 0)

        def sequence(s, carry):
            pl.when(s + 3 < N)(lambda: fetch(s + 3).start())
            fetch(s).wait()
            stage[...] = landing[lax.rem(s, 4)].astype(F32)

            def token(j, inner):
                wanted = ids[s, 0, j] - start_row

                @pl.when((wanted >= 0) & (wanted < rows))
                def _():
                    at = pl.ds(wanted, 1)
                    grads[at, :] = grads[at, :] + stage[pl.ds(j, 1), :]

                return inner

            return lax.fori_loop(0, S, token, carry)

        lax.fori_loop(0, N, sequence, 0)

    grad = grads[pl.ds(pl.multiple_of(step * block, 8), block), :] * factor[0:1, 0:1]
    w_out[...], m_out[...], v_out[...] = adamw(w[...], grad, m[...], v[...], learn_rate)


def update_table(sizes, ids, ge, factor, w, m, v):
    NR, NF, S, D, rows = sizes
    block = 424
    steps = pl.cdiv(rows, block)
    part = pl.BlockSpec((block, D), lambda i: (i, 0))
    return pl.pallas_call(
        functools.partial(table_kernel, sizes),
        name="table",
        grid=(steps,),
        out_shape=(jax.ShapeDtypeStruct((rows, D), F32),) * 3,
        in_specs=[
            pl.BlockSpec(memory_space=pltpu.SMEM), pl.BlockSpec(memory_space=pl.ANY),
            pl.BlockSpec((8, 128), lambda i: (0, 0)), part, part, part,
        ],
        out_specs=(part, part, part),
        scratch_shapes=[
            pltpu.VMEM((steps * block, D), F32), pltpu.VMEM((4, S, D), BF), pltpu.VMEM((S, D), F32),
            pltpu.SemaphoreType.DMA((4,)),
        ],
        compiler_params=pltpu.CompilerParams(vmem_limit_bytes=60_000_000),
    )(ids, ge, factor, w, m, v)


def local(
    sizes,
    token_ids,
    lengths,
    slot_order,
    pair_labels,
    embedding,
    attend_weight,
    attention_output_matrix,
    gate_up,
    contract_kernel,
    norm_params,
    embedding_first,
    embedding_second,
    attend_first,
    attend_second,
    output_first,
    output_second,
    gate_up_first,
    gate_up_second,
    down_first,
    down_second,
    norm_first,
    norm_second,
):
    NR, NF, S, D, rows = sizes
    nr = D // NF
    f = lax.axis_index("fsdp")
    N = NR * NF
    positions = jnp.arange(S)
    angles = (
        positions.astype(F32)[:, None]
        * (1000.0 ** (-2.0 * jnp.arange(HD // 2).astype(F32) / HD))[None, :]
    )
    cosine, sine = jnp.tile(jnp.cos(angles), (1, 128 * 2 // HD)), jnp.tile(jnp.sin(angles), (1, 128 * 2 // HD))
    ids, ffn, att, norms, stats, lists, ge = run_step(
        sizes,
        lengths,
        token_ids,
        norm_params,
        slot_order.reshape(1, N),
        pair_labels.reshape(1, N),
        cosine,
        sine,
        attend_weight,
        attention_output_matrix,
        gate_up,
        contract_kernel,
        embedding,
    )
    loss_value, grad_norm = stats[0, 0], stats[1, 0]
    if rows % CHUNK == 0:
        norm_next, *rest = split_three(
            finish(
                sizes, lists, ge, ffn, att, norms, stats, (norm_params, norm_first, norm_second),
                (
                    (embedding, embedding_first, embedding_second),
                    (attend_weight, attend_first, attend_second),
                    (attention_output_matrix, output_first, output_second),
                    (gate_up, gate_up_first, gate_up_second),
                    (contract_kernel, down_first, down_second),
                ),
            )
        )
        return (loss_value, grad_norm, *(item for state in rest for item in state), *norm_next)
    factor = jnp.minimum(1.0, clip_level / (grad_norm + 1e-06))
    factor_tile = jnp.broadcast_to(factor, (8, 128))
    emb_next = update_table(sizes, ids, ge, factor_tile, embedding, embedding_first, embedding_second)
    fin = ffn.reshape(TP, 3, nr, D)
    grad_attend = att[:3].transpose(1, 0, 2).reshape(nr, 3 * D).astype(F32)
    grad_output = att[3].astype(F32)
    grad_hidden = (
        fin[:, :2].reshape(TP, 2, nr, NF, nr).transpose(2, 1, 3, 0, 4).reshape(nr, 8 * D).astype(F32)
    )
    grad_down = fin[:, 2].reshape(TP * nr, D).astype(F32)
    grad_norms = lax.dynamic_slice(norms, (0, f * nr), (6, nr))
    att_next = adamw(attend_weight, grad_attend * factor, attend_first, attend_second, learn_rate)
    out_next = adamw(
        attention_output_matrix, grad_output * factor, output_first, output_second, learn_rate
    )
    gate_next = adamw(gate_up, grad_hidden * factor, gate_up_first, gate_up_second, learn_rate)
    down_next = adamw(contract_kernel, grad_down * factor, down_first, down_second, learn_rate)
    norm_next = adamw(norm_params, grad_norms * factor, norm_first, norm_second, norm_rate)
    return (
        loss_value, grad_norm, *emb_next, *att_next, *out_next, *gate_next, *down_next, *norm_next
    )


def split_three(flat):
    return [flat[i : i + 3] for i in range(0, len(flat), 3)]


def solution(mesh):
    NR, NF = mesh.shape["rep"], mesh.shape["fsdp"]
    rows_spec, cols_spec = P("fsdp", None), P(None, "fsdp")

    def step(*args):
        S, D, rows = args[0].shape[1], args[4].shape[1], args[4].shape[0] // NF
        run = jax.shard_map(
            functools.partial(local, (NR, NF, S, D, rows)),
            mesh=mesh,
            in_specs=(P(("rep", "fsdp"), None), P(("rep", "fsdp")), P(), P())
            + (rows_spec,) * 5 + (cols_spec,) + (rows_spec,) * 10 + (cols_spec,) * 2,
            out_specs=(P(), P()) + (rows_spec,) * 15 + (cols_spec,) * 3,
            check_vma=False,
        )
        return run(*args)

    return step
```

```python
import functools
import types

import jax
import jax.numpy as jnp
from jax import lax
from jax.experimental import pallas as pl
from jax.experimental.pallas import tpu as pltpu
from jax.sharding import PartitionSpec as P

H = 12
HD = 64
STEP = 4
TP = 4
MESH = pl.DeviceIdType.MESH
BF = jnp.bfloat16
F32 = jnp.float32

logit_divisor = 0.05
clip_level = 0.001
learn_rate = 0.02
norm_rate = 0.3
weight_decay = 0.01
beta_first = 0.5
beta_second = 0.75
adam_floor = 1e-08


def dot(a, b):
    return lax.dot_general(a, b, (((1,), (0,)), ((), ())), preferred_element_type=F32)


def dot_nt(a, b):
    return lax.dot_general(a, b, (((1,), (1,)), ((), ())), preferred_element_type=F32)


def dot_tn(a, b):
    return lax.dot_general(a, b, (((0,), (0,)), ((), ())), preferred_element_type=F32)


def layer_norm(values, gain, shift):
    centred = values - jnp.mean(values, axis=-1, keepdims=True)
    inverse = lax.rsqrt(jnp.mean(centred * centred, axis=-1, keepdims=True) + 1e-06)
    normed = centred * inverse
    return normed * gain + shift, normed, inverse


def norm_back(upstream, normed, inverse, gain):
    scaled = upstream * gain
    inner = (
        scaled
        - jnp.mean(scaled, axis=-1, keepdims=True)
        - normed * jnp.mean(scaled * normed, axis=-1, keepdims=True)
    )
    return (
        inner * inverse,
        jnp.sum(upstream * normed, axis=0, keepdims=True),
        jnp.sum(upstream, axis=0, keepdims=True),
    )


def step_layout(sizes):
    NR, NF, S, D, rows = sizes
    NZ, NG = NF // 2, NR // TP
    N, nr = NR * NF, D // NF
    block = (S, D)
    buffers = dict(
        pool=((max(0 if rows % 8 else rows, 30 * S), D), F32),
        table=((rows, D) if rows % 8 else (8, 128), F32),
        stage=(block, F32),
        W7=((7, D, D), BF),
        GW=((4, D, D), BF),
        EX=((4, NZ, S, D), BF),
        GNB=((NF, 8, 128), F32),
        H0B=(block, BF), QKV=((3, S, D), BF), ATT=(block, BF), PS=((D // HD, S, S), F32),
        H1=((TP, S, D), BF), MIX=((TP, S, D), BF), DF=((TP, S, D), BF), DG=((2, TP, S, D), BF),
        LX=((TP, S, D), BF), RX=((TP, S, D), BF), DQB=((3, S, D), BF), DB=((3, S, D), BF),
        INV=((3, S, 1), F32), YS=((2, S, D), BF), YR=((2, S, D), BF),
        PB=((N, 1, D), F32), PROW=((1, 1, D), F32), PM=((N, D), F32),
        XR=((4, NZ, nr, D), BF), ZS=((4, NZ, nr, D), BF), ZR=((4, NZ, nr, D), BF),
        NGS=((4, 8, D), F32), NGR=((3, 8, D), F32), NGZ=((NZ, 8, D), F32),
        SQ=((1, 1, 128), F32), SQS=((N, 1, 128), F32),
        PA=((nr, D), F32), PD=((nr, D), F32), PG=((nr, 8 * D), F32), IDF=((N, S), F32), RANK=((2, N, S), F32),
        FG=((NG, 4 * nr, D) if NG > 1 else (1, 16, 128), BF),
    )
    copies = dict(
        ids=1, gn=1, ex=NZ, ez=NZ, wu=3 * NZ, wd=3 * NZ, wx0=NZ, wx1=NZ, wx2=NZ, wx3=NZ, vu=2 * NZ, vd=2 * NZ, ay=NF, ac=2 * NF,
        h1=3, fc=2, fy=1, pool=1, df=3, bc=2, by=1, lx=TP, rx=TP, gx=4 * NZ, gz=4 * NZ, nc=1, ny=1, nx=1,
        nz=NZ, ff=3, fa=3, gg=2 * NG, sq=1, eu=2 * NZ, ed=2 * NZ, e0x=NZ, e0y=NF, e0c=2 * NF, e1x=2 * NZ, e1y=NZ,
        e1c=2 * NF, eg=NG,
    )
    return buffers, copies


def step_kernel(sizes, *refs):
    NR, NF, S, D, rows = sizes
    NX, NZ, NG = 2, NF // 2, NR // TP
    N, nr = NR * NF, D // NF
    HI = lax.Precision.HIGHEST
    buffers, copies = step_layout(sizes)
    given = (
        "length_in", "ids_in", "gn_in", "order_in", "labels_in", "cos_in", "sin_in", "qkv_in", "o_in", "gu_in", "down_in",
        "w_in", "ids_out", "ff_out", "fa_out", "ng_out", "stats_out", "list_out", "ge_out",
    )
    v = types.SimpleNamespace(**dict(zip((*given, *buffers, "sids", "ssem", "rsem", "lsem"), refs, strict=True)))
    pool, W7, GW, DB, DQB, QKV = v.pool, v.W7, v.GW, v.DB, v.DQB, v.QKV
    ssem, rsem, lsem, ids_out, ge_out = v.ssem, v.rsem, v.lsem, v.ids_out, v.ge_out
    r = lax.axis_index("rep")
    f = lax.axis_index("fsdp")
    d = r * NF + f
    z, x = lax.div(f, NX), lax.rem(f, NX)
    g, t = lax.div(r, TP), lax.rem(r, TP)
    y, c = lax.div(t, 2), lax.rem(t, 2)
    ty = (1 - y) * 2 + c
    tc = y * 2 + 1 - c
    tyc = (1 - y) * 2 + 1 - c
    dev_x = (r, z * NX + 1 - x)
    dev_y = (g * TP + ty, f)
    dev_c = (g * TP + tc, f)

    GATE, UP, PT, PT2 = 0, 4 * S, 8 * S, 12 * S
    CR, CR2 = 16 * S, 18 * S
    H0F, H1F, HAT, DS2, DS1, DQ = 20 * S, 21 * S, 22 * S, 25 * S, 26 * S, 27 * S

    def blk(offset, index=0):
        return pl.ds(pl.multiple_of(offset + index * S, 128), S)

    sem_at, used = {}, 0
    for name, many in copies.items():
        sem_at[name] = used
        used += many
    later = []

    def copy(name, index, src, dst, dev, landing=None):
        base = sem_at[name]
        return pltpu.make_async_remote_copy(
            src_ref=src, dst_ref=dst, send_sem=ssem.at[base + index],
            recv_sem=rsem.at[base + (index if landing is None else landing)],
            device_id=dev, device_id_type=MESH,
        )

    def send(name, index, src, dst, dev, only=None, landing=None):
        def start():
            copy(name, index, src, dst, dev, landing).start()

        def finish():
            copy(name, index, src, dst, dev, landing).wait_send()

        if only is None:
            start()
            later.append(finish)
        else:
            pl.when(only)(start)
            later.append(lambda: pl.when(only)(finish))

    def arrive(name, index, dst, only=None):
        def wait():
            pltpu.make_async_copy(dst, dst, rsem.at[sem_at[name] + index]).wait()

        if only is None:
            wait()
        else:
            pl.when(only)(wait)

    def spread(name, src, dst):
        base = sem_at[name]

        def one(k, carry):
            to = lax.rem(d + k, N)
            pltpu.make_async_remote_copy(
                src_ref=src, dst_ref=dst.at[d], send_sem=ssem.at[base], recv_sem=rsem.at[base],
                device_id=(lax.div(to, NF), lax.rem(to, NF)), device_id_type=MESH,
            ).start()
            return carry

        lax.fori_loop(1, N, one, 0)
        rest = dst.at[pl.ds(0, N - 1)]
        later.append(lambda: pltpu.make_async_copy(rest, rest, ssem.at[base]).wait())

    def gather_all(name, dst):
        rest = dst.at[pl.ds(0, N - 1)]
        pltpu.make_async_copy(rest, rest, rsem.at[sem_at[name]]).wait()

    def keep(only, ref, at, value):
        @pl.when(only)
        def _():
            ref[at] = value

    def load(src, dst, sem):
        done = pltpu.make_async_copy(src, dst, lsem.at[sem])
        done.start()
        return done

    table = v.table if rows % 8 else pool.at[pl.ds(0, rows)]
    slots = [t, 4, 5, 6]

    def wrow(index):
        return pl.ds(pl.multiple_of(index * nr, 16), nr)

    got_gate = load(v.gu_in, v.PG, 1)
    got_down = load(v.down_in.at[wrow(t)], v.PD, 2)

    @pl.when(t < 3)
    def _():
        load(v.qkv_in.at[:, pl.ds(pl.multiple_of(jnp.minimum(t, 2) * D, 128), D)], v.PA, 3)

    @pl.when(t == 3)
    def _():
        load(v.o_in, v.PA, 3)

    length = v.length_in[0]
    ids_out[d, :, pl.ds(0, S)] = v.ids_in[...]
    ids_out[d, :, pl.ds(S, S)] = jnp.zeros((1, S), jnp.int32) + length
    v.GNB[f] = jnp.zeros((8, 128), F32)
    v.GNB[f, 0:6, 0:nr] = v.gn_in[...].astype(BF).astype(F32)
    barrier = pltpu.get_barrier_semaphore()

    def greet(k, carry):
        to = lax.rem(d + k, N)
        pl.semaphore_signal(
            barrier, inc=1, device_id=(lax.div(to, NF), lax.rem(to, NF)), device_id_type=MESH
        )
        return carry

    lax.fori_loop(1, N, greet, 0)
    pltpu.make_async_copy(v.o_in, v.PA, lsem.at[3]).wait()
    W7[t, wrow(f), :] = v.PA[...].astype(BF)
    got_down.wait()
    W7[6, wrow(f), :] = v.PD[...].astype(BF)
    got_gate.wait()
    got_table = load(v.w_in, table, 0)
    quarter, span = D // TP, D // 3
    unit_row = lax.broadcasted_iota(jnp.int32, (D, span), 0)
    unit_col = lax.broadcasted_iota(jnp.int32, (D, span), 1)
    unit_group = lax.div(unit_row, nr)
    unit_at = lax.div(unit_group, TP) * nr + (unit_row - unit_group * nr)
    unit_mine = lax.rem(unit_group, TP) == t
    tiles = [jnp.zeros((2 * nr, 128), F32) for _ in range(D // 128)]
    for b in range(TP):
        first = quarter * b // 128 * 128
        choose = unit_mine & (unit_at + (quarter * b - first) == unit_col)
        both = jnp.concatenate(
            [v.PG[:, pl.ds(b * D, D)], v.PG[:, pl.ds((TP + b) * D, D)]], axis=0
        ).astype(BF)
        found = dot(both, jnp.where(choose, 1.0, 0.0).astype(BF))
        for i in range(span // 128):
            tiles[first // 128 + i] = tiles[first // 128 + i] + found[:, i * 128 : (i + 1) * 128]
    hidden = jnp.concatenate(tiles, axis=1).astype(BF)
    W7[4, wrow(f), :] = hidden[:nr]
    W7[5, wrow(f), :] = hidden[nr:]
    pl.semaphore_wait(barrier, N - 1)

    spread("ids", ids_out.at[d], ids_out)

    def piece(m, origin_z, origin_x):
        return W7.at[slots[m], wrow(origin_z * NX + origin_x)]

    def up_to(m, origin, only, which):
        here = piece(m, origin, which)
        if m < 3:
            send("wu", m * NZ + origin, here, here, (r, f + NX), only)
        else:
            send("vu", which * NZ + origin, here, here, (r, f + NX), only)

    def down_to(m, origin, only, which):
        here = piece(m, origin, which)
        if m < 3:
            send("wd", m * NZ + origin, here, here, (r, f - NX), only)
        else:
            send("vd", which * NZ + origin, here, here, (r, f - NX), only)

    def across(m, origin, only=None):
        here = piece(m, origin, x)
        send(f"wx{m}", origin, here, here, dev_x, only)

    def publish(index, only=None):
        here = W7.at[t, wrow(index)]
        send("ay", index, here, here, dev_y, only)
        send("ac", index, here, here, dev_c, only)

    def own_pieces(m):
        up_to(m, z, z + 1 < NZ, x)
        down_to(m, z, z >= 1, x)
        across(m, z)

    def relay(m, k):
        low, high = z - k, z + k
        below, above = jnp.maximum(low, 0), jnp.minimum(high, NZ - 1)
        for which in (x,) if m < 3 else (x, 1 - x):
            first = m * NZ if m < 3 else which * NZ
            arrive("wu" if m < 3 else "vu", first + below, piece(m, below, which), low >= 0)
            up_to(m, below, (low >= 0) & (z + 1 < NZ), which)
            if m < 3:
                across(m, below, low >= 0)
            if m == 0:
                publish(below * NX + x, low >= 0)
            arrive("wd" if m < 3 else "vd", first + above, piece(m, above, which), high < NZ)
            down_to(m, above, (high < NZ) & (z >= 1), which)
            if m < 3:
                across(m, above, high < NZ)
            if m == 0:
                publish(above * NX + x, high < NZ)

    own_pieces(0)
    publish(f)
    base_gn = sem_at["gn"]

    def gn_one(k, carry):
        pltpu.make_async_remote_copy(
            src_ref=v.GNB.at[f], dst_ref=v.GNB.at[f], send_sem=ssem.at[base_gn], recv_sem=rsem.at[base_gn],
            device_id=(r, lax.rem(f + k, NF)), device_id_type=MESH,
        ).start()
        return carry

    lax.fori_loop(1, NF, gn_one, 0)
    gn_rest = v.GNB.at[pl.ds(0, NF - 1)]
    later.append(lambda: pltpu.make_async_copy(gn_rest, gn_rest, ssem.at[base_gn]).wait())
    for m in (1, 2, 3):
        own_pieces(m)

    gather_all("ids", ids_out)
    got_sids = load(ids_out.at[pl.ds(pl.multiple_of(r * NF, NF), NF)], v.sids, 5)
    got_sids.wait()
    got_table.wait()
    start_row = f * rows
    EXS, EXO, EXR, EZR = (v.EX.at[i] for i in range(4))

    def rows_of(i, other):
        owner = i * NX + other

        def token(j, inner):
            wanted = v.sids[owner, 0, j] - start_row
            inside = (wanted >= 0) & (wanted < rows)
            row = table[pl.ds(jnp.clip(wanted, 0, rows - 1), 1), :]
            v.stage[pl.ds(j, 1), :] = jnp.where(inside, row, 0.0)
            return inner

        lax.fori_loop(0, S, token, 0, unroll=8)
        return v.stage[...].astype(BF)

    steps = [(m, k) for k in range(1, NZ) for m in (0, 1, 2, 3)]
    jobs = [(i, True) for i in range(NZ)] + [(i, False) for i in range(NZ)]
    at_step = 0
    for number, (i, away) in enumerate(jobs):
        if away:
            EXS[i] = rows_of(i, 1 - x)
            send("ex", i, EXS.at[i], EXR.at[i], dev_x)
        else:
            EXO[i] = rows_of(i, x)
        if number == 1:
            arrive("wx3", z, piece(3, z, 1 - x))
            up_to(3, z, z + 1 < NZ, 1 - x)
            down_to(3, z, z >= 1, 1 - x)
        while at_step < len(steps) * (number + 1) // len(jobs):
            relay(*steps[at_step])
            at_step += 1

    for i in range(NZ):
        arrive("ex", i, EXR.at[i])
        total = EXO[i] + EXR[i]
        EXO[i] = total
        keep(z == i, EZR, i, total)
        send("ez", i, EXO.at[i], EZR.at[z], (r, i * NX + x), z != i, z)
    while at_step < len(steps):
        relay(*steps[at_step])
        at_step += 1

    for i in range(NZ):
        arrive("wx0", i, piece(0, i, 1 - x))
        publish(i * NX + 1 - x)
    for i in range(NF):
        there = W7.at[ty, wrow(i)]
        arrive("ay", i, there)
        send("ac", NF + i, there, there, dev_c)

    arrive("gn", 0, gn_rest)
    tiles = jnp.concatenate([v.GNB[i] for i in range(NF)], axis=1).astype(BF)
    at_row = lax.broadcasted_iota(jnp.int32, (NF * 128, D), 0)
    at_col = lax.broadcasted_iota(jnp.int32, (NF * 128, D), 1)
    lane = lax.bitwise_and(at_row, 127)
    pick = (lane < nr) & (lax.shift_right_logical(at_row, 7) * nr + lane == at_col)
    gains = dot(tiles, jnp.where(pick, 1.0, 0.0).astype(BF))
    gain = [gains[i : i + 1] for i in range(6)]

    for i in range(NZ):
        pl.when(z != i)(functools.partial(arrive, "ez", i, EZR.at[i]))
    embedded = EZR[0].astype(F32)
    for i in range(1, NZ):
        embedded = embedded + EZR[i].astype(F32)
    normed, hat, inverse = layer_norm(embedded, gain[0], gain[1])
    pool[blk(H0F), :] = normed
    pool[blk(HAT, 0), :] = hat
    v.INV[0] = inverse
    v.H0B[...] = normed.astype(BF)

    def to_rank(name, which, src, buffer):
        send(name, which, src, buffer.at[t], (g * TP + which, f), t != which, t)
        keep(t == which, buffer, which, src[...])


    for i in range(NF):
        arrive("ac", i, W7.at[tc, wrow(i)])
    for i in range(NF):
        arrive("ac", NF + i, W7.at[tyc, wrow(i)])
    tables = [jnp.concatenate([ref[...]] * (D // 128), axis=1) for ref in (v.cos_in, v.sin_in)]
    in_half = lax.bitwise_and(lax.broadcasted_iota(jnp.int32, (S, D), 1), HD - 1) < HD // 2

    def turn(values, sign):
        partner = jnp.where(
            in_half, pltpu.roll(values, D - HD // 2, 1), pltpu.roll(values, HD // 2, 1)
        )
        signed = jnp.where(in_half, -sign, sign) * tables[1]
        return values * tables[0] + partner * signed

    for j in range(3):
        projected = dot(v.H0B[...], W7[j])
        QKV[j] = (turn(projected, 1.0) if j < 2 else projected).astype(BF)
    allowed = lax.broadcasted_iota(jnp.int32, (1, S), 1) < length
    scaling = HD ** (-0.5)
    first_half = lax.broadcasted_iota(jnp.int32, (S, 128), 1) < HD

    def half(values, which):
        keep = first_half if which == 0 else jnp.logical_not(first_half)
        return jnp.where(keep, values, jnp.zeros_like(values))

    def attend(p, carry):
        lanes = pl.ds(pl.multiple_of(p * 128, 128), 128)
        query, keys, values = QKV[0, :, lanes], QKV[1, :, lanes], QKV[2, :, lanes]
        result = jnp.zeros((S, 128), F32)
        for which in range(2):
            scores = dot_nt(query, half(keys, which)) * scaling
            scores = jnp.where(allowed, scores, -1000000000.0)
            raised = jnp.exp(scores - jnp.max(scores, axis=-1, keepdims=True))
            chances = raised / jnp.sum(raised, axis=-1, keepdims=True)
            v.PS[2 * p + which] = chances
            result = result + dot(chances.astype(BF), half(values, which))
        v.ATT[:, lanes] = result.astype(BF)
        return carry

    lax.fori_loop(0, D // 128, attend, 0)
    branch = dot(v.ATT[...], W7[3])
    normed, hat, inverse = layer_norm(pool[blk(H0F), :] + branch, gain[2], gain[3])
    pool[blk(H1F), :] = normed
    pool[blk(HAT, 1), :] = hat
    v.INV[1] = inverse
    v.H1[t] = normed.astype(BF)

    def share(name, buffer):
        send(name, 0, buffer.at[t], buffer.at[t], dev_y)
        send(name, 1, buffer.at[t], buffer.at[t], dev_c)
        arrive(name, 0, buffer.at[ty])
        send(name, 2, buffer.at[ty], buffer.at[ty], dev_c)
        arrive(name, 1, buffer.at[tc])
        arrive(name, 2, buffer.at[tyc])

    def reduce(names, offset, landing, which):
        for i in range(2):
            send(names[0], i, pool.at[blk(offset, i * 2 + 1 - c)], pool.at[blk(landing, i)], dev_c)
        for i in range(2):
            arrive(names[0], i, pool.at[blk(landing, i)])
        away = pool[blk(offset, (1 - y) * 2 + c), :] + pool[blk(landing, 1 - y), :]
        v.YS[which] = away.astype(BF)
        send(names[1], 0, v.YS.at[which], v.YR.at[which], dev_y)
        mine = pool[blk(offset, t), :] + pool[blk(landing, y), :]
        arrive(names[1], 0, v.YR.at[which])
        return mine + v.YR[which].astype(F32)

    share("h1", v.H1)
    for m in range(1, 3):
        for i in range(NZ):
            arrive(f"wx{m}", i, piece(m, i, 1 - x))

    def forward(b, carry):
        gate, up = dot(v.H1[b], W7[4]), dot(v.H1[b], W7[5])
        pool[blk(GATE, b), :] = gate
        pool[blk(UP, b), :] = up
        mixed = (gate / (1.0 + jnp.exp(-gate)) * up).astype(BF)
        v.MIX[b] = mixed
        pool[blk(PT, b), :] = dot(mixed, W7[6])
        return carry

    lax.fori_loop(0, TP, forward, 0)
    feed = reduce(("fc", "fy"), PT, CR, 0)
    for which in range(3):
        to_rank("lx", which, v.H0B, v.LX)
    to_rank("lx", 3, v.ATT, v.LX)
    normed, hat, inverse = layer_norm(pool[blk(H1F), :] + feed, gain[4], gain[5])
    pool[blk(HAT, 2), :] = hat
    v.INV[2] = inverse
    present = jnp.where(lax.broadcasted_iota(jnp.int32, (S, 1), 0) < length, 1.0, 0.0)
    share_of = length.astype(F32)
    v.PROW[0] = jnp.sum(normed * present, axis=0, keepdims=True) / share_of

    spread("pool", v.PROW.at[0], v.PB)
    v.PB[d] = v.PROW[0]
    row_at = lax.broadcasted_iota(jnp.int32, (N, N), 0)
    col_at = lax.broadcasted_iota(jnp.int32, (N, N), 1)

    def own_lists():
        for i in range(N):
            v.IDF[pl.ds(i, 1), :] = ids_out[i, :, pl.ds(0, S)].astype(F32)
            v.PM[pl.ds(i, 1), pl.ds(0, S)] = ids_out[i, :, pl.ds(S, S)].astype(F32)
        local_row = v.IDF[...] - (f * rows).astype(F32)
        valid = lax.broadcasted_iota(jnp.int32, (N, S), 1).astype(F32) < v.PM[:, 0:S]
        mine = valid & (local_row >= 0.0) & (local_row < 1.0 * rows)
        marks = jnp.where(mine, 1.0, 0.0).astype(BF)
        before = lax.broadcasted_iota(jnp.int32, (S, S), 0) < lax.broadcasted_iota(jnp.int32, (S, S), 1)
        prefix = dot(marks, jnp.where(before, 1.0, 0.0).astype(BF))
        counts = jnp.zeros((N, S), F32) + jnp.sum(marks.astype(F32), axis=1, keepdims=True)
        offsets = dot(jnp.where(row_at > col_at, 1.0, 0.0).astype(BF), counts.astype(BF))
        place = prefix + offsets
        high = jnp.floor(place * (1.0 / S))
        v.RANK[0] = high
        v.RANK[1] = jnp.where(mine, place - high * S, -1.0)
        v.IDF[...] = jnp.where(mine, local_row, 0.0)
        slot_at = lax.broadcasted_iota(jnp.int32, (N, S), 0).astype(F32)
        low_at = lax.broadcasted_iota(jnp.int32, (S, S), 0).astype(F32)
        token_at = lax.broadcasted_iota(jnp.int32, (1, S), 1).astype(F32)

        def one(i, carry):
            at = pl.ds(i, 1)
            row = v.IDF[at, :]
            row_high = jnp.floor(row * (1.0 / 64))
            spot = v.RANK[0, at, :] == slot_at
            left = jnp.concatenate(
                [jnp.where(spot, item, 0.0) for item in (row_high, row - row_high * 64.0, token_at)], axis=0
            ).astype(BF)
            right = jnp.where(v.RANK[1, at, :] == low_at, 1.0, 0.0).astype(BF)
            return carry + dot_nt(left, right)

        found = lax.fori_loop(0, N, one, jnp.zeros((3 * N, S), F32))
        v.list_out[0] = (found[:N] * 64.0 + found[N : 2 * N]).astype(jnp.int32)
        v.list_out[1] = found[2 * N :].astype(jnp.int32)
        v.list_out[2] = offsets.astype(jnp.int32)
        v.list_out[3] = (offsets + counts).astype(jnp.int32)

    own_lists()
    gather_all("pool", v.PB)
    for i in range(N):
        v.PM[pl.ds(i, 1), :] = v.PB[i]
    pooled = v.PM[...]
    wide = lax.broadcasted_iota(jnp.int32, (N, D), 1)
    order, labels = v.order_in[...].astype(F32), v.labels_in[...].astype(F32)

    def column(row):
        return jnp.sum(jnp.where(row_at == col_at, row, 0.0), axis=1, keepdims=True)

    slot_has = jnp.where(column(order) == col_at.astype(F32), 1.0, 0.0).astype(BF)
    label_is = jnp.where(column(labels) == order, 1.0, 0.0).astype(BF)
    paired = dot(slot_has, label_is)
    loss_value = jnp.zeros((1, 1), F32)
    d_pooled = jnp.zeros((N, D), F32)
    for width in (D // 12, D // 3, D):
        portion = jnp.where(wide < width, pooled, 0.0)
        inverse = lax.rsqrt(jnp.sum(portion * portion, axis=1, keepdims=True) + 1e-06)
        unit = portion * inverse
        similar = lax.dot_general(
            unit, unit, (((1,), (1,)), ((), ())), precision=HI, preferred_element_type=F32
        ) / logit_divisor
        similar = jnp.where(row_at == col_at, -1000000000.0, similar)
        row_max = jnp.max(similar, axis=1, keepdims=True)
        raised = jnp.exp(similar - row_max)
        total = jnp.sum(raised, axis=1, keepdims=True)
        target = jnp.sum(jnp.where(paired > 0.0, similar, 0.0), axis=1, keepdims=True)
        term = row_max + jnp.log(total) - target
        loss_value = loss_value + jnp.sum(term, axis=0, keepdims=True) / N
        col_max = jnp.max(similar, axis=0, keepdims=True)
        raised_t = jnp.exp(similar - col_max)
        turned = raised_t / jnp.sum(raised_t, axis=0, keepdims=True)
        d_similar = (raised / total + turned - 2.0 * paired) / (3.0 * N) / logit_divisor
        d_unit = lax.dot_general(
            d_similar, unit, (((1,), (0,)), ((), ())), precision=HI, preferred_element_type=F32
        )
        inner = jnp.sum(d_unit * unit, axis=1, keepdims=True)
        d_pooled = d_pooled + inverse * (d_unit - unit * inner)
    loss_value = loss_value / 3.0
    own_row = lax.broadcasted_iota(jnp.int32, (N, D), 0) == d
    d_mine = jnp.sum(jnp.where(own_row, d_pooled, 0.0), axis=0, keepdims=True)

    d_two = d_mine * present / share_of
    d_sum, d_gain_two, d_shift_two = norm_back(d_two, pool[blk(HAT, 2), :], v.INV[2], gain[4])
    pool[blk(DS2), :] = d_sum
    v.DF[t] = d_sum.astype(BF)
    share("df", v.DF)

    def back(b, carry):
        d_mixed = dot_nt(v.DF[b], W7[6])
        gate, up = pool[blk(GATE, b), :], pool[blk(UP, b), :]
        logistic = 1.0 / (1.0 + jnp.exp(-gate))
        d_gate = (d_mixed * up * (logistic * (1.0 + gate * (1.0 - logistic)))).astype(BF)
        d_up = (d_mixed * (gate * logistic)).astype(BF)
        v.DG[0, b] = d_gate
        v.DG[1, b] = d_up
        pool[blk(PT2, b), :] = dot_nt(d_gate, W7[4]) + dot_nt(d_up, W7[5])
        return carry

    TILE = 256

    def product(left, right, m):
        def tile(i, carry):
            at = pl.ds(pl.multiple_of(i * TILE, TILE), TILE)
            GW[m, at, :] = dot_tn(left(at), right()).astype(BF)
            return carry

        lax.fori_loop(0, D // TILE, tile, 0)

    def part(m, i, other):
        return GW.at[m, wrow(i * NX + other)]

    def give(m):
        for i in range(NZ):
            send("gx", m * NZ + i, part(m, i, 1 - x), v.XR.at[m, i], dev_x)

    def pass_on(m):
        for i in range(NZ):
            arrive("gx", m * NZ + i, v.XR.at[m, i])
            total = (part(m, i, x)[...].astype(F32) + v.XR[m, i].astype(F32)).astype(BF)
            v.ZS[m, i] = total
            keep(z == i, v.ZR, (m, i), total)
            send("gz", m * NZ + i, v.ZS.at[m, i], v.ZR.at[m, z], (r, i * NX + x), z != i, m * NZ + z)

    def product_rows(buffer):
        return lambda at: buffer[:, :, at].reshape(TP * S, TILE)

    product(product_rows(v.MIX), lambda: v.DF[...].reshape(TP * S, D), 3)
    give(3)
    lax.fori_loop(0, TP, back, 0)
    for i in range(2):
        send("bc", i, pool.at[blk(PT2, i * 2 + 1 - c)], pool.at[blk(CR2, i)], dev_c)
    product(product_rows(v.H1), lambda: v.DG[0].reshape(TP * S, D), 1)
    give(1)
    for i in range(2):
        arrive("bc", i, pool.at[blk(CR2, i)])
    away = pool[blk(PT2, (1 - y) * 2 + c), :] + pool[blk(CR2, 1 - y), :]
    v.YS[1] = away.astype(BF)
    send("by", 0, v.YS.at[1], v.YR.at[1], dev_y)
    product(product_rows(v.H1), lambda: v.DG[1].reshape(TP * S, D), 2)
    give(2)
    pass_on(3)
    mine = pool[blk(PT2, t), :] + pool[blk(CR2, y), :]
    arrive("by", 0, v.YR.at[1])
    d_one = pool[blk(DS2), :] + (mine + v.YR[1].astype(F32))

    d_sum, d_gain_one, d_shift_one = norm_back(d_one, pool[blk(HAT, 1), :], v.INV[1], gain[2])
    pool[blk(DS1), :] = d_sum
    DB[0] = d_sum.astype(BF)
    to_rank("rx", 3, DB.at[0], v.RX)
    DB[1] = dot_nt(DB[0], W7[3]).astype(BF)
    pass_on(1)

    def attend_back(p, carry):
        lanes = pl.ds(pl.multiple_of(p * 128, 128), 128)
        query, keys, values = QKV[0, :, lanes], QKV[1, :, lanes], QKV[2, :, lanes]
        grad = DB[1, :, lanes]
        d_query = jnp.zeros((S, 128), F32)
        d_keys = jnp.zeros((S, 128), F32)
        d_values = jnp.zeros((S, 128), F32)
        for which in range(2):
            chances = v.PS[2 * p + which]
            d_values = d_values + dot_tn(chances.astype(BF), half(grad, which))
            d_chances = dot_nt(grad, half(values, which))
            inner = jnp.sum(chances * d_chances, axis=-1, keepdims=True)
            d_scores = (chances * (d_chances - inner)).astype(BF)
            d_query = d_query + dot(d_scores, half(keys, which)) * scaling
            d_keys = d_keys + dot_tn(d_scores, half(query, which)) * scaling
        pool[blk(DQ, 0), lanes] = d_query
        pool[blk(DQ, 1), lanes] = d_keys
        DQB[2, :, lanes] = d_values.astype(BF)
        return carry

    lax.fori_loop(0, D // 128, attend_back, 0)
    for j in range(2):
        DQB[j] = turn(pool[blk(DQ, j), :], -1.0).astype(BF)

    for which in range(3):
        to_rank("rx", which, DQB.at[which], v.RX)
    d_zero = pool[blk(DS1), :]
    for j in range(3):
        d_zero = d_zero + dot_nt(DQB[j], W7[j])
    d_embedded, d_gain_zero, d_shift_zero = norm_back(d_zero, pool[blk(HAT, 0), :], v.INV[0], gain[0])
    DB[2] = d_embedded.astype(BF)

    got_own = load(DB.at[2], ge_out.at[d], 0)
    cut = D // 2
    cols = [pl.ds(0, cut), pl.ds(cut, D - cut)]

    def line(rep, which_x, order, i):
        return ge_out.at[rep * NF + i * NX + which_x, :, cols[order]]

    def all_of(rep, order):
        return ge_out.at[pl.ds(pl.multiple_of(rep * NF, NF), NF), :, cols[order]]

    def ge_up(order, origin, src, only):
        send("eu", order * NZ + origin, src, line(r, x, order, origin), (r, f + NX), only)

    def ge_down(order, origin, src, only):
        send("ed", order * NZ + origin, src, line(r, x, order, origin), (r, f - NX), only)

    ry, rc, ryc = g * TP + ty, g * TP + tc, g * TP + tyc

    def ge_line(order, i, only=None, src=None):
        here = line(r, x, order, i)
        src = here if src is None else src
        if order == 0:
            send("e0x", i, src, here, dev_x, only)
            send("e0y", i * NX + x, src, here, dev_y, only)
            send("e0c", i * NX + x, src, here, dev_c, only)
        else:
            send("e1y", i, src, here, dev_y, only)
            send("e1x", i, src, here, dev_x, only)
            send("e1c", i * NX + x, src, here, dev_c, only)

    def ge_second(i, only):
        here = line(r, 1 - x, 0, i)
        arrive("e0x", i, here, only)
        send("e0y", i * NX + 1 - x, here, here, dev_y, only)
        send("e0c", i * NX + 1 - x, here, here, dev_c, only)
        here = line(ry, x, 1, i)
        arrive("e1y", i, here, only)
        send("e1x", NZ + i, here, here, dev_x, only)
        send("e1c", NF + i * NX + x, here, here, dev_c, only)

    def ge_third(i, only):
        for which_x in (x, 1 - x):
            here = line(ry, which_x, 0, i)
            arrive("e0y", i * NX + which_x, here, only)
            send("e0c", NF + i * NX + which_x, here, here, dev_c, only)
        for which, rep in enumerate((r, ry)):
            here = line(rep, 1 - x, 1, i)
            arrive("e1x", which * NZ + i, here, only)
            send("e1c", which * NF + i * NX + 1 - x, here, here, dev_c, only)

    def at_distance(step, k):
        low, high = z - k, z + k
        step(jnp.maximum(low, 0), low >= 0)
        if k:
            step(jnp.minimum(high, NZ - 1), high < NZ)

    for order in range(2):
        own_cols = DB.at[2, :, cols[order]]
        ge_up(order, z, own_cols, z + 1 < NZ)
        ge_down(order, z, own_cols, z >= 1)
        ge_line(order, z, None, own_cols)

    def ge_relay(k):
        low, high = z - k, z + k
        below, above = jnp.maximum(low, 0), jnp.minimum(high, NZ - 1)
        for order in range(2):
            arrive("eu", order * NZ + below, line(r, x, order, below), low >= 0)
            ge_up(order, below, line(r, x, order, below), (low >= 0) & (z + 1 < NZ))
            ge_line(order, below, low >= 0)
            arrive("ed", order * NZ + above, line(r, x, order, above), high < NZ)
            ge_down(order, above, line(r, x, order, above), (high < NZ) & (z >= 1))
            ge_line(order, above, high < NZ)

    v.NGS[0] = jnp.concatenate(
        [d_gain_zero, d_shift_zero, d_gain_one, d_shift_one, d_gain_two, d_shift_two,
         jnp.zeros((2, D), F32)], axis=0)
    stages = (("nc", dev_c), ("ny", dev_y), ("nx", dev_x))

    def norm_send(i):
        send(stages[i][0], 0, v.NGS.at[i], v.NGR.at[i], stages[i][1])

    def norm_add(i):
        arrive(stages[i][0], 0, v.NGR.at[i])
        v.NGS[i + 1] = v.NGS[i] + v.NGR[i]

    def settle(m, out, at):
        for i in range(NZ):
            arrive("gz", m * NZ + i, v.ZR.at[m, i], z != i)
        total = v.ZR[m, 0].astype(F32)
        for i in range(1, NZ):
            total = total + v.ZR[m, i].astype(F32)
        out[t, at, :] = total.astype(BF)

    def group_sum(out, first, size):
        own = v.FG.at[g, pl.ds(first, size)]
        own[...] = out[t]
        for k in range(1, NG):
            other = lax.rem(g + k, NG)
            index = (0 if first else NG) + k
            send("gg", index, own, own, (other * TP + t, f), None, (0 if first else NG) + g)
        for k in range(1, NG):
            other = lax.rem(g + k, NG)
            arrive("gg", (0 if first else NG) + other, v.FG.at[other, pl.ds(first, size)])
        total = v.FG[0, pl.ds(first, size)].astype(F32)
        for k in range(1, NG):
            total = total + v.FG[k, pl.ds(first, size)].astype(F32)
        out[t] = total.astype(BF)

    def share_start(name, buffer):
        send(name, 0, buffer.at[t], buffer.at[t], dev_y)
        send(name, 1, buffer.at[t], buffer.at[t], dev_c)

    def share_pass(name, buffer):
        arrive(name, 0, buffer.at[ty])
        send(name, 2, buffer.at[ty], buffer.at[ty], dev_c)

    def share_end(name, buffer):
        arrive(name, 1, buffer.at[tc])
        arrive(name, 2, buffer.at[tyc])

    norm_send(0)
    pass_on(2)
    for which in range(TP):
        arrive("lx", which, v.LX.at[which], t != which)
        arrive("rx", which, v.RX.at[which], t != which)
    product(product_rows(v.LX), lambda: v.RX[...].reshape(TP * S, D), 0)
    give(0)
    norm_add(0)
    norm_send(1)
    got_own.wait()
    ge_relay(1)
    at_distance(ge_second, 0)
    settle(3, v.ff_out, pl.ds(2 * nr, nr))
    settle(1, v.ff_out, pl.ds(0, nr))
    norm_add(1)
    norm_send(2)
    settle(2, v.ff_out, pl.ds(nr, nr))
    if NG > 1:
        group_sum(v.ff_out, nr, 3 * nr)
    share_start("ff", v.ff_out)
    pass_on(0)
    for k in range(2, NZ):
        ge_relay(k)
        at_distance(ge_second, k - 1)
    at_distance(ge_second, NZ - 1)
    norm_add(2)
    for i in range(NZ):
        send("nz", i, v.NGS.at[3], v.NGZ.at[z], (r, i * NX + x), z != i, z)
        keep(z == i, v.NGZ, i, v.NGS[3])
    own = v.ff_out[t].astype(F32)
    squares = jnp.sum(own * own)
    settle(0, v.fa_out, pl.ds(0, nr))
    if NG > 1:
        group_sum(v.fa_out, 0, nr)
    share_start("fa", v.fa_out)
    own = v.fa_out[t].astype(F32)
    squares = squares + jnp.sum(own * own)
    squares = jnp.where(g == 0, squares, 0.0)
    for k in range(NZ):
        at_distance(ge_third, k)
    for name, buffer in (("ff", v.ff_out), ("fa", v.fa_out)):
        share_pass(name, buffer)
    for i in range(NZ):
        arrive("nz", i, v.NGZ.at[i], z != i)
    total_norms = v.NGZ[0]
    for i in range(1, NZ):
        total_norms = total_norms + v.NGZ[i]
    for name, buffer in (("ff", v.ff_out), ("fa", v.fa_out)):
        share_end(name, buffer)
    for order, name in enumerate(("e0c", "e1c")):
        for which, rep in enumerate((rc, ryc)):
            for i in range(NF):
                arrive(name, which * NF + i, ge_out.at[rep * NF + i, :, cols[order]])
    if NG > 1:

        def group(which):
            return ge_out.at[pl.ds(pl.multiple_of(which * TP * NF, TP * NF), TP * NF)]

        for k in range(1, NG):
            other = lax.rem(g + k, NG)
            send("eg", k, group(g), group(g), (other * TP + t, f), None, g)
        for k in range(1, NG):
            other = lax.rem(g + k, NG)
            arrive("eg", other, group(other))

    def fetch(b):
        return pltpu.make_async_copy(
            ge_out.at[pl.ds(b * NZ, NZ)], v.EX.at[2 + lax.rem(b, 2)], lsem.at[1 + lax.rem(b, 2)]
        )

    fetch(0).start()
    same = lax.broadcasted_iota(jnp.int32, (S, S), 0) == lax.broadcasted_iota(jnp.int32, (S, S), 1)
    own_ids = jnp.sum(
        jnp.where(same, ids_out[d, :, pl.ds(0, S)].astype(F32), 0.0), axis=1, keepdims=True
    )

    def pairs_of(b, carry):
        pl.when(b + 1 < N // NZ)(lambda: fetch(b + 1).start())
        fetch(b).wait()
        for i in range(NZ):
            both = dot_nt(DB[2], v.EX[2 + lax.rem(b, 2), i])
            theirs = ids_out[b * NZ + i, :, pl.ds(0, S)].astype(F32)
            carry = carry + jnp.where(own_ids == theirs, both, 0.0)
        return carry

    both = lax.fori_loop(0, N // NZ, pairs_of, jnp.zeros((S, S), F32))
    squares = squares + jnp.sum(both)
    squares = squares + jnp.where(d == 0, jnp.sum(total_norms * total_norms), 0.0)
    v.SQ[0] = jnp.zeros((1, 128), F32) + squares
    spread("sq", v.SQ.at[0], v.SQS)
    v.SQS[d] = v.SQ[0]
    v.ng_out[...] = total_norms
    gather_all("sq", v.SQS)
    all_squares = v.SQS[0]
    for i in range(1, N):
        all_squares = all_squares + v.SQS[i]
    v.stats_out[...] = jnp.concatenate(
        [jnp.zeros((1, 128), F32) + loss_value, jnp.sqrt(all_squares), jnp.zeros((6, 128), F32)], axis=0
    )
    for finish in later:
        finish()


def run_step(sizes, *args):
    NR, NF, S, D, rows = sizes
    N, nr = NR * NF, D // NF
    vmem = pl.BlockSpec(memory_space=pltpu.VMEM)
    smem = pl.BlockSpec(memory_space=pltpu.SMEM)
    hbm = pl.BlockSpec(memory_space=pl.ANY)
    buffers, copies = step_layout(sizes)
    many = sum(copies.values())
    return pl.pallas_call(
        functools.partial(step_kernel, sizes),
        name="step",
        out_shape=(
            jax.ShapeDtypeStruct((N, 1, 2 * S), jnp.int32),
            jax.ShapeDtypeStruct((TP, 3 * nr, D), BF),
            jax.ShapeDtypeStruct((TP, nr, D), BF),
            jax.ShapeDtypeStruct((8, D), F32),
            jax.ShapeDtypeStruct((8, 128), F32),
            jax.ShapeDtypeStruct((4, N, S), jnp.int32),
            jax.ShapeDtypeStruct((N, S, D), BF),
        ),
        in_specs=[smem] + [vmem] * 6 + [hbm] * 5,
        out_specs=(vmem,) * 6 + (hbm,),
        scratch_shapes=[pltpu.VMEM(*item) for item in buffers.values()]
        + [
            pltpu.SMEM((NF, 1, 2 * S), jnp.int32), pltpu.SemaphoreType.DMA((many,)),
            pltpu.SemaphoreType.DMA((many,)), pltpu.SemaphoreType.DMA((8,)),
        ],
        compiler_params=pltpu.CompilerParams(
            collective_id=0, has_side_effects=True, vmem_limit_bytes=67_000_000
        ),
    )(*args)


def adamw(weight, grad, first, second, rate):
    first_new = beta_first * first + (1.0 - beta_first) * grad
    second_new = beta_second * second + (1.0 - beta_second) * grad * grad
    first_fix = 1.0 - beta_first**STEP
    second_fix = 1.0 - beta_second**STEP
    update = first_new / first_fix / (jnp.sqrt(second_new / second_fix) + adam_floor)
    return (weight - rate * (update + weight_decay * weight), first_new, second_new)


CHUNK, SLOTS = 424, 7


def finish_kernel(sizes, *refs):
    NR, NF, S, D, rows = sizes
    N, nr = NR * NF, D // NF
    names = ("lists", "ge", "ff", "fa", "norms", "stats", "pw", "pm", "pv") + tuple(
        f"{kind}{which}" for kind in "eaogd" for which in range(3)
    )
    results = ("qw", "qm", "qv") + tuple(f"{kind}{which}_new" for kind in "eaogd" for which in range(3))
    scratch = (
        "grads", "landing", "stage", "TB", "LA", "LO", "LG", "LD", "sems",
        "ins", "outs", "tin", "tout",
    )
    v = types.SimpleNamespace(**dict(zip((*names, *results, *scratch), refs, strict=True)))
    n_chunks = rows // CHUNK

    def fetch(s):
        return pltpu.make_async_copy(v.ge.at[s], v.landing.at[lax.rem(s, 4)], v.sems.at[lax.rem(s, 4)])

    for s in range(3):
        fetch(s).start()
    layers = (("a", v.LA), ("o", v.LO), ("d", v.LD), ("g", v.LG))

    def layer(index, inward):
        kind, buffer = layers[index]
        for which in range(3):
            if inward:
                yield pltpu.make_async_copy(
                    getattr(v, f"{kind}{which}"), buffer.at[which], v.ins.at[index * 3 + which]
                )
            else:
                yield pltpu.make_async_copy(
                    buffer.at[which], getattr(v, f"{kind}{which}_new"), v.outs.at[index * 3 + which]
                )

    def chunk(k, inward):
        at, slot = pl.ds(k * CHUNK, CHUNK), k % SLOTS
        for which in range(3):
            old, new = getattr(v, f"e{which}"), getattr(v, f"e{which}_new")
            if inward:
                yield pltpu.make_async_copy(old.at[at], v.TB.at[slot, which], v.tin.at[slot, which])
            else:
                yield pltpu.make_async_copy(v.TB.at[slot, which], new.at[at], v.tout.at[slot, which])

    for index in range(4):
        for item in layer(index, True):
            item.start()
    for k in range(min(SLOTS, n_chunks)):
        for item in chunk(k, True):
            item.start()

    factor = jnp.minimum(1.0, clip_level / (v.stats[1:2, 0:1] + 1e-06))

    def apply(buffer, at, grad):
        index = tuple(at)
        new = adamw(
            buffer[(0, *index)], grad * factor, buffer[(1, *index)], buffer[(2, *index)], learn_rate
        )
        for which in range(3):
            buffer[(which, *index)] = new[which]

    def finish_layer(index):
        for item in layer(index, False):
            item.start()

    whole = pl.ds(0, nr)
    for item in layer(0, True):
        item.wait()
    for q in range(3):
        apply(v.LA, (whole, pl.ds(q * D, D)), v.fa[q].astype(F32))
    finish_layer(0)
    for item in layer(1, True):
        item.wait()
    apply(v.LO, (whole, pl.ds(0, D)), v.fa[3].astype(F32))
    finish_layer(1)
    for item in layer(2, True):
        item.wait()

    def down(q, carry):
        at = pl.ds(pl.multiple_of(q * nr, 16), nr)
        apply(v.LD, (at, pl.ds(0, D)), v.ff[q, pl.ds(2 * nr, nr), :].astype(F32))
        return carry

    lax.fori_loop(0, TP, down, 0)
    finish_layer(2)
    for item in layer(3, True):
        item.wait()
    quarter, span = D // TP, 2 * D // 6
    at_row = lax.broadcasted_iota(jnp.int32, (span, D), 0)
    at_col = lax.broadcasted_iota(jnp.int32, (span, D), 1)
    group = lax.div(at_col, nr)
    unit = lax.div(group, TP) * nr + (at_col - group * nr)
    holder = lax.rem(group, TP)
    for b in range(TP):
        first = quarter * b // 128 * 128
        total = jnp.zeros((2 * nr, D), F32)
        for q in range(TP):
            pick = (at_row + (first - quarter * b) == unit) & (holder == q)
            total = total + dot(
                v.ff[q, pl.ds(0, 2 * nr), pl.ds(first, span)], jnp.where(pick, 1.0, 0.0).astype(BF)
            )
        apply(v.LG, (whole, pl.ds(b * D, D)), total[:nr])
        apply(v.LG, (whole, pl.ds((TP + b) * D, D)), total[nr:])
    finish_layer(3)
    at_row = lax.broadcasted_iota(jnp.int32, (D, 128), 0)
    at_col = lax.broadcasted_iota(jnp.int32, (D, 128), 1)
    pick = (at_row - lax.axis_index("fsdp") * nr == at_col) & (at_col < nr)
    mine = lax.dot_general(
        v.norms[...], jnp.where(pick, 1.0, 0.0), (((1,), (0,)), ((), ())),
        precision=lax.Precision.HIGHEST, preferred_element_type=F32,
    )
    v.qw[...], v.qm[...], v.qv[...] = adamw(
        v.pw[...], mine[:6, :nr] * factor, v.pm[...], v.pv[...], norm_rate
    )

    def clear(i, carry):
        v.grads[pl.ds(pl.multiple_of(i * CHUNK, 8), CHUNK), :] = jnp.zeros((CHUNK, D), F32)
        return carry

    lax.fori_loop(0, n_chunks, clear, 0)

    def sequence(s, carry):
        pl.when(s + 3 < N)(lambda: fetch(s + 3).start())
        fetch(s).wait()
        v.stage[...] = v.landing[lax.rem(s, 4)].astype(F32)

        def token(k, inner):
            high, low = lax.shift_right_logical(k, shift), lax.bitwise_and(k, S - 1)
            at = pl.ds(v.lists[0, high, low], 1)
            v.grads[at, :] = v.grads[at, :] + v.stage[pl.ds(v.lists[1, high, low], 1), :]
            return inner

        return lax.fori_loop(v.lists[2, s, 0], v.lists[3, s, 0], token, carry)

    shift = S.bit_length() - 1
    lax.fori_loop(0, N, sequence, 0)

    for k in range(n_chunks):
        for item in chunk(k, True):
            item.wait()
        slot = k % SLOTS

        def part(first, size, k=k, slot=slot):
            at = pl.ds(pl.multiple_of(k * CHUNK + first, 8), size)
            grad = v.grads[at, :]
            apply(v.TB.at[slot], (pl.ds(pl.multiple_of(first, 8), size), pl.ds(0, D)), grad)

        def tile(i, carry, part=part):
            part(i * 32, 32)
            return carry

        lax.fori_loop(0, CHUNK // 32, tile, 0)
        if CHUNK % 32:
            part(CHUNK // 32 * 32, CHUNK % 32)
        for item in chunk(k, False):
            item.start()
        if k >= 1 and k - 1 + SLOTS < n_chunks:
            for item in chunk(k - 1, False):
                item.wait()
            for item in chunk(k - 1 + SLOTS, True):
                item.start()
    for k in range(n_chunks):
        if k + SLOTS >= n_chunks or k == n_chunks - 1:
            for item in chunk(k, False):
                item.wait()
    for index in range(4):
        for item in layer(index, False):
            item.wait()


def finish(sizes, lists, ge, ff, fa, norms, stats, norm_state, states):
    NR, NF, S, D, rows = sizes
    N, nr = NR * NF, D // NF
    hbm = pl.BlockSpec(memory_space=pl.ANY)
    vmem = pl.BlockSpec(memory_space=pltpu.VMEM)
    smem = pl.BlockSpec(memory_space=pltpu.SMEM)
    flat = [item for state in states for item in state]
    shapes = [jax.ShapeDtypeStruct(item.shape, F32) for item in (*norm_state, *flat)]
    return pl.pallas_call(
        functools.partial(finish_kernel, sizes),
        name="finish",
        out_shape=tuple(shapes),
        in_specs=[smem, hbm] + [vmem] * 7 + [hbm] * 15,
        out_specs=(vmem,) * 3 + (hbm,) * 15,
        scratch_shapes=[
            pltpu.VMEM((rows, D), F32), pltpu.VMEM((4, S, D), BF), pltpu.VMEM((S, D), F32),
            pltpu.VMEM((SLOTS, 3, CHUNK, D), F32),
            pltpu.VMEM((3, nr, 3 * D), F32), pltpu.VMEM((3, nr, D), F32), pltpu.VMEM((3, nr, 8 * D), F32),
            pltpu.VMEM((3, 4 * nr, D), F32),
            pltpu.SemaphoreType.DMA((4,)), pltpu.SemaphoreType.DMA((12,)),
            pltpu.SemaphoreType.DMA((12,)), pltpu.SemaphoreType.DMA((SLOTS, 3)),
            pltpu.SemaphoreType.DMA((SLOTS, 3)),
        ],
        compiler_params=pltpu.CompilerParams(vmem_limit_bytes=62_000_000),
    )(lists, ge, ff, fa, norms, stats, *norm_state, *flat)


def table_kernel(sizes, ids, ge, factor, w, m, v, w_out, m_out, v_out, grads, landing, stage, sems):
    NR, NF, S, D, rows = sizes
    N = NR * NF
    step = pl.program_id(0)
    block = w.shape[0]

    @pl.when(step == 0)
    def _():
        start_row = lax.axis_index("fsdp") * rows

        def fetch(s):
            return pltpu.make_async_copy(ge.at[s], landing.at[lax.rem(s, 4)], sems.at[lax.rem(s, 4)])

        for s in range(3):
            fetch(s).start()

        def clear(i, carry):
            grads[pl.ds(pl.multiple_of(i * block, 8), block), :] = jnp.zeros((block, D), F32)
            return carry

        lax.fori_loop(0, grads.shape[0] // block, clear, 0)

        def sequence(s, carry):
            pl.when(s + 3 < N)(lambda: fetch(s + 3).start())
            fetch(s).wait()
            stage[...] = landing[lax.rem(s, 4)].astype(F32)

            def token(j, inner):
                wanted = ids[s, 0, j] - start_row

                @pl.when((wanted >= 0) & (wanted < rows))
                def _():
                    at = pl.ds(wanted, 1)
                    grads[at, :] = grads[at, :] + stage[pl.ds(j, 1), :]

                return inner

            return lax.fori_loop(0, S, token, carry)

        lax.fori_loop(0, N, sequence, 0)

    grad = grads[pl.ds(pl.multiple_of(step * block, 8), block), :] * factor[0:1, 0:1]
    w_out[...], m_out[...], v_out[...] = adamw(w[...], grad, m[...], v[...], learn_rate)


def update_table(sizes, ids, ge, factor, w, m, v):
    NR, NF, S, D, rows = sizes
    block = 424
    steps = pl.cdiv(rows, block)
    part = pl.BlockSpec((block, D), lambda i: (i, 0))
    return pl.pallas_call(
        functools.partial(table_kernel, sizes),
        name="table",
        grid=(steps,),
        out_shape=(jax.ShapeDtypeStruct((rows, D), F32),) * 3,
        in_specs=[
            pl.BlockSpec(memory_space=pltpu.SMEM), pl.BlockSpec(memory_space=pl.ANY),
            pl.BlockSpec((8, 128), lambda i: (0, 0)), part, part, part,
        ],
        out_specs=(part, part, part),
        scratch_shapes=[
            pltpu.VMEM((steps * block, D), F32), pltpu.VMEM((4, S, D), BF), pltpu.VMEM((S, D), F32),
            pltpu.SemaphoreType.DMA((4,)),
        ],
        compiler_params=pltpu.CompilerParams(vmem_limit_bytes=60_000_000),
    )(ids, ge, factor, w, m, v)


def local(
    sizes,
    token_ids,
    lengths,
    slot_order,
    pair_labels,
    embedding,
    attend_weight,
    attention_output_matrix,
    gate_up,
    contract_kernel,
    norm_params,
    embedding_first,
    embedding_second,
    attend_first,
    attend_second,
    output_first,
    output_second,
    gate_up_first,
    gate_up_second,
    down_first,
    down_second,
    norm_first,
    norm_second,
):
    NR, NF, S, D, rows = sizes
    nr = D // NF
    f = lax.axis_index("fsdp")
    N = NR * NF
    positions = jnp.arange(S)
    angles = (
        positions.astype(F32)[:, None]
        * (1000.0 ** (-2.0 * jnp.arange(HD // 2).astype(F32) / HD))[None, :]
    )
    cosine, sine = jnp.tile(jnp.cos(angles), (1, 128 * 2 // HD)), jnp.tile(jnp.sin(angles), (1, 128 * 2 // HD))
    ids, ffn, att, norms, stats, lists, ge = run_step(
        sizes,
        lengths,
        token_ids,
        norm_params,
        slot_order.reshape(1, N),
        pair_labels.reshape(1, N),
        cosine,
        sine,
        attend_weight,
        attention_output_matrix,
        gate_up,
        contract_kernel,
        embedding,
    )
    loss_value, grad_norm = stats[0, 0], stats[1, 0]
    if rows % CHUNK == 0:
        norm_next, *rest = split_three(
            finish(
                sizes, lists, ge, ffn, att, norms, stats, (norm_params, norm_first, norm_second),
                (
                    (embedding, embedding_first, embedding_second),
                    (attend_weight, attend_first, attend_second),
                    (attention_output_matrix, output_first, output_second),
                    (gate_up, gate_up_first, gate_up_second),
                    (contract_kernel, down_first, down_second),
                ),
            )
        )
        return (loss_value, grad_norm, *(item for state in rest for item in state), *norm_next)
    factor = jnp.minimum(1.0, clip_level / (grad_norm + 1e-06))
    factor_tile = jnp.broadcast_to(factor, (8, 128))
    emb_next = update_table(sizes, ids, ge, factor_tile, embedding, embedding_first, embedding_second)
    fin = ffn.reshape(TP, 3, nr, D)
    grad_attend = att[:3].transpose(1, 0, 2).reshape(nr, 3 * D).astype(F32)
    grad_output = att[3].astype(F32)
    grad_hidden = (
        fin[:, :2].reshape(TP, 2, nr, NF, nr).transpose(2, 1, 3, 0, 4).reshape(nr, 8 * D).astype(F32)
    )
    grad_down = fin[:, 2].reshape(TP * nr, D).astype(F32)
    grad_norms = lax.dynamic_slice(norms, (0, f * nr), (6, nr))
    att_next = adamw(attend_weight, grad_attend * factor, attend_first, attend_second, learn_rate)
    out_next = adamw(
        attention_output_matrix, grad_output * factor, output_first, output_second, learn_rate
    )
    gate_next = adamw(gate_up, grad_hidden * factor, gate_up_first, gate_up_second, learn_rate)
    down_next = adamw(contract_kernel, grad_down * factor, down_first, down_second, learn_rate)
    norm_next = adamw(norm_params, grad_norms * factor, norm_first, norm_second, norm_rate)
    return (
        loss_value, grad_norm, *emb_next, *att_next, *out_next, *gate_next, *down_next, *norm_next
    )


def split_three(flat):
    return [flat[i : i + 3] for i in range(0, len(flat), 3)]


def solution(mesh):
    NR, NF = mesh.shape["rep"], mesh.shape["fsdp"]
    rows_spec, cols_spec = P("fsdp", None), P(None, "fsdp")

    def step(*args):
        S, D, rows = args[0].shape[1], args[4].shape[1], args[4].shape[0] // NF
        run = jax.shard_map(
            functools.partial(local, (NR, NF, S, D, rows)),
            mesh=mesh,
            in_specs=(P(("rep", "fsdp"), None), P(("rep", "fsdp")), P(), P())
            + (rows_spec,) * 5 + (cols_spec,) + (rows_spec,) * 10 + (cols_spec,) * 2,
            out_specs=(P(), P()) + (rows_spec,) * 15 + (cols_spec,) * 3,
            check_vma=False,
        )
        return run(*args)

    return step
```
